32 devices in a mesh: dp: 8 (over z, x), mp: 4 (over y, core).
Axes of the slice: x: 2, y: 2, z: 4, core: 2. Of those that a mesh axis runs over, the one named last changes fastest.
Arguments:
- block_in: bfloat16 [16384, 1024], P('dp', 'mp')
- out_grad: bfloat16 [16384, 1024], P('dp', 'mp')
- lengths: int32 [16], P('dp'), may hold values from 256 to 1024
- group_ids: int32 [16], P('dp'), may hold values from 0 to 7
- time_embed: float32 [8, 1024], replicated, may hold values from -6 to 6
- weights: float32 [1024, 14, 1024], P('dp', None, 'mp')
- first_moments: float32 [1024, 14, 1024], P('dp', None, 'mp')
- second_moments: float32 [1024, 14, 1024], P('dp', None, 'mp'), as said below
- owners: int32 [14, 8], replicated, may hold values from 0 to 7, each once within a row
- left_basis: float32 [14, 1024, 128], P(None, 'dp'), may hold values from -1 to 1, as said below
- right_basis: float32 [14, 1024, 256], P(None, 'mp'), may hold values from -1 to 1, as said below
- biases: float32 [13, 1024], P(None, 'mp'), may hold values from -2.5 to 2.5
- bias_first: float32 [13, 1024], P(None, 'mp')
- bias_second: float32 [13, 1024], P(None, 'mp'), as said below
Outputs:
- block_out: bfloat16 [16384, 1024], P('dp', 'mp')
- input_grad: float32 [16384, 1024], P('dp', 'mp')
- weight_grads: float32 [1024, 14, 1024], P('dp', None, 'mp')
- new_first: float32 [1024, 14, 1024], P('dp', None, 'mp')
- new_second: float32 [1024, 14, 1024], P('dp', None, 'mp')
- new_weights: float32 [1024, 14, 1024], P('dp', None, 'mp')
- new_weights_low: bfloat16 [1024, 14, 1024], P('dp', None, 'mp')
- new_bias_first: float32 [13, 1024], P(None, 'mp')
- new_bias_second: float32 [13, 1024], P(None, 'mp')
- new_biases: float32 [13, 1024], P(None, 'mp')
The draws below stay inside these ranges and needn't reach their ends.
Inputs may be any that keep to these rules, and one draw needn't show every extreme that they name: Each block left_basis[k, a * 128 to a * 128 + 127, :] is an orthogonal matrix. Each block right_basis[k, c * 256 to c * 256 + 255, :] is an orthogonal matrix. `second_moments`: positive. `bias_second`: positive.
All inputs are finite; a program needn't handle non-finite values.
Results may differ from the reference program's by a relative error of at most 0.02.
The reference program's roundings to bfloat16 on the way count: a program that leaves them out, or rounds other values in their place, can miss the bound.
Values may be sent and summed in bfloat16 or wider, within the bound.
No kernel may reach another device: no remote copies, remote signals or barrier semaphores. Data moves between devices by JAX's collectives and lax.ppermute only.
A program may use at most 192 MiB of HBM per device.

```python
import math
import jax
import jax.numpy as jnp
from jax import lax

D = 1024
HEADS = 16
HEAD_DIM = 64
LEN = 1024
GROUPS = 8
SLICES = 14
BROWS = 13
STEP = 10
UTTS = 16
TOKENS = 16384
DSH = 128
CSH = 256
N_DP = 8
N_MP = 4


slice_scales = (0.9, 0.9, 0.9, 0.08, 0.55, 0.55, 0.36, 0.36, 0.6, 0.6, 0.6, 0.6, 0.6, 0.6)


weight_scales = (1.3, 1.3, 1.0, 8.0, 1.0, 1.0, 1.41, 1.41, 1.0, 1.0, 1.0, 1.0, 1.0, 1.0)


bias_scales = (0.8, 0.8, 0.9, 0.6, 0.5, 0.5, 0.6, 1.0, 1.0, 1.0, 1.0, 1.0, 1.0)


def draw_block_in(key, part):
    feature_ramp = jnp.arange(D, dtype=jnp.float32) / (D - 1)
    values = jax.random.normal(key, (TOKENS, D), jnp.float32) * (0.5 + feature_ramp)
    return values.astype(jnp.bfloat16)


def draw_out_grad(key, part):
    feature_ramp = jnp.arange(D, dtype=jnp.float32) / (D - 1)
    sub_key = jax.random.fold_in(key, 7)
    values = jax.random.normal(sub_key, (TOKENS, D), jnp.float32) * (0.5 + feature_ramp)
    return values.astype(jnp.bfloat16)


def draw_weights(key, part):
    factors = jnp.array(weight_scales, jnp.float32)[None, :, None] / math.sqrt(D)
    values = jnp.clip(jax.random.normal(key, (D, SLICES, D), jnp.float32), -5.0, 5.0)
    return values * factors


def draw_first_moments(key, part):
    grad_size = jnp.array(slice_scales, jnp.float32)[None, :, None] * math.sqrt(TOKENS)
    values = jnp.clip(jax.random.normal(key, (D, SLICES, D), jnp.float32), -5.0, 5.0)
    return values * (0.053 * grad_size)


def draw_second_moments(key, part):
    grad_size = jnp.array(slice_scales, jnp.float32)[None, :, None] * math.sqrt(TOKENS)
    factors = jnp.exp(jax.random.uniform(key, (D, SLICES, D), jnp.float32, 0.0, math.log(4.0)))
    return factors * 0.053 * grad_size * grad_size


def orthogonal_blocks(key, block_count, order_size):
    positions = jnp.arange(order_size, dtype=jnp.int32)
    common = jnp.bitwise_and(positions[:, None], positions[None, :])
    parity = jnp.zeros((order_size, order_size), jnp.int32)
    for shift_bits in range(16):
        parity = jnp.bitwise_xor(parity, jnp.bitwise_and(jnp.right_shift(common, shift_bits), 1))
    hadamard = (1.0 - 2.0 * parity.astype(jnp.float32)) / math.sqrt(order_size)
    sub_keys = jax.random.split(key, 4)
    orders = jax.vmap(lambda part_key: jax.random.permutation(part_key, order_size))(jax.random.split(sub_keys[0], block_count))
    rows_sign = (2 * jax.random.randint(sub_keys[1], (block_count, order_size, 1), 0, 2) - 1).astype(jnp.float32)
    column_sign = (2 * jax.random.randint(sub_keys[2], (block_count, 1, order_size), 0, 2) - 1).astype(jnp.float32)
    base = hadamard[orders] * rows_sign * column_sign
    angles = jax.random.uniform(sub_keys[3], (block_count, order_size // 2, 1), jnp.float32, -math.pi, math.pi)
    pair_view = base.reshape(block_count, order_size // 2, 2, order_size)
    first_row = pair_view[:, :, 0, :]
    second_row = pair_view[:, :, 1, :]
    cosine_part = jnp.cos(angles)
    sine_part = jnp.sin(angles)
    turned = jnp.stack([cosine_part * first_row - sine_part * second_row, sine_part * first_row + cosine_part * second_row], axis=2)
    return turned.reshape(block_count, order_size, order_size)


def draw_left_basis(key, part):
    return orthogonal_blocks(key, SLICES * (D // DSH), DSH).reshape(SLICES, D, DSH)


def draw_right_basis(key, part):
    return orthogonal_blocks(key, SLICES * (D // CSH), CSH).reshape(SLICES, D, CSH)


def draw_bias_first(key, part):
    grad_size = jnp.array(bias_scales, jnp.float32)[:, None] * math.sqrt(TOKENS)
    values = jnp.clip(jax.random.normal(key, (BROWS, D), jnp.float32), -5.0, 5.0)
    return values * (0.111 * grad_size)


def draw_bias_second(key, part):
    grad_size = jnp.array(bias_scales, jnp.float32)[:, None] * math.sqrt(TOKENS)
    factors = jnp.exp(jax.random.uniform(key, (BROWS, D), jnp.float32, 0.0, math.log(4.0)))
    return factors * 0.001 * grad_size * grad_size


def set_ends(values, key, low, top_value):
    extent = values.shape
    place = [jax.random.randint(jax.random.fold_in(key, axis), (), 0, extent[axis]) for axis in range(len(extent))]
    values = values.at[tuple(place)].set(low)
    longest = extent.index(max(extent))
    place[longest] = (place[longest] + 1) % extent[longest]
    return values.at[tuple(place)].set(top_value)


def levels(own_key, dims, shards, smallest, top_value):
    gain = 1.0
    for dim, parts in shards:
        draws = jax.random.uniform(jax.random.fold_in(jax.random.fold_in(own_key, 6), dim), (parts,), jnp.float32, smallest / len(shards), top_value / len(shards))
        gain = gain * jnp.repeat(jnp.exp(draws), dims[dim] // parts).reshape((-1,) + (1,) * (len(dims) - 1 - dim))
    return gain


def bell_draw(own_key, shape, scale, reach, cuts=(), kind=jnp.bfloat16):
    values = jax.random.normal(own_key, shape, jnp.float32) * scale
    if len(cuts) > 0:
        values = levels(own_key, shape, cuts, -0.22, 0.18) * values
    return jnp.clip(values, min=-reach, max=reach).astype(kind)


def setup_inputs(seed: int = 0) -> dict:
    key_of = jax.random.split(jax.random.key(seed), 15)
    block_in = draw_block_in(jax.random.fold_in(key_of[14], 71), 0)
    out_grad = draw_out_grad(jax.random.fold_in(key_of[14], 71), 0)
    lengths = set_ends(jax.random.randint(key_of[2], (UTTS,), LEN // 4, LEN + 1), jax.random.fold_in(key_of[2], 1), LEN // 4, LEN).astype(jnp.int32)
    group_ids = set_ends(jax.random.randint(key_of[3], (UTTS,), 0, GROUPS), jax.random.fold_in(key_of[3], 1), 0, GROUPS - 1).astype(jnp.int32)
    time_embed = bell_draw(key_of[4], (GROUPS, D), 1.0, 6.0, (), jnp.float32)
    weights = draw_weights(jax.random.fold_in(key_of[14], 71), 0)
    first_moments = draw_first_moments(jax.random.fold_in(key_of[14], 71), 0)
    second_moments = draw_second_moments(jax.random.fold_in(key_of[14], 71), 0)
    owners = jax.vmap(lambda own: jax.random.permutation(own, N_DP))(jax.random.split(key_of[8], SLICES)).reshape((SLICES, N_DP)).astype(jnp.int32)
    left_basis = draw_left_basis(jax.random.fold_in(key_of[14], 71), 0)
    right_basis = draw_right_basis(jax.random.fold_in(key_of[14], 71), 0)
    biases = bell_draw(key_of[11], (BROWS, D), 0.3, 2.5, ((1, 4),), jnp.float32)
    bias_first = draw_bias_first(jax.random.fold_in(key_of[14], 71), 0)
    bias_second = draw_bias_second(jax.random.fold_in(key_of[14], 71), 0)
    return dict(block_in=block_in, out_grad=out_grad, lengths=lengths, group_ids=group_ids, time_embed=time_embed, weights=weights, first_moments=first_moments, second_moments=second_moments, owners=owners, left_basis=left_basis, right_basis=right_basis, biases=biases, bias_first=bias_first, bias_second=bias_second)


@jax.custom_vjp
def low(v):
    return lax.optimization_barrier(v.astype(jnp.bfloat16)).astype(jnp.float32)

@jax.custom_vjp
def low_back(v):
    return v

def low_keep(v):
    return (low(v), None)

def low_pass(kept, grad):
    return (grad,)

def back_keep(v):
    return (v, None)

def back_low(kept, grad):
    return (low(grad),)
low.defvjp(low_keep, low_pass)
low_back.defvjp(back_keep, back_low)
norm_epsilon = 1e-06
soap_first = 0.95
soap_second = 0.95
soap_epsilon = 1e-08
soap_rate = 0.05
soap_decay = 0.01
vector_first = 0.9
vector_second = 0.999
vector_epsilon = 1e-08
vector_rate = 0.1
masked_score = -1e+30

def layer_norm(values):
    centre = values - lax.optimization_barrier(jnp.mean(values, axis=-1, keepdims=True))
    spread = lax.optimization_barrier(jnp.mean(centre * centre, axis=-1, keepdims=True))
    return centre * lax.rsqrt(spread + norm_epsilon)

def rotary(values):
    half_dim = HEAD_DIM // 2
    places = jnp.arange(LEN, dtype=jnp.float32)
    frequencies = 10000.0 ** (-(jnp.arange(half_dim, dtype=jnp.float32) * 2.0 / HEAD_DIM))
    angles = places[:, None] * frequencies[None, :]
    cosine_table = jnp.cos(angles)[:, None, :]
    sine_table = jnp.sin(angles)[:, None, :]
    pair_view = values.reshape(LEN, values.shape[1], half_dim, 2)
    even_part = pair_view[..., 0]
    odd_part = pair_view[..., 1]
    turned = jnp.stack([even_part * cosine_table - odd_part * sine_table, odd_part * cosine_table + even_part * sine_table], axis=-1)
    return turned.reshape(values.shape)

def true_order(stored, owners):
    blocks = stored.reshape(N_DP, DSH, SLICES, stored.shape[2])
    picked = [jnp.take(blocks[:, :, slot_index, :], owners[slot_index], axis=0) for slot_index in range(SLICES)]
    return jnp.stack(picked, axis=2).reshape(stored.shape)

def stored_order(values, owners):
    blocks = values.reshape(N_DP, DSH, SLICES, values.shape[2])
    placed = [jnp.take(blocks[:, :, slot_index, :], jnp.argsort(owners[slot_index]), axis=0) for slot_index in range(SLICES)]
    return jnp.stack(placed, axis=2).reshape(values.shape)

def utterance(frame_rows, mod_row, length, matrices, shifts):
    highest = lax.Precision.HIGHEST
    valid_rows = jnp.arange(LEN) < length
    keep_rows = valid_rows.astype(frame_rows.dtype)[:, None]
    normed_in = low(layer_norm(frame_rows) * (1.0 + mod_row[1]) + mod_row[0])
    query_pre = low_back(jnp.dot(normed_in, matrices[:, 0, :], precision=highest) + shifts[0])
    key_pre = low_back(jnp.dot(normed_in, matrices[:, 1, :], precision=highest) + shifts[1])
    values_in = low(low_back(jnp.dot(normed_in, matrices[:, 2, :], precision=highest) + shifts[2]))
    queries = low(rotary(query_pre.reshape(LEN, HEADS, HEAD_DIM)))
    keys_in = low(rotary(key_pre.reshape(LEN, HEADS, HEAD_DIM)))
    values_in = values_in.reshape(LEN, HEADS, HEAD_DIM)
    scores = low_back(jnp.einsum('qhd,khd->hqk', queries, keys_in, precision=highest) * HEAD_DIM ** (-0.5))
    scores = jnp.where(valid_rows[None, None, :], scores, masked_score)
    chances = low(jax.nn.softmax(scores, axis=-1))
    mixed = low(low_back(jnp.einsum('hqk,khd->qhd', chances, values_in, precision=highest))).reshape(LEN, D)
    attended = low_back(jnp.dot(mixed, matrices[:, 3, :].T, precision=highest) + shifts[3]) * keep_rows
    middle = frame_rows + mod_row[2] * attended
    normed_mid = low(layer_norm(middle) * (1.0 + mod_row[4]) + mod_row[3])
    hidden = low_back(jnp.einsum('td,dec->tec', normed_mid, matrices[:, 4:6, :], precision=highest) + shifts[4:6])
    active = low(jax.nn.gelu(hidden, approximate=True))
    fed_rows = low_back(jnp.einsum('tec,oec->to', active, matrices[:, 6:8, :], precision=highest) + shifts[6])
    return middle + mod_row[5] * fed_rows

def reference(block_in, out_grad, lengths, group_ids, time_embed, weights, first_moments, second_moments, owners, left_basis, right_basis, biases, bias_first, bias_second):
    highest = lax.Precision.HIGHEST
    condition = low(jax.nn.silu(time_embed[group_ids]))
    rounded = true_order(weights, owners).astype(jnp.bfloat16).astype(jnp.float32)

    def forward(inputs, matrices, shifts):
        mods = jnp.einsum('ud,dkc->ukc', condition, matrices[:, 8:, :], precision=highest) + shifts[7:]

        def one_utterance(pieces):
            return utterance(pieces[0], pieces[1], pieces[2], matrices, shifts)
        outputs = lax.map(jax.checkpoint(one_utterance), (inputs.reshape(UTTS, LEN, D), mods, lengths))
        return outputs.reshape(TOKENS, D)
    result, pullback = jax.vjp(forward, block_in.astype(jnp.float32), rounded, biases)
    grad_in, grad_matrices, grad_biases = pullback(out_grad.astype(jnp.float32))
    grad_stored = stored_order(grad_matrices, owners)
    grad_blocks = grad_stored.reshape(N_DP, DSH, SLICES, N_MP, CSH)
    left_blocks = left_basis.reshape(SLICES, N_DP, DSH, DSH)
    right_blocks = right_basis.reshape(SLICES, N_MP, CSH, CSH)
    turned = jnp.einsum('kaij,aikbc->ajkbc', left_blocks, grad_blocks, precision=highest)
    turned = jnp.einsum('ajkbc,kbce->ajkbe', turned, right_blocks, precision=highest).reshape(D, SLICES, D)
    first_new = soap_first * first_moments + (1.0 - soap_first) * turned
    second_new = soap_second * second_moments + (1.0 - soap_second) * turned * turned
    direction = first_new / (1.0 - soap_first ** STEP) / (jnp.sqrt(second_new / (1.0 - soap_second ** STEP)) + soap_epsilon)
    rotated_back = jnp.einsum('kaij,ajkbe->aikbe', left_blocks, direction.reshape(N_DP, DSH, SLICES, N_MP, CSH), precision=highest)
    rotated_back = jnp.einsum('aikbe,kbce->aikbc', rotated_back, right_blocks, precision=highest).reshape(D, SLICES, D)
    new_weights = weights - soap_rate * (rotated_back + soap_decay * weights)
    bias_first_new = vector_first * bias_first + (1.0 - vector_first) * grad_biases
    bias_second_new = vector_second * bias_second + (1.0 - vector_second) * grad_biases * grad_biases
    new_biases = biases - vector_rate * (bias_first_new / (1.0 - vector_first ** STEP)) / (jnp.sqrt(bias_second_new / (1.0 - vector_second ** STEP)) + vector_epsilon)
    return (result.astype(jnp.bfloat16), grad_in, grad_stored, first_new, second_new, new_weights, new_weights.astype(jnp.bfloat16), bias_first_new, bias_second_new, new_biases)
```

```python
import functools
import math

import jax
import jax.numpy as jnp
from jax import lax
from jax.experimental import pallas as pl
from jax.experimental.pallas import tpu as pltpu
from jax.sharding import Mesh
from jax.sharding import PartitionSpec as P

D = 1024
HEAD_DIM = 64
LEN = 1024
GROUPS = 8
STEP = 10
CW = 256
TB = 256
NT = LEN // TB
BF = jnp.bfloat16
F32 = jnp.float32
LOG2E = math.log2(math.e)
LN2 = math.log(2.0)

norm_epsilon = 1e-06
soap_first = 0.95
soap_second = 0.95
soap_epsilon = 1e-08
soap_rate = 0.05
soap_decay = 0.01
vector_first = 0.9
vector_second = 0.999
vector_epsilon = 1e-08
vector_rate = 0.1
masked_score = -1e30
VMEM_LIMIT = 60 * 1024 * 1024

SWAP = [(0, 1), (1, 0)]


def params(n=1):
    return pltpu.CompilerParams(
        dimension_semantics=("arbitrary",) * n, vmem_limit_bytes=VMEM_LIMIT
    )


def nt_dot(a, b):
    return lax.dot_general(a, b, (((1,), (1,)), ((), ())), preferred_element_type=F32)


def nn_dot(a, b):
    return lax.dot_general(a, b, (((1,), (0,)), ((), ())), preferred_element_type=F32)


def whole(shape):
    return pl.BlockSpec(shape, lambda *_: (0,) * len(shape))


def rows_spec(width):
    return pl.BlockSpec((TB, width), lambda i, *_: (i, 0))


ANY = pl.BlockSpec(memory_space=pl.ANY)


def cost(flops, nbytes, trans=0):
    return pl.CostEstimate(flops=int(flops), bytes_accessed=int(nbytes), transcendentals=int(trans))


def fetch_weights(meta, rowtab, arrays, dest, sem, mats, base, start):
    n_dp, _, rows, _ = arrays[0].shape
    y = meta[0]
    for other in range(2):
        col = y if other == 0 else 1 - y
        for mat in range(mats):

            def step(slot, carry, other=other, mat=mat, col=col):
                first = pl.multiple_of(rowtab[base + mat, slot] * rows, rows)
                copy = pltpu.make_async_copy(
                    arrays[other].at[slot, base % 4 + mat],
                    dest.at[mat, col, pl.ds(first, rows), :],
                    sem,
                )
                if start:
                    copy.start()
                else:
                    copy.wait()
                return carry

            lax.fori_loop(0, n_dp, step, 0, unroll=n_dp <= 8)


def store_grads(slottab, staged, target, sem, mat, local, start):
    n_dp, _, rows, _ = target.shape

    def step(block, carry):
        copy = pltpu.make_async_copy(
            staged.at[pl.ds(pl.multiple_of(block * rows, rows), rows), :],
            target.at[slottab[mat, block], local],
            sem,
        )
        if start:
            copy.start()
        else:
            copy.wait()
        return carry

    lax.fori_loop(0, n_dp, step, 0, unroll=n_dp <= 8)


def layer_norm(x):
    mean = jnp.mean(x, axis=1, keepdims=True)
    centre = x - mean
    var = jnp.mean(centre * centre, axis=1, keepdims=True)
    inv = lax.rsqrt(var + norm_epsilon)
    return centre * inv, inv


def prep_kernel(w_ref, cond_ref, wp_ref, mod_ref):
    for k in range(8):
        wp_ref[k] = w_ref[:, k, :].astype(BF)
    for c in range(6):
        mod_ref[c] = nn_dot(cond_ref[c], w_ref[:, 8 + c, :].astype(BF))


def prep(weights, condk):
    rows = weights.shape[0]
    return pl.pallas_call(
        prep_kernel,
        out_shape=(
            jax.ShapeDtypeStruct((8, rows, CW), BF),
            jax.ShapeDtypeStruct((6, GROUPS, CW), F32),
        ),
        grid=(1,),
        in_specs=[whole(weights.shape), whole(condk.shape)],
        out_specs=(whole((8, rows, CW)), whole((6, GROUPS, CW))),
        compiler_params=params(),
        cost_estimate=cost(2e6, weights.size * 6),
        name="prep",
    )(weights, condk)


def rope(x, ct, s1, s2, sign):
    width = x.shape[1]
    up = pltpu.roll(x, 1, 1)
    down = pltpu.roll(x, width - 1, 1)
    reps = width // 128
    ct = jnp.concatenate([ct] * reps, axis=1) if reps > 1 else ct
    s1 = jnp.concatenate([s1] * reps, axis=1) if reps > 1 else s1
    s2 = jnp.concatenate([s2] * reps, axis=1) if reps > 1 else s2
    turn = up * s1 + down * s2
    return x * ct + turn if sign > 0 else x * ct - turn


def qkv_kernel(meta, rowtab, x_ref, vec_ref, ct_ref, s1_ref, s2_ref, wa, wb, h1_ref, q_ref, k_ref, v_ref, wsc, sem):
    @pl.when(pl.program_id(0) == 0)
    def _():
        fetch_weights(meta, rowtab, (wa, wb), wsc, sem, 3, 0, True)

    n1, _ = layer_norm(x_ref[...].astype(F32))
    h1 = (n1 * (1.0 + vec_ref[8:9, :]) + vec_ref[7:8, :]).astype(BF)
    h1_ref[...] = h1

    @pl.when(pl.program_id(0) == 0)
    def _():
        fetch_weights(meta, rowtab, (wa, wb), wsc, sem, 3, 0, False)

    c = meta[1]
    ct, s1, s2 = ct_ref[...], s1_ref[...], s2_ref[...]
    for col in range(2):
        off = pl.multiple_of((col * 2 + c) * CW, CW)
        for k, out in ((0, q_ref), (1, k_ref), (2, v_ref)):
            acc = nn_dot(h1, wsc[k, col]) + vec_ref[k : k + 1, pl.ds(off, CW)]
            if k < 2:
                acc = rope(acc, ct, s1, s2, 1.0)
            if k == 0:
                acc = acc * (LOG2E * HEAD_DIM**-0.5)
            out[:, col * CW : (col + 1) * CW] = acc.astype(BF)


def qkv(meta, rowtab, x, vec, tables, wa, wb):
    half = 2 * CW
    return pl.pallas_call(
        qkv_kernel,
        out_shape=(jax.ShapeDtypeStruct((LEN, D), BF),) + (jax.ShapeDtypeStruct((LEN, half), BF),) * 3,
        grid_spec=pltpu.PrefetchScalarGridSpec(
            num_scalar_prefetch=2,
            grid=(NT,),
            in_specs=[rows_spec(D), whole(vec.shape)] + [rows_spec(128)] * 3 + [ANY, ANY],
            out_specs=(rows_spec(D),) + (rows_spec(half),) * 3,
            scratch_shapes=[pltpu.VMEM((3, 2, D, CW), BF), pltpu.SemaphoreType.DMA(())],
        ),
        compiler_params=params(),
        cost_estimate=cost(2 * LEN * D * 3 * half, 12e6),
        name="qkv",
    )(meta, rowtab, x, vec, *tables, wa, wb)


def lane_iota(rows):
    return lax.broadcasted_iota(jnp.int32, (rows, 128), 1)


def split3(v):
    hi = v.astype(BF).astype(F32)
    mid = (v - hi).astype(BF).astype(F32)
    return hi, mid, v - hi - mid


def attend_kernel(meta, rowtab, q_ref, k_ref, v_ref, kaug_ref, wa, wb, o_ref, qaug_ref, pa_ref, wsc, osc, sem):
    @pl.when(pl.program_id(0) == 0)
    def _():
        fetch_weights(meta, rowtab, (wa, wb), wsc, sem, 1, 3, True)

    lane = lane_iota(TB)
    first = lane < HEAD_DIM
    mask_one = jnp.where(lane == 3, 1.0, 0.0).astype(BF)
    ones = jnp.ones((LEN, 128), BF)
    kaug = kaug_ref[...]

    def pair(p, carry):
        off = pl.multiple_of(p * 128, 128)
        q2 = q_ref[:, pl.ds(off, 128)]
        kcat = jnp.concatenate([k_ref[:, pl.ds(off, 128)], kaug], axis=1)
        vcat = jnp.concatenate([v_ref[:, pl.ds(off, 128)], ones], axis=1)
        outs = []
        for head in range(2):
            mine = first if head == 0 else jnp.logical_not(first)
            qm = jnp.where(mine, q2.astype(F32), 0.0).astype(BF)
            s = nt_dot(jnp.concatenate([qm, mask_one], axis=1), kcat)
            top = jnp.max(s, axis=1, keepdims=True)
            probs = jnp.exp2(s - top).astype(BF)
            acc = nn_dot(probs, vcat)
            total = acc[:, 128:256]
            outs.append(acc[:, :128] / total)
            lse = jnp.broadcast_to(top, (TB, 128)) + jnp.log(total) * LOG2E
            hi, mid, lo = split3(-lse)
            aug = jnp.where(lane == 0, hi, jnp.where(lane == 1, mid, jnp.where(lane == 2, lo, jnp.where(lane == 3, 1.0, 0.0))))
            qaug_ref[2 * p + head] = aug.astype(BF)
        osc[:, pl.ds(off, 128)] = jnp.where(first, outs[0], outs[1]).astype(BF)
        return carry

    lax.fori_loop(0, 4, pair, 0)
    o_ref[...] = osc[...]

    @pl.when(pl.program_id(0) == 0)
    def _():
        fetch_weights(meta, rowtab, (wa, wb), wsc, sem, 1, 3, False)

    pa = nt_dot(osc[:, :CW], wsc[0, 0]) + nt_dot(osc[:, CW:], wsc[0, 1])
    pa_ref[...] = pa.astype(BF)


def attend(meta, rowtab, q, k, v, kaug, wa, wb):
    half = 2 * CW
    return pl.pallas_call(
        attend_kernel,
        out_shape=(
            jax.ShapeDtypeStruct((LEN, half), BF),
            jax.ShapeDtypeStruct((8, LEN, 128), BF),
            jax.ShapeDtypeStruct((LEN, D), BF),
        ),
        grid_spec=pltpu.PrefetchScalarGridSpec(
            num_scalar_prefetch=2,
            grid=(NT,),
            in_specs=[rows_spec(half), whole((LEN, half)), whole((LEN, half)), whole((LEN, 128)), ANY, ANY],
            out_specs=(rows_spec(half), pl.BlockSpec((8, TB, 128), lambda i, *_: (0, i, 0)), rows_spec(D)),
            scratch_shapes=[
                pltpu.VMEM((1, 2, D, CW), BF),
                pltpu.VMEM((TB, half), BF),
                pltpu.SemaphoreType.DMA(()),
            ],
        ),
        compiler_params=params(),
        cost_estimate=cost(12e9, 10e6, 8e6),
        name="attend",
    )(meta, rowtab, q, k, v, kaug, wa, wb)


def middle_rows(x, pa, pb, vec, valid):
    a = (pa.astype(F32) + pb.astype(F32) + vec[3:4, :]) * valid
    return a, x.astype(F32) + vec[9:10, :] * a


def valid_rows(start, rows, length):
    return (start + lax.broadcasted_iota(jnp.int32, (rows, 1), 0) < length).astype(F32)


def gelu_parts(v):
    c0 = math.sqrt(2.0 / math.pi)
    sq = v * v
    t = jnp.tanh(v * (c0 + (c0 * 0.044715) * sq))
    half = 0.5 * (1.0 + t)
    slope = half + (0.5 * v) * (1.0 - t * t) * (c0 + (3.0 * c0 * 0.044715) * sq)
    return v * half, slope


def feed_kernel(
    meta, rowtab, slottab, x_ref, pa_ref, pb_ref, g_ref, vec_ref, wa, wb,
    pf_ref, pg_ref, gb_ref, keep_ref, send_ref,
    wsc, h2, gf, h2t, gft, facc, gacc, zsc, ghsc, stage, sem, gsem,
):
    y, c, length = meta[0], meta[1], meta[2]
    step = pl.program_id(0)
    other = jnp.where(step < 2, 1, 0)
    half = step % 2
    col = jnp.bitwise_xor(other, y)

    @pl.when(step == 0)
    def _():
        fetch_weights(meta, rowtab, (wa, wb), wsc, sem, 4, 4, True)
        gb_ref[...] = jnp.zeros_like(gb_ref)

        def rows(i, carry):
            at = pl.ds(pl.multiple_of(i * TB, TB), TB)
            _, x1 = middle_rows(x_ref[at, :], pa_ref[at, :], pb_ref[at, :], vec_ref, valid_rows(i * TB, TB, length))
            n2, _ = layer_norm(x1)
            hh = (n2 * (1.0 + vec_ref[11:12, :]) + vec_ref[10:11, :]).astype(BF)
            gg = (vec_ref[12:13, :] * g_ref[at, :].astype(F32)).astype(BF)
            h2[at, :] = hh
            gf[at, :] = gg
            h2t[:, at] = hh.T
            gft[:, at] = gg.T
            gb_ref[2:3, :] += jnp.sum(gg.astype(F32), axis=0, keepdims=True)
            return carry

        lax.fori_loop(0, NT, rows, 0)
        fetch_weights(meta, rowtab, (wa, wb), wsc, sem, 4, 4, False)

    off = pl.multiple_of((col * 2 + c) * CW, CW)
    w_in = wsc.at[half, col]
    w_out = wsc.at[2 + half, col]
    bias = vec_ref[pl.ds(4 + half, 1), pl.ds(off, CW)]

    def rows(i, total):
        at = pl.ds(pl.multiple_of(i * TB, TB), TB)
        z, slope = gelu_parts(nn_dot(h2[at, :], w_in[...]) + bias)
        zb = z.astype(BF)
        gh = nn_dot(gf[at, :], w_out[...]) * slope
        ghb = gh.astype(BF)
        zsc[at, :] = zb
        ghsc[at, :] = ghb
        fpart = nt_dot(zb, w_out[...])
        gpart = nt_dot(ghb, w_in[...])

        @pl.when(step == 0)
        def _():
            facc[at, :] = fpart
            gacc[at, :] = gpart

        @pl.when(step > 0)
        def _():
            facc[at, :] += fpart
            gacc[at, :] += gpart

        return total + jnp.sum(ghb.astype(F32), axis=0, keepdims=True)

    total = lax.fori_loop(0, NT, rows, jnp.zeros((1, CW), F32))
    gb_ref[pl.ds(half, 1), pl.ds(off, CW)] = total

    def copies(which, start):
        local = half + 2 * which

        @pl.when(other == 0)
        def _():
            store_grads(slottab, stage.at[which], keep_ref, gsem, 4 + local, local, start)

        @pl.when(other == 1)
        def _():
            store_grads(slottab, stage.at[which], send_ref, gsem, 4 + local, local, start)

    @pl.when(step > 0)
    def _():
        for which in range(2):
            store_grads(slottab, stage.at[which], keep_ref, gsem, 4, 0, False)

    for which, (lhs, rhs) in enumerate(((h2t, ghsc), (gft, zsc))):
        for r in range(NT):
            stage[which, r * TB : (r + 1) * TB, :] = nn_dot(lhs[r * TB : (r + 1) * TB, :], rhs[...]).astype(BF)
        copies(which, True)

    @pl.when(step == 3)
    def _():
        for which in range(2):
            store_grads(slottab, stage.at[which], keep_ref, gsem, 4, 0, False)
        pf_ref[...] = facc[...].astype(BF)
        pg_ref[...] = gacc[...].astype(BF)


def feed(meta, rowtab, slottab, x, pa, pb, g, vec, wa, wb):
    grads = jax.ShapeDtypeStruct(wa.shape[:1] + (4,) + wa.shape[2:], BF)
    return pl.pallas_call(
        feed_kernel,
        out_shape=(
            jax.ShapeDtypeStruct((LEN, D), BF),
            jax.ShapeDtypeStruct((LEN, D), BF),
            jax.ShapeDtypeStruct((8, D), F32),
            grads,
            grads,
        ),
        grid_spec=pltpu.PrefetchScalarGridSpec(
            num_scalar_prefetch=3,
            grid=(4,),
            in_specs=[whole((LEN, D))] * 4 + [whole(vec.shape), ANY, ANY],
            out_specs=(whole((LEN, D)), whole((LEN, D)), whole((8, D)), ANY, ANY),
            scratch_shapes=[
                pltpu.VMEM((4, 2, D, CW), BF),
                pltpu.VMEM((LEN, D), BF),
                pltpu.VMEM((LEN, D), BF),
                pltpu.VMEM((D, LEN), BF),
                pltpu.VMEM((D, LEN), BF),
                pltpu.VMEM((LEN, D), F32),
                pltpu.VMEM((LEN, D), F32),
                pltpu.VMEM((LEN, CW), BF),
                pltpu.VMEM((LEN, CW), BF),
                pltpu.VMEM((2, D, CW), BF),
                pltpu.SemaphoreType.DMA(()),
                pltpu.SemaphoreType.DMA(()),
            ],
        ),
        compiler_params=params(),
        cost_estimate=cost(2 * LEN * D * D * 6, 24e6, 1e6),
        name="feed",
    )(meta, rowtab, slottab, x, pa, pb, g, vec, wa, wb)


def proj_back_kernel(
    meta, rowtab, slottab, x_ref, pa_ref, pb_ref, g_ref, ga_ref, gb_ref, o_ref, vec_ref, wa, wb,
    gx_ref, go_ref, sums_ref, keep_ref, send_ref, wsc, wacc, stage, sem, gsem,
):
    y, length = meta[0], meta[2]
    step = pl.program_id(0)

    @pl.when(step == 0)
    def _():
        fetch_weights(meta, rowtab, (wa, wb), wsc, sem, 1, 3, True)
        sums_ref[...] = jnp.zeros_like(sums_ref)

    a, x1 = middle_rows(x_ref[...], pa_ref[...], pb_ref[...], vec_ref, valid_rows(step * TB, TB, length))
    n2, inv = layer_norm(x1)
    gh2 = ga_ref[...].astype(F32) + gb_ref[...].astype(F32)
    gn = gh2 * (1.0 + vec_ref[11:12, :])
    m0 = jnp.mean(gn, axis=1, keepdims=True)
    m1 = jnp.mean(gn * n2, axis=1, keepdims=True)
    gx = g_ref[...].astype(F32) + (gn - m0 - n2 * m1) * inv
    gx_ref[...] = gx
    gatt = (vec_ref[9:10, :] * gx * valid_rows(step * TB, TB, length)).astype(BF)
    sums_ref[0:1, :] += jnp.sum(gx * a, axis=0, keepdims=True)
    sums_ref[1:2, :] += jnp.sum(gh2, axis=0, keepdims=True)
    sums_ref[2:3, :] += jnp.sum(gh2 * n2, axis=0, keepdims=True)
    sums_ref[3:4, :] += jnp.sum(gatt.astype(F32), axis=0, keepdims=True)

    @pl.when(step == 0)
    def _():
        fetch_weights(meta, rowtab, (wa, wb), wsc, sem, 1, 3, False)

    go_ref[:, :CW] = nn_dot(gatt, wsc[0, 0]).astype(BF)
    go_ref[:, CW:] = nn_dot(gatt, wsc[0, 1]).astype(BF)
    part = nn_dot(gatt.T, o_ref[...])

    @pl.when(step == 0)
    def _():
        wacc[...] = part

    @pl.when(step > 0)
    def _():
        wacc[...] += part

    @pl.when(step == NT - 1)
    def _():
        for col in range(2):
            stage[col] = wacc[:, col * CW : (col + 1) * CW].astype(BF)
        store_grads(slottab, stage.at[y], keep_ref, gsem, 3, 0, True)
        store_grads(slottab, stage.at[1 - y], send_ref, gsem, 3, 0, True)
        store_grads(slottab, stage.at[y], keep_ref, gsem, 3, 0, False)
        store_grads(slottab, stage.at[1 - y], send_ref, gsem, 3, 0, False)


def proj_back(meta, rowtab, slottab, x, pa, pb, g, ga, gb, o, vec, wa, wb):
    grads = jax.ShapeDtypeStruct(wa.shape[:1] + (1,) + wa.shape[2:], BF)
    half = 2 * CW
    return pl.pallas_call(
        proj_back_kernel,
        out_shape=(
            jax.ShapeDtypeStruct((LEN, D), F32),
            jax.ShapeDtypeStruct((LEN, half), BF),
            jax.ShapeDtypeStruct((8, D), F32),
            grads,
            grads,
        ),
        grid_spec=pltpu.PrefetchScalarGridSpec(
            num_scalar_prefetch=3,
            grid=(NT,),
            in_specs=[rows_spec(D)] * 6 + [rows_spec(half), whole(vec.shape), ANY, ANY],
            out_specs=(rows_spec(D), rows_spec(half), whole((8, D)), ANY, ANY),
            scratch_shapes=[
                pltpu.VMEM((1, 2, D, CW), BF),
                pltpu.VMEM((D, half), F32),
                pltpu.VMEM((2, D, CW), BF),
                pltpu.SemaphoreType.DMA(()),
                pltpu.SemaphoreType.DMA(()),
            ],
        ),
        compiler_params=params(),
        cost_estimate=cost(2 * LEN * D * half * 2, 20e6),
        name="proj_back",
    )(meta, rowtab, slottab, x, pa, pb, g, ga, gb, o, vec, wa, wb)


def attend_back_kernel(
    q_ref, k_ref, v_ref, go_ref, o_ref, qaug_ref, kaug_ref, ct_ref, s1_ref, s2_ref,
    gq_ref, gk_ref, gv_ref, gb_ref, qcat, gocat, kt, gqt,
):
    lane = lane_iota(LEN)
    first = lane < HEAD_DIM
    lane_kb = lane_iota(TB)
    first_kb = lane_kb < HEAD_DIM
    vaug = jnp.where(lane_kb < 3, 1.0, 0.0).astype(BF)
    go2 = go_ref[...].astype(F32)
    q2 = q_ref[...].astype(F32)
    dots = go2 * o_ref[...].astype(F32)
    for head in range(2):
        mine = first if head == 0 else jnp.logical_not(first)
        qcat[head, :, :128] = jnp.where(mine, q2, 0.0).astype(BF)
        qcat[head, :, 128:] = qaug_ref[head]
        gocat[head, :, :128] = jnp.where(mine, go2, 0.0).astype(BF)
        inner = jnp.sum(jnp.where(mine, dots, 0.0), axis=1, keepdims=True)
        hi, mid, lo = split3(-jnp.broadcast_to(inner, (LEN, 128)))
        aug = jnp.where(lane == 0, hi, jnp.where(lane == 1, mid, jnp.where(lane == 2, lo, 0.0)))
        gocat[head, :, 128:] = aug.astype(BF)
    kt[...] = k_ref[...].T
    gqt[...] = jnp.zeros_like(gqt)
    gb_ref[...] = jnp.zeros_like(gb_ref)

    for kb in range(NT):
        at = slice(kb * TB, (kb + 1) * TB)
        kcat = jnp.concatenate([k_ref[at, :], kaug_ref[at, :]], axis=1)
        vcat = jnp.concatenate([v_ref[at, :], vaug], axis=1)
        gvs, gks = [], []
        for head in range(2):
            pt = jnp.exp2(nt_dot(kcat, qcat[head]))
            gpt = nt_dot(vcat, gocat[head])
            gst = (pt * gpt).astype(BF)
            gvs.append(nn_dot(pt.astype(BF), go_ref[...]))
            gks.append(nn_dot(gst, q_ref[...]))
            rows = slice(head * HEAD_DIM, (head + 1) * HEAD_DIM)
            gqt[rows, :] += nn_dot(kt[rows, at], gst)
        gv = jnp.where(first_kb, gvs[0], gvs[1]).astype(BF)
        gk = jnp.where(first_kb, gks[0], gks[1]) * LN2
        gk = rope(gk, ct_ref[at, :], s1_ref[at, :], s2_ref[at, :], -1.0).astype(BF)
        gv_ref[at, :] = gv
        gk_ref[at, :] = gk
        gb_ref[1:2, :] += jnp.sum(gk.astype(F32), axis=0, keepdims=True)
        gb_ref[2:3, :] += jnp.sum(gv.astype(F32), axis=0, keepdims=True)
    gq = gqt[...].T * (HEAD_DIM**-0.5)
    gq = rope(gq, ct_ref[...], s1_ref[...], s2_ref[...], -1.0).astype(BF)
    gq_ref[...] = gq
    gb_ref[0:1, :] += jnp.sum(gq.astype(F32), axis=0, keepdims=True)


def attend_back(q, k, v, go, o, qaug, kaug, tables):
    half = 2 * CW
    pair = pl.BlockSpec((LEN, 128), lambda i: (0, i))
    return pl.pallas_call(
        attend_back_kernel,
        out_shape=(jax.ShapeDtypeStruct((LEN, half), BF),) * 3 + (jax.ShapeDtypeStruct((8, half), F32),),
        grid=(4,),
        in_specs=[pair] * 5
        + [pl.BlockSpec((2, LEN, 128), lambda i: (i, 0, 0))]
        + [whole((LEN, 128))] * 4,
        out_specs=(pair,) * 3 + (pl.BlockSpec((8, 128), lambda i: (0, i)),),
        scratch_shapes=[
            pltpu.VMEM((2, LEN, 256), BF),
            pltpu.VMEM((2, LEN, 256), BF),
            pltpu.VMEM((128, LEN), BF),
            pltpu.VMEM((128, LEN), F32),
        ],
        compiler_params=params(),
        cost_estimate=cost(30e9, 12e6, 8e6),
        name="attend_back",
    )(q, k, v, go, o, qaug, kaug, *tables)


def qkv_back_kernel(
    meta, rowtab, slottab, h1_ref, gq_ref, gk_ref, gv_ref, wa, wb, pg_ref, keep_ref, send_ref,
    wsc, h1t, stage, sem, gsem,
):
    y = meta[0]
    fetch_weights(meta, rowtab, (wa, wb), wsc, sem, 3, 0, True)

    def turn(i, carry):
        at = pl.ds(pl.multiple_of(i * TB, TB), TB)
        h1t[:, at] = h1_ref[at, :].T
        return carry

    lax.fori_loop(0, NT, turn, 0)
    for yr in (1, 0):
        col = jnp.bitwise_xor(y, yr)
        off = pl.multiple_of(col * CW, CW)
        target = send_ref if yr == 1 else keep_ref
        for k, src in enumerate((gq_ref, gk_ref, gv_ref)):
            rhs = src[:, pl.ds(off, CW)]

            def rows(i, carry, k=k, rhs=rhs, yr=yr):
                at = pl.ds(pl.multiple_of(i * TB, TB), TB)
                stage[yr, k, at, :] = nn_dot(h1t[at, :], rhs).astype(BF)
                return carry

            lax.fori_loop(0, NT, rows, 0)
            store_grads(slottab, stage.at[yr, k], target, gsem, k, k, True)
    fetch_weights(meta, rowtab, (wa, wb), wsc, sem, 3, 0, False)

    def rows(i, carry):
        at = pl.ds(pl.multiple_of(i * TB, TB), TB)
        acc = jnp.zeros((TB, D), F32)
        for k, src in enumerate((gq_ref, gk_ref, gv_ref)):
            for col in range(2):
                acc += nt_dot(src[at, col * CW : (col + 1) * CW], wsc[k, col])
        pg_ref[at, :] = acc.astype(BF)
        return carry

    lax.fori_loop(0, NT, rows, 0)
    for yr in (1, 0):
        target = send_ref if yr == 1 else keep_ref
        for k in range(3):
            store_grads(slottab, stage.at[yr, k], target, gsem, k, k, False)


def qkv_back(meta, rowtab, slottab, h1, gq, gk, gv, wa, wb):
    grads = jax.ShapeDtypeStruct(wa.shape[:1] + (3,) + wa.shape[2:], BF)
    half = 2 * CW
    return pl.pallas_call(
        qkv_back_kernel,
        out_shape=(jax.ShapeDtypeStruct((LEN, D), BF), grads, grads),
        grid_spec=pltpu.PrefetchScalarGridSpec(
            num_scalar_prefetch=3,
            grid=(1,),
            in_specs=[whole((LEN, D))] + [whole((LEN, half))] * 3 + [ANY, ANY],
            out_specs=(whole((LEN, D)), ANY, ANY),
            scratch_shapes=[
                pltpu.VMEM((3, 2, D, CW), BF),
                pltpu.VMEM((D, LEN), BF),
                pltpu.VMEM((2, 3, D, CW), BF),
                pltpu.SemaphoreType.DMA(()),
                pltpu.SemaphoreType.DMA(()),
            ],
        ),
        compiler_params=params(),
        cost_estimate=cost(2 * LEN * D * half * 6, 16e6),
        name="qkv_back",
    )(meta, rowtab, slottab, h1, gq, gk, gv, wa, wb)


def final_kernel(
    meta, x_ref, pa_ref, pb_ref, g_ref, fa_ref, fb_ref, ga_ref, gb_ref, gx_ref, vec_ref,
    outk_ref, outs_ref, gink_ref, gins_ref, sums_ref, osc, isc,
):
    y, c, length = meta[0], meta[1], meta[2]
    step = pl.program_id(0)

    @pl.when(step == 0)
    def _():
        sums_ref[...] = jnp.zeros_like(sums_ref)

    _, x1 = middle_rows(x_ref[...], pa_ref[...], pb_ref[...], vec_ref, valid_rows(step * TB, TB, length))
    f = fa_ref[...].astype(F32) + fb_ref[...].astype(F32) + vec_ref[6:7, :]
    osc[...] = x1 + vec_ref[12:13, :] * f
    n1, inv = layer_norm(x_ref[...].astype(F32))
    gh1 = ga_ref[...].astype(F32) + gb_ref[...].astype(F32)
    gn = gh1 * (1.0 + vec_ref[8:9, :])
    m0 = jnp.mean(gn, axis=1, keepdims=True)
    m1 = jnp.mean(gn * n1, axis=1, keepdims=True)
    isc[...] = gx_ref[...] + (gn - m0 - n1 * m1) * inv
    sums_ref[0:1, :] += jnp.sum(gh1, axis=0, keepdims=True)
    sums_ref[1:2, :] += jnp.sum(gh1 * n1, axis=0, keepdims=True)
    sums_ref[2:3, :] += jnp.sum(g_ref[...].astype(F32) * f, axis=0, keepdims=True)
    mine = pl.ds(pl.multiple_of((y * 2 + c) * CW, CW), CW)
    theirs = pl.ds(pl.multiple_of(((1 - y) * 2 + c) * CW, CW), CW)
    outk_ref[...] = osc[:, mine].astype(BF)
    outs_ref[...] = osc[:, theirs].astype(BF)
    gink_ref[...] = isc[:, mine]
    gins_ref[...] = isc[:, theirs].astype(BF)


def final(meta, x, pa, pb, g, fa, fb, ga, gb, gx, vec):
    return pl.pallas_call(
        final_kernel,
        out_shape=(
            jax.ShapeDtypeStruct((LEN, CW), BF),
            jax.ShapeDtypeStruct((LEN, CW), BF),
            jax.ShapeDtypeStruct((LEN, CW), F32),
            jax.ShapeDtypeStruct((LEN, CW), BF),
            jax.ShapeDtypeStruct((8, D), F32),
        ),
        grid_spec=pltpu.PrefetchScalarGridSpec(
            num_scalar_prefetch=1,
            grid=(NT,),
            in_specs=[rows_spec(D)] * 9 + [whole(vec.shape)],
            out_specs=(rows_spec(CW),) * 4 + (whole((8, D)),),
            scratch_shapes=[pltpu.VMEM((TB, D), F32), pltpu.VMEM((TB, D), F32)],
        ),
        compiler_params=params(),
        cost_estimate=cost(1e8, 22e6),
        name="final",
    )(meta, x, pa, pb, g, fa, fb, ga, gb, gx, vec)


def xor_pairs(size, step):
    return [(i, i ^ step) for i in range(size)]


def swap(v, axis):
    return lax.ppermute(v, axis, SWAP)


def true_blocks(mine, other_y, y, c):
    cm, cy = swap(mine, "c"), swap(other_y, "c")
    flip_c = c == 1
    own0, own1 = jnp.where(flip_c, cm, mine), jnp.where(flip_c, mine, cm)
    oth0, oth1 = jnp.where(flip_c, cy, other_y), jnp.where(flip_c, other_y, cy)
    flip_y = y == 1
    return (
        jnp.where(flip_y, oth0, own0),
        jnp.where(flip_y, oth1, own1),
        jnp.where(flip_y, own0, oth0),
        jnp.where(flip_y, own1, oth1),
    )


def rotary_tables():
    half_dim = HEAD_DIM // 2
    places = jnp.arange(LEN, dtype=F32)
    frequencies = 10000.0 ** (-(jnp.arange(half_dim, dtype=F32) * 2.0 / HEAD_DIM))
    angles = places[:, None] * frequencies[None, :]
    pairs = jnp.tile(jnp.repeat(angles, 2, axis=1), (1, 2))
    odd = (jnp.arange(128) % 2 == 1)[None, :]
    cos, sin = jnp.cos(pairs), jnp.sin(pairs)
    return cos, jnp.where(odd, sin, 0.0), jnp.where(odd, 0.0, -sin)


def body(fast, block_in, out_grad, lengths, group_ids, time_embed, weights, first_moments, second_moments,
         owners, left_basis, right_basis, biases, bias_first, bias_second):
    highest = lax.Precision.HIGHEST
    rows = weights.shape[0]
    n_dp = owners.shape[1]
    z, x, y, c = (lax.axis_index(name) for name in ("z", "x", "y", "c"))
    dp = z * 2 + x
    slots = jnp.arange(n_dp, dtype=jnp.int32)
    if fast:
        blocks_of = jnp.bitwise_xor(slots % 4, z) * 2 + jnp.bitwise_xor(slots // 4, x)
        slot_of = jnp.bitwise_xor(slots // 2, z) + 4 * jnp.bitwise_xor(slots % 2, x)
    else:
        blocks_of = slots
        slot_of = slots
    hits = owners[:, :, None] == blocks_of[None, None, :]
    rowtab = jnp.sum(jnp.where(hits, slots[None, :, None], 0), axis=1).astype(jnp.int32)
    slottab = jnp.sum(
        jnp.where(owners[:, :, None] == slots[None, None, :], slot_of[None, None, :], 0), axis=2
    ).astype(jnp.int32)
    meta = jnp.stack([y, c, lengths[y]]).astype(jnp.int32)

    cond = jax.nn.silu(time_embed).astype(BF)
    own_rows = (owners[8:] == dp).astype(F32)
    condk = jnp.sum(
        own_rows[:, None, :, None] * cond.astype(F32).reshape(1, GROUPS, n_dp, rows), axis=2
    ).astype(BF)
    own_weights, mod_part = prep(weights, condk)

    def to_chip(v):
        mine = lax.dynamic_slice_in_dim(v, y * LEN, LEN, 0)
        other = lax.dynamic_slice_in_dim(v, (1 - y) * LEN, LEN, 0)
        return jnp.concatenate(true_blocks(mine, swap(other, "y"), y, c), axis=1)

    def gather(piece):
        piece = piece[None]
        if fast:
            parts = [piece] + [lax.ppermute(piece, "z", xor_pairs(4, s)) for s in (1, 2, 3)]
            four = jnp.concatenate(parts, axis=0)
            own = jnp.concatenate([four, swap(four, "x")], axis=0)
        else:
            own = lax.all_gather(piece, ("z", "x"), axis=0, tiled=True)
        return own, swap(own, "y")

    xs = to_chip(block_in)
    w_attn = gather(own_weights[:4])
    w_feed = gather(own_weights[4:])
    gs = to_chip(out_grad)

    if fast:
        mod_all = mod_part
        for axis, size, step in (("x", 2, 1), ("z", 4, 1), ("z", 4, 2)):
            mod_all = mod_all + lax.ppermute(mod_all, axis, xor_pairs(size, step))
    else:
        mod_all = lax.psum(mod_part, ("z", "x"))

    def utterance_rows(index):
        hit = (jnp.arange(GROUPS) == group_ids[index]).astype(F32)
        mods = jnp.sum(mod_all * hit[None, :, None], axis=1) + biases[7:]
        return jnp.concatenate([biases[:7], mods, jnp.zeros((3, CW), F32)], axis=0)

    vec = jnp.concatenate(
        true_blocks(utterance_rows(y), swap(utterance_rows(1 - y), "y"), y, c), axis=1
    )
    tables = rotary_tables()
    lane = jnp.arange(128)[None, :]
    padded = (jnp.arange(LEN, dtype=jnp.int32) >= meta[2])[:, None]
    kaug = jnp.where(lane < 3, 1.0, jnp.where((lane == 3) & padded, masked_score, 0.0)).astype(BF)

    h1, q, k, v = qkv(meta, rowtab, xs, vec, tables, *w_attn)
    o, qaug, pa = attend(meta, rowtab, q, k, v, kaug, *w_attn)
    pb = swap(pa, "c")
    fa, g2a, gb_feed, keep_feed, send_feed = feed(meta, rowtab, slottab, xs, pa, pb, gs, vec, *w_feed)
    g2b = swap(g2a, "c")
    fb = swap(fa, "c")

    def scatter(keep, send):
        got = swap(send, "y")
        if fast:
            total = keep.astype(F32) + got.astype(F32)
            low = total[4:].astype(BF)
            four = total[:4] + swap(low, "x").astype(F32)
            own = four[0]
            for s in (1, 2, 3):
                own = own + lax.ppermute(four[s].astype(BF), "z", xor_pairs(4, s)).astype(F32)
            return own
        total = (keep.astype(F32) + got.astype(F32)).astype(BF)
        return lax.psum_scatter(total, ("z", "x"), scatter_dimension=0, tiled=True)[0].astype(F32)

    grads_feed = scatter(keep_feed, send_feed)
    gx, go, sums_mid, keep_proj, send_proj = proj_back(
        meta, rowtab, slottab, xs, pa, pb, gs, g2a, g2b, o, vec, *w_attn
    )
    grads_proj = scatter(keep_proj, send_proj)
    gq, gk, gv, gb_qkv = attend_back(q, k, v, go, o, qaug, kaug, tables)
    g1a, keep_qkv, send_qkv = qkv_back(meta, rowtab, slottab, h1, gq, gk, gv, *w_attn)
    g1b = swap(g1a, "c")
    grads_qkv = scatter(keep_qkv, send_qkv)
    out_keep, out_send, gin_keep, gin_send, sums_end = final(
        meta, xs, pa, pb, gs, fa, fb, g1a, g1b, gx, vec
    )
    out_got = swap(out_send, "y")
    gin_got = swap(gin_send, "y").astype(F32)

    def both(mine, other):
        return jnp.where(
            y == 0, jnp.concatenate([mine, other], axis=0), jnp.concatenate([other, mine], axis=0)
        )

    block_out = both(out_keep, out_got)
    input_grad = both(gin_keep, gin_got)

    local = jnp.stack(
        [
            jnp.concatenate(
                [
                    gb_qkv[:3, col * CW : (col + 1) * CW],
                    lax.dynamic_slice_in_dim(
                        jnp.concatenate(
                            [sums_mid[3:4], gb_feed[:3], sums_end[:2], sums_mid[:3], sums_end[2:3]], axis=0
                        ),
                        (col * 2 + c) * CW,
                        CW,
                        1,
                    ),
                ],
                axis=0,
            )
            for col in range(2)
        ]
    )
    hot = (jnp.arange(CW) == group_ids[y]).astype(F32)
    local = jnp.concatenate([local, jnp.broadcast_to(hot[None, None], (2, 3, CW))], axis=1)
    mine = jnp.where(y == 0, local[0], local[1])
    other = jnp.where(y == 0, local[1], local[0])
    vecs = jnp.stack([mine, swap(other, "y")])
    if fast:
        everything = [vecs]
        for zs in range(4):
            for xstep in range(2):
                if zs or xstep:
                    everything.append(
                        lax.ppermute(
                            vecs,
                            ("z", "x"),
                            [(i * 2 + j, (i ^ zs) * 2 + (j ^ xstep)) for i in range(4) for j in range(2)],
                        )
                    )
        everything = jnp.concatenate(everything, axis=0)
    else:
        everything = lax.all_gather(vecs, ("z", "x"), axis=0, tiled=True)
    bias_grad = jnp.sum(everything[:, :13], axis=0)
    grouped = jnp.einsum("ug,ukc->kgc", everything[:, 13, :GROUPS], everything[:, 7:13], precision=highest)
    grads_mod = jnp.einsum("kgr,kgc->krc", condk.astype(F32), grouped, precision=highest)
    reduced = jnp.concatenate([grads_qkv, grads_proj, grads_feed, grads_mod], axis=0)

    turned = jnp.einsum("kij,kic->kjc", left_basis, reduced, precision=highest)
    turned = jnp.einsum("kjc,kce->kje", turned, right_basis, precision=highest)
    first_old = jnp.transpose(first_moments, (1, 0, 2))
    second_old = jnp.transpose(second_moments, (1, 0, 2))
    first_new = soap_first * first_old + (1.0 - soap_first) * turned
    second_new = soap_second * second_old + (1.0 - soap_second) * turned * turned
    direction = (
        first_new
        / (1.0 - soap_first**STEP)
        / (jnp.sqrt(second_new / (1.0 - soap_second**STEP)) + soap_epsilon)
    )
    rotated_back = jnp.einsum("kij,kje->kie", left_basis, direction, precision=highest)
    rotated_back = jnp.einsum("kie,kce->ikc", rotated_back, right_basis, precision=highest)
    new_weights = weights - soap_rate * (rotated_back + soap_decay * weights)
    bias_first_new = vector_first * bias_first + (1.0 - vector_first) * bias_grad
    bias_second_new = vector_second * bias_second + (1.0 - vector_second) * bias_grad * bias_grad
    new_biases = biases - vector_rate * (bias_first_new / (1.0 - vector_first**STEP)) / (
        jnp.sqrt(bias_second_new / (1.0 - vector_second**STEP)) + vector_epsilon
    )
    back = lambda v: jnp.transpose(v, (1, 0, 2))
    return (
        block_out,
        input_grad,
        back(reduced),
        back(first_new),
        back(second_new),
        new_weights,
        new_weights.astype(BF),
        bias_first_new,
        bias_second_new,
        new_biases,
    )


def solution(mesh):
    n_dp = mesh.shape["dp"]
    fine = Mesh(mesh.devices.reshape(n_dp // 2, 2, 2, 2), ("z", "x", "y", "c"))
    dp, mp = ("z", "x"), ("y", "c")
    return jax.shard_map(
        functools.partial(body, n_dp == 8),
        mesh=fine,
        in_specs=(
            P(dp, mp),
            P(dp, mp),
            P(dp),
            P(dp),
            P(),
            P(dp, None, mp),
            P(dp, None, mp),
            P(dp, None, mp),
            P(),
            P(None, dp, None),
            P(None, mp, None),
            P(None, mp),
            P(None, mp),
            P(None, mp),
        ),
        out_specs=(
            P(dp, mp),
            P(dp, mp),
            P(dp, None, mp),
            P(dp, None, mp),
            P(dp, None, mp),
            P(dp, None, mp),
            P(dp, None, mp),
            P(None, mp),
            P(None, mp),
            P(None, mp),
        ),
        check_vma=False,
    )
```

```python
import functools
import math

import jax
import jax.numpy as jnp
from jax import lax
from jax.experimental import pallas as pl
from jax.experimental.pallas import tpu as pltpu
from jax.sharding import Mesh
from jax.sharding import PartitionSpec as P

D = 1024
HEAD_DIM = 64
LEN = 1024
GROUPS = 8
STEP = 10
CW = 256
TB = 256
NT = LEN // TB
BF = jnp.bfloat16
F32 = jnp.float32
LOG2E = math.log2(math.e)
LN2 = math.log(2.0)

norm_epsilon = 1e-06
soap_first = 0.95
soap_second = 0.95
soap_epsilon = 1e-08
soap_rate = 0.05
soap_decay = 0.01
vector_first = 0.9
vector_second = 0.999
vector_epsilon = 1e-08
vector_rate = 0.1
masked_score = -1e30
VMEM_LIMIT = 60 * 1024 * 1024

SWAP = [(0, 1), (1, 0)]


def params(n=1):
    return pltpu.CompilerParams(
        dimension_semantics=("arbitrary",) * n, vmem_limit_bytes=VMEM_LIMIT
    )


def nt_dot(a, b):
    return lax.dot_general(a, b, (((1,), (1,)), ((), ())), preferred_element_type=F32)


def nn_dot(a, b):
    return lax.dot_general(a, b, (((1,), (0,)), ((), ())), preferred_element_type=F32)


def whole(shape):
    return pl.BlockSpec(shape, lambda *_: (0,) * len(shape))


def rows_spec(width):
    return pl.BlockSpec((TB, width), lambda i, *_: (i, 0))


ANY = pl.BlockSpec(memory_space=pl.ANY)


def cost(flops, nbytes, trans=0):
    return pl.CostEstimate(flops=int(flops), bytes_accessed=int(nbytes), transcendentals=int(trans))


def fetch_weights(rowcol, sources, dest, sem, start):
    for at, (mat, arrays, index) in enumerate(sources):
        n_dp, _, rows, _ = arrays[0].shape
        for side in range(2):

            def step(slot, carry, at=at, mat=mat, index=index, side=side, array=arrays[side], n_dp=n_dp, rows=rows):
                code = rowcol[mat, side * n_dp + slot]
                first = pl.multiple_of((code // 2) * rows, rows)
                copy = pltpu.make_async_copy(
                    array.at[slot, index], dest.at[at, code % 2, pl.ds(first, rows), :], sem
                )
                if start:
                    copy.start()
                else:
                    copy.wait()
                return carry

            lax.fori_loop(0, n_dp, step, 0, unroll=n_dp <= 8)


def store_grads(slottab, mat, col, staged, targets, index, sem, start):
    n_dp, _, rows, _ = targets[0].shape

    def step(block, carry):
        source = staged.at[pl.ds(pl.multiple_of(block * rows, rows), rows), :]
        if not start:
            pltpu.make_async_copy(source, targets[0].at[0, index], sem).wait()
            return carry
        code = slottab[mat, block * 2 + col]

        @pl.when(code < n_dp)
        def _():
            pltpu.make_async_copy(source, targets[0].at[code, index], sem).start()

        @pl.when(code >= n_dp)
        def _():
            pltpu.make_async_copy(source, targets[1].at[code - n_dp, index], sem).start()

        return carry

    lax.fori_loop(0, n_dp, step, 0, unroll=n_dp <= 8)


def layer_norm(x):
    mean = jnp.mean(x, axis=1, keepdims=True)
    centre = x - mean
    var = jnp.mean(centre * centre, axis=1, keepdims=True)
    inv = lax.rsqrt(var + norm_epsilon)
    return centre * inv, inv


def prep_kernel(w_ref, cond_ref, wp_ref, mod_ref):
    for k in range(8):
        wp_ref[k] = w_ref[k].astype(BF)
    for c in range(6):
        mod_ref[c] = nn_dot(cond_ref[c], w_ref[8 + c].astype(BF))


def prep(weights, condk):
    rows = weights.shape[1]
    return pl.pallas_call(
        prep_kernel,
        out_shape=(
            jax.ShapeDtypeStruct((8, rows, CW), BF),
            jax.ShapeDtypeStruct((6, GROUPS, CW), F32),
        ),
        grid=(1,),
        in_specs=[whole(weights.shape), whole(condk.shape)],
        out_specs=(whole((8, rows, CW)), whole((6, GROUPS, CW))),
        compiler_params=params(),
        cost_estimate=cost(2e6, weights.size * 6),
        name="prep",
    )(weights, condk)


def rope(x, ct, s1, s2, sign):
    width = x.shape[1]
    up = pltpu.roll(x, 1, 1)
    down = pltpu.roll(x, width - 1, 1)
    reps = width // 128
    ct = jnp.concatenate([ct] * reps, axis=1) if reps > 1 else ct
    s1 = jnp.concatenate([s1] * reps, axis=1) if reps > 1 else s1
    s2 = jnp.concatenate([s2] * reps, axis=1) if reps > 1 else s2
    turn = up * s1 + down * s2
    return x * ct + turn if sign > 0 else x * ct - turn


def qkv_sources(a0, a1, b0, b1):
    return ((0, (a0, a1), 0), (1, (a0, a1), 1), (2, (b0, b1), 0))


def qkv_kernel(
    meta, rowtab, x_ref, vec_ref, ct_ref, s1_ref, s2_ref, a0, a1, b0, b1, h1_ref, q_ref, k_ref, v_ref, wsc, sem
):
    @pl.when(pl.program_id(0) == 0)
    def _():
        fetch_weights(rowtab, qkv_sources(a0, a1, b0, b1), wsc, sem, True)

    n1, _ = layer_norm(x_ref[...].astype(F32))
    h1 = (n1 * (1.0 + vec_ref[8:9, :]) + vec_ref[7:8, :]).astype(BF)
    h1_ref[...] = h1

    @pl.when(pl.program_id(0) == 0)
    def _():
        fetch_weights(rowtab, qkv_sources(a0, a1, b0, b1), wsc, sem, False)

    c = meta[1]
    ct, s1, s2 = ct_ref[...], s1_ref[...], s2_ref[...]
    for col in range(2):
        off = pl.multiple_of((col * 2 + c) * CW, CW)
        for k, out in ((0, q_ref), (1, k_ref), (2, v_ref)):
            acc = nn_dot(h1, wsc[k, col]) + vec_ref[k : k + 1, pl.ds(off, CW)]
            if k < 2:
                acc = rope(acc, ct, s1, s2, 1.0)
            if k == 0:
                acc = acc * (LOG2E * HEAD_DIM**-0.5)
            out[:, col * CW : (col + 1) * CW] = acc.astype(BF)


def qkv(meta, rowtab, x, vec, tables, w_attn):
    half = 2 * CW
    return pl.pallas_call(
        qkv_kernel,
        out_shape=(jax.ShapeDtypeStruct((LEN, D), BF),) + (jax.ShapeDtypeStruct((LEN, half), BF),) * 3,
        grid_spec=pltpu.PrefetchScalarGridSpec(
            num_scalar_prefetch=2,
            grid=(NT,),
            in_specs=[rows_spec(D), whole(vec.shape)] + [rows_spec(128)] * 3 + [ANY] * 4,
            out_specs=(rows_spec(D),) + (rows_spec(half),) * 3,
            scratch_shapes=[pltpu.VMEM((3, 2, D, CW), BF), pltpu.SemaphoreType.DMA(())],
        ),
        compiler_params=params(),
        cost_estimate=cost(2 * LEN * D * 3 * half, 12e6),
        name="qkv",
    )(meta, rowtab, x, vec, *tables, *w_attn)


def lane_iota(rows):
    return lax.broadcasted_iota(jnp.int32, (rows, 128), 1)


def split3(v):
    hi = v.astype(BF).astype(F32)
    mid = (v - hi).astype(BF).astype(F32)
    return hi, mid, v - hi - mid


def attend_kernel(meta, rowtab, q_ref, k_ref, v_ref, kaug_ref, wa, wb, o_ref, qaug_ref, pa_ref, wsc, osc, sem):
    @pl.when(pl.program_id(0) == 0)
    def _():
        fetch_weights(rowtab, ((3, (wa, wb), 1),), wsc, sem, True)

    lane = lane_iota(TB)
    first = lane < HEAD_DIM
    mask_one = jnp.where(lane == 3, 1.0, 0.0).astype(BF)
    ones = jnp.ones((LEN, 128), BF)
    kaug = kaug_ref[...]

    def pair(p, carry):
        off = pl.multiple_of(p * 128, 128)
        q2 = q_ref[:, pl.ds(off, 128)]
        kcat = jnp.concatenate([k_ref[:, pl.ds(off, 128)], kaug], axis=1)
        vcat = jnp.concatenate([v_ref[:, pl.ds(off, 128)], ones], axis=1)
        outs = []
        for head in range(2):
            mine = first if head == 0 else jnp.logical_not(first)
            qm = jnp.where(mine, q2.astype(F32), 0.0).astype(BF)
            s = nt_dot(jnp.concatenate([qm, mask_one], axis=1), kcat)
            top = jnp.max(s, axis=1, keepdims=True)
            probs = jnp.exp2(s - top).astype(BF)
            acc = nn_dot(probs, vcat)
            total = acc[:, 128:256]
            outs.append(acc[:, :128] / total)
            lse = jnp.broadcast_to(top, (TB, 128)) + jnp.log(total) * LOG2E
            hi, mid, lo = split3(-lse)
            aug = jnp.where(lane == 0, hi, jnp.where(lane == 1, mid, jnp.where(lane == 2, lo, jnp.where(lane == 3, 1.0, 0.0))))
            qaug_ref[2 * p + head] = aug.astype(BF)
        osc[:, pl.ds(off, 128)] = jnp.where(first, outs[0], outs[1]).astype(BF)
        return carry

    lax.fori_loop(0, 4, pair, 0)
    o_ref[...] = osc[...]

    @pl.when(pl.program_id(0) == 0)
    def _():
        fetch_weights(rowtab, ((3, (wa, wb), 1),), wsc, sem, False)

    pa = nt_dot(osc[:, :CW], wsc[0, 0]) + nt_dot(osc[:, CW:], wsc[0, 1])
    pa_ref[...] = pa.astype(BF)


def attend(meta, rowtab, q, k, v, kaug, wa, wb):
    half = 2 * CW
    return pl.pallas_call(
        attend_kernel,
        out_shape=(
            jax.ShapeDtypeStruct((LEN, half), BF),
            jax.ShapeDtypeStruct((8, LEN, 128), BF),
            jax.ShapeDtypeStruct((LEN, D), BF),
        ),
        grid_spec=pltpu.PrefetchScalarGridSpec(
            num_scalar_prefetch=2,
            grid=(NT,),
            in_specs=[rows_spec(half), whole((LEN, half)), whole((LEN, half)), whole((LEN, 128)), ANY, ANY],
            out_specs=(rows_spec(half), pl.BlockSpec((8, TB, 128), lambda i, *_: (0, i, 0)), rows_spec(D)),
            scratch_shapes=[
                pltpu.VMEM((1, 2, D, CW), BF),
                pltpu.VMEM((TB, half), BF),
                pltpu.SemaphoreType.DMA(()),
            ],
        ),
        compiler_params=params(),
        cost_estimate=cost(12e9, 10e6, 8e6),
        name="attend",
    )(meta, rowtab, q, k, v, kaug, wa, wb)


def middle_rows(x, pa, pb, vec, valid):
    a = (pa.astype(F32) + pb.astype(F32) + vec[3:4, :]) * valid
    return a, x.astype(F32) + vec[9:10, :] * a


def valid_rows(start, rows, length):
    return (start + lax.broadcasted_iota(jnp.int32, (rows, 1), 0) < length).astype(F32)


def gelu_parts(v):
    c0 = math.sqrt(2.0 / math.pi)
    sq = v * v
    t = jnp.tanh(v * (c0 + (c0 * 0.044715) * sq))
    half = 0.5 * (1.0 + t)
    slope = half + (0.5 * v) * (1.0 - t * t) * (c0 + (3.0 * c0 * 0.044715) * sq)
    return v * half, slope


def feed_kernel(
    meta, rowtab, slottab, x_ref, pa_ref, pb_ref, g_ref, vec_ref, c0, c1, d0, d1,
    pfk_ref, pfs_ref, pg_ref, gb_ref, gck_ref, gcs_ref, gdk_ref, gds_ref,
    wsc, h2, gf, h2t, gft, facc, gacc, zsc, ghsc, stage, sem, gsem,
):
    c, length = meta[1], meta[2]
    step = pl.program_id(0)
    half = step % 2
    col = step // 2
    sources = ((4, (c0, c1), 0), (5, (c0, c1), 1), (6, (d0, d1), 0), (7, (d0, d1), 1))

    @pl.when(step == 0)
    def _():
        fetch_weights(rowtab, sources, wsc, sem, True)
        gb_ref[...] = jnp.zeros_like(gb_ref)

        def rows(i, carry):
            at = pl.ds(pl.multiple_of(i * TB, TB), TB)
            _, x1 = middle_rows(x_ref[at, :], pa_ref[at, :], pb_ref[at, :], vec_ref, valid_rows(i * TB, TB, length))
            n2, _ = layer_norm(x1)
            hh = (n2 * (1.0 + vec_ref[11:12, :]) + vec_ref[10:11, :]).astype(BF)
            gg = (vec_ref[12:13, :] * g_ref[at, :].astype(F32)).astype(BF)
            h2[at, :] = hh
            gf[at, :] = gg
            h2t[:, at] = hh.T
            gft[:, at] = gg.T
            gb_ref[2:3, :] += jnp.sum(gg.astype(F32), axis=0, keepdims=True)
            return carry

        lax.fori_loop(0, NT, rows, 0)
        fetch_weights(rowtab, sources, wsc, sem, False)

    off = pl.multiple_of((col * 2 + c) * CW, CW)
    w_in = wsc.at[half, col]
    w_out = wsc.at[2 + half, col]
    bias = vec_ref[pl.ds(4 + half, 1), pl.ds(off, CW)]

    def rows(i, total):
        at = pl.ds(pl.multiple_of(i * TB, TB), TB)
        z, slope = gelu_parts(nn_dot(h2[at, :], w_in[...]) + bias)
        zb = z.astype(BF)
        gh = nn_dot(gf[at, :], w_out[...]) * slope
        ghb = gh.astype(BF)
        zsc[at, :] = zb
        ghsc[at, :] = ghb
        fpart = nt_dot(zb, w_out[...])
        gpart = nt_dot(ghb, w_in[...])

        @pl.when(step == 0)
        def _():
            facc[at, :] = fpart
            gacc[at, :] = gpart

        @pl.when(step > 0)
        def _():
            facc[at, :] += fpart
            gacc[at, :] += gpart

        return total + jnp.sum(ghb.astype(F32), axis=0, keepdims=True)

    total = lax.fori_loop(0, NT, rows, jnp.zeros((1, CW), F32))
    gb_ref[pl.ds(half, 1), pl.ds(off, CW)] = total

    targets = ((gck_ref, gcs_ref), (gdk_ref, gds_ref))

    @pl.when(step > 0)
    def _():
        for which in range(2):
            store_grads(slottab, 4, 0, stage.at[which], targets[0], 0, gsem, False)

    for which, (lhs, rhs) in enumerate(((h2t, ghsc), (gft, zsc))):
        for r in range(NT):
            stage[which, r * TB : (r + 1) * TB, :] = nn_dot(lhs[r * TB : (r + 1) * TB, :], rhs[...]).astype(BF)
        store_grads(slottab, 4 + 2 * which + half, col, stage.at[which], targets[which], half, gsem, True)

    @pl.when(step == 3)
    def _():
        for which in range(2):
            store_grads(slottab, 4, 0, stage.at[which], targets[0], 0, gsem, False)
        for block in range(2):
            mine = pl.ds(pl.multiple_of((block * 2 + c) * CW, CW), CW)
            theirs = pl.ds(pl.multiple_of((block * 2 + 1 - c) * CW, CW), CW)
            pfk_ref[:, block * CW : (block + 1) * CW] = facc[:, mine].astype(BF)
            pfs_ref[:, block * CW : (block + 1) * CW] = facc[:, theirs].astype(BF)
        pg_ref[...] = gacc[...].astype(BF)


def feed(meta, rowtab, slottab, x, pa, pb, g, vec, w_feed):
    grads = jax.ShapeDtypeStruct(w_feed[0].shape, BF)
    part = jax.ShapeDtypeStruct((LEN, 2 * CW), BF)
    return pl.pallas_call(
        feed_kernel,
        out_shape=(part, part, jax.ShapeDtypeStruct((LEN, D), BF), jax.ShapeDtypeStruct((8, D), F32)) + (grads,) * 4,
        grid_spec=pltpu.PrefetchScalarGridSpec(
            num_scalar_prefetch=3,
            grid=(4,),
            in_specs=[whole((LEN, D))] * 4 + [whole(vec.shape)] + [ANY] * 4,
            out_specs=(whole((LEN, 2 * CW)), whole((LEN, 2 * CW)), whole((LEN, D)), whole((8, D))) + (ANY,) * 4,
            scratch_shapes=[
                pltpu.VMEM((4, 2, D, CW), BF),
                pltpu.VMEM((LEN, D), BF),
                pltpu.VMEM((LEN, D), BF),
                pltpu.VMEM((D, LEN), BF),
                pltpu.VMEM((D, LEN), BF),
                pltpu.VMEM((LEN, D), F32),
                pltpu.VMEM((LEN, D), F32),
                pltpu.VMEM((LEN, CW), BF),
                pltpu.VMEM((LEN, CW), BF),
                pltpu.VMEM((2, D, CW), BF),
                pltpu.SemaphoreType.DMA(()),
                pltpu.SemaphoreType.DMA(()),
            ],
        ),
        compiler_params=params(),
        cost_estimate=cost(2 * LEN * D * D * 6, 24e6, 1e6),
        name="feed",
    )(meta, rowtab, slottab, x, pa, pb, g, vec, *w_feed)


def proj_back_kernel(
    meta, rowtab, slottab, x_ref, pa_ref, pb_ref, g_ref, ga_ref, gb_ref, o_ref, vec_ref, wa, wb,
    gx_ref, go_ref, sums_ref, keep_ref, send_ref, wsc, wacc, stage, sem, gsem,
):
    length = meta[2]
    step = pl.program_id(0)

    @pl.when(step == 0)
    def _():
        fetch_weights(rowtab, ((3, (wa, wb), 1),), wsc, sem, True)
        sums_ref[...] = jnp.zeros_like(sums_ref)

    a, x1 = middle_rows(x_ref[...], pa_ref[...], pb_ref[...], vec_ref, valid_rows(step * TB, TB, length))
    n2, inv = layer_norm(x1)
    gh2 = ga_ref[...].astype(F32) + gb_ref[...].astype(F32)
    gn = gh2 * (1.0 + vec_ref[11:12, :])
    m0 = jnp.mean(gn, axis=1, keepdims=True)
    m1 = jnp.mean(gn * n2, axis=1, keepdims=True)
    gx = g_ref[...].astype(F32) + (gn - m0 - n2 * m1) * inv
    gx_ref[...] = gx
    gatt = (vec_ref[9:10, :] * gx * valid_rows(step * TB, TB, length)).astype(BF)
    sums_ref[0:1, :] += jnp.sum(gx * a, axis=0, keepdims=True)
    sums_ref[1:2, :] += jnp.sum(gh2, axis=0, keepdims=True)
    sums_ref[2:3, :] += jnp.sum(gh2 * n2, axis=0, keepdims=True)
    sums_ref[3:4, :] += jnp.sum(gatt.astype(F32), axis=0, keepdims=True)

    @pl.when(step == 0)
    def _():
        fetch_weights(rowtab, ((3, (wa, wb), 1),), wsc, sem, False)

    go_ref[:, :CW] = nn_dot(gatt, wsc[0, 0]).astype(BF)
    go_ref[:, CW:] = nn_dot(gatt, wsc[0, 1]).astype(BF)
    part = nn_dot(gatt.T, o_ref[...])

    @pl.when(step == 0)
    def _():
        wacc[...] = part

    @pl.when(step > 0)
    def _():
        wacc[...] += part

    @pl.when(step == NT - 1)
    def _():
        for col in range(2):
            stage[col] = wacc[:, col * CW : (col + 1) * CW].astype(BF)
            store_grads(slottab, 3, col, stage.at[col], (keep_ref, send_ref), 0, gsem, True)
        for col in range(2):
            store_grads(slottab, 3, col, stage.at[col], (keep_ref, send_ref), 0, gsem, False)


def proj_back(meta, rowtab, slottab, x, pa, pb, g, ga, gb, o, vec, wa, wb):
    grads = jax.ShapeDtypeStruct(wa.shape[:1] + (1,) + wa.shape[2:], BF)
    half = 2 * CW
    return pl.pallas_call(
        proj_back_kernel,
        out_shape=(
            jax.ShapeDtypeStruct((LEN, D), F32),
            jax.ShapeDtypeStruct((LEN, half), BF),
            jax.ShapeDtypeStruct((8, D), F32),
            grads,
            grads,
        ),
        grid_spec=pltpu.PrefetchScalarGridSpec(
            num_scalar_prefetch=3,
            grid=(NT,),
            in_specs=[rows_spec(D)] * 6 + [rows_spec(half), whole(vec.shape), ANY, ANY],
            out_specs=(rows_spec(D), rows_spec(half), whole((8, D)), ANY, ANY),
            scratch_shapes=[
                pltpu.VMEM((1, 2, D, CW), BF),
                pltpu.VMEM((D, half), F32),
                pltpu.VMEM((2, D, CW), BF),
                pltpu.SemaphoreType.DMA(()),
                pltpu.SemaphoreType.DMA(()),
            ],
        ),
        compiler_params=params(),
        cost_estimate=cost(2 * LEN * D * half * 2, 20e6),
        name="proj_back",
    )(meta, rowtab, slottab, x, pa, pb, g, ga, gb, o, vec, wa, wb)


def attend_back_kernel(
    q_ref, k_ref, v_ref, go_ref, o_ref, qaug_ref, kaug_ref, ct_ref, s1_ref, s2_ref,
    gq_ref, gk_ref, gv_ref, gb_ref, qcat, gocat, kt, gqt,
):
    lane = lane_iota(LEN)
    first = lane < HEAD_DIM
    lane_kb = lane_iota(TB)
    first_kb = lane_kb < HEAD_DIM
    vaug = jnp.where(lane_kb < 3, 1.0, 0.0).astype(BF)
    go2 = go_ref[...].astype(F32)
    q2 = q_ref[...].astype(F32)
    dots = go2 * o_ref[...].astype(F32)
    for head in range(2):
        mine = first if head == 0 else jnp.logical_not(first)
        qcat[head, :, :128] = jnp.where(mine, q2, 0.0).astype(BF)
        qcat[head, :, 128:] = qaug_ref[head]
        gocat[head, :, :128] = jnp.where(mine, go2, 0.0).astype(BF)
        inner = jnp.sum(jnp.where(mine, dots, 0.0), axis=1, keepdims=True)
        hi, mid, lo = split3(-jnp.broadcast_to(inner, (LEN, 128)))
        aug = jnp.where(lane == 0, hi, jnp.where(lane == 1, mid, jnp.where(lane == 2, lo, 0.0)))
        gocat[head, :, 128:] = aug.astype(BF)
    kt[...] = k_ref[...].T
    gqt[...] = jnp.zeros_like(gqt)
    gb_ref[...] = jnp.zeros_like(gb_ref)

    for kb in range(NT):
        at = slice(kb * TB, (kb + 1) * TB)
        kcat = jnp.concatenate([k_ref[at, :], kaug_ref[at, :]], axis=1)
        vcat = jnp.concatenate([v_ref[at, :], vaug], axis=1)
        gvs, gks = [], []
        for head in range(2):
            pt = jnp.exp2(nt_dot(kcat, qcat[head]))
            gpt = nt_dot(vcat, gocat[head])
            gst = (pt * gpt).astype(BF)
            gvs.append(nn_dot(pt.astype(BF), go_ref[...]))
            gks.append(nn_dot(gst, q_ref[...]))
            rows = slice(head * HEAD_DIM, (head + 1) * HEAD_DIM)
            gqt[rows, :] += nn_dot(kt[rows, at], gst)
        gv = jnp.where(first_kb, gvs[0], gvs[1]).astype(BF)
        gk = jnp.where(first_kb, gks[0], gks[1]) * LN2
        gk = rope(gk, ct_ref[at, :], s1_ref[at, :], s2_ref[at, :], -1.0).astype(BF)
        gv_ref[at, :] = gv
        gk_ref[at, :] = gk
        gb_ref[1:2, :] += jnp.sum(gk.astype(F32), axis=0, keepdims=True)
        gb_ref[2:3, :] += jnp.sum(gv.astype(F32), axis=0, keepdims=True)
    gq = gqt[...].T * (HEAD_DIM**-0.5)
    gq = rope(gq, ct_ref[...], s1_ref[...], s2_ref[...], -1.0).astype(BF)
    gq_ref[...] = gq
    gb_ref[0:1, :] += jnp.sum(gq.astype(F32), axis=0, keepdims=True)


def attend_back(q, k, v, go, o, qaug, kaug, tables):
    half = 2 * CW
    pair = pl.BlockSpec((LEN, 128), lambda i: (0, i))
    return pl.pallas_call(
        attend_back_kernel,
        out_shape=(jax.ShapeDtypeStruct((LEN, half), BF),) * 3 + (jax.ShapeDtypeStruct((8, half), F32),),
        grid=(4,),
        in_specs=[pair] * 5
        + [pl.BlockSpec((2, LEN, 128), lambda i: (i, 0, 0))]
        + [whole((LEN, 128))] * 4,
        out_specs=(pair,) * 3 + (pl.BlockSpec((8, 128), lambda i: (0, i)),),
        scratch_shapes=[
            pltpu.VMEM((2, LEN, 256), BF),
            pltpu.VMEM((2, LEN, 256), BF),
            pltpu.VMEM((128, LEN), BF),
            pltpu.VMEM((128, LEN), F32),
        ],
        compiler_params=params(),
        cost_estimate=cost(30e9, 12e6, 8e6),
        name="attend_back",
    )(q, k, v, go, o, qaug, kaug, *tables)


def qkv_back_kernel(
    meta, rowtab, slottab, h1_ref, gq_ref, gk_ref, gv_ref, a0, a1, b0, b1,
    pg_ref, gak_ref, gas_ref, gbk_ref, gbs_ref, wsc, h1t, stage, sem, gsem,
):
    fetch_weights(rowtab, qkv_sources(a0, a1, b0, b1), wsc, sem, True)

    def turn(i, carry):
        at = pl.ds(pl.multiple_of(i * TB, TB), TB)
        h1t[:, at] = h1_ref[at, :].T
        return carry

    lax.fori_loop(0, NT, turn, 0)
    targets = ((gak_ref, gas_ref), (gak_ref, gas_ref), (gbk_ref, gbs_ref))
    sources = (gq_ref, gk_ref, gv_ref)
    for k in range(3):

        def rows(i, carry, k=k):
            at = pl.ds(pl.multiple_of(i * TB, TB), TB)
            part = nn_dot(h1t[at, :], sources[k][...]).astype(BF)
            stage[k, 0, at, :] = part[:, :CW]
            stage[k, 1, at, :] = part[:, CW:]
            return carry

        lax.fori_loop(0, NT, rows, 0)
        for col in range(2):
            store_grads(slottab, k, col, stage.at[k, col], targets[k], k % 2, gsem, True)
    fetch_weights(rowtab, qkv_sources(a0, a1, b0, b1), wsc, sem, False)

    def rows(i, carry):
        at = pl.ds(pl.multiple_of(i * TB, TB), TB)
        acc = jnp.zeros((TB, D), F32)
        for k in range(3):
            for col in range(2):
                acc += nt_dot(sources[k][at, col * CW : (col + 1) * CW], wsc[k, col])
        pg_ref[at, :] = acc.astype(BF)
        return carry

    lax.fori_loop(0, NT, rows, 0)
    for k in range(3):
        for col in range(2):
            store_grads(slottab, k, col, stage.at[k, col], targets[k], k % 2, gsem, False)


def qkv_back(meta, rowtab, slottab, h1, gq, gk, gv, w_attn):
    n_dp, _, rows, _ = w_attn[0].shape
    two = jax.ShapeDtypeStruct((n_dp, 2, rows, CW), BF)
    one = jax.ShapeDtypeStruct((n_dp, 1, rows, CW), BF)
    half = 2 * CW
    return pl.pallas_call(
        qkv_back_kernel,
        out_shape=(jax.ShapeDtypeStruct((LEN, D), BF), two, two, one, one),
        grid_spec=pltpu.PrefetchScalarGridSpec(
            num_scalar_prefetch=3,
            grid=(1,),
            in_specs=[whole((LEN, D))] + [whole((LEN, half))] * 3 + [ANY] * 4,
            out_specs=(whole((LEN, D)),) + (ANY,) * 4,
            scratch_shapes=[
                pltpu.VMEM((3, 2, D, CW), BF),
                pltpu.VMEM((D, LEN), BF),
                pltpu.VMEM((3, 2, D, CW), BF),
                pltpu.SemaphoreType.DMA(()),
                pltpu.SemaphoreType.DMA(()),
            ],
        ),
        compiler_params=params(),
        cost_estimate=cost(2 * LEN * D * half * 6, 16e6),
        name="qkv_back",
    )(meta, rowtab, slottab, h1, gq, gk, gv, *w_attn)


def emit_kernel(meta, x0, x1, pa0, pa1, pb0, pb1, g0, g1, fk_ref, fr_ref, vec_ref, outk_ref, outs_ref, sums_ref):
    y, c, length = meta[0], meta[1], meta[2]
    step = pl.program_id(0)

    @pl.when(step == 0)
    def _():
        sums_ref[...] = jnp.zeros_like(sums_ref)

    valid = valid_rows(step * TB, TB, length)
    outs = []
    for col, (x, pa, pb, g) in enumerate(((x0, pa0, pb0, g0), (x1, pa1, pb1, g1))):
        off = pl.ds(pl.multiple_of((col * 2 + c) * CW, CW), CW)
        here = slice(col * CW, (col + 1) * CW)
        a = (pa[...].astype(F32) + pb[...].astype(F32) + vec_ref[3:4, off]) * valid
        middle = x[...].astype(F32) + vec_ref[9:10, off] * a
        f = fk_ref[:, here].astype(F32) + fr_ref[:, here].astype(F32) + vec_ref[6:7, off]
        outs.append((middle + vec_ref[12:13, off] * f).astype(BF))
        sums_ref[0:1, here] += jnp.sum(g[...].astype(F32) * f, axis=0, keepdims=True)
    outk_ref[...] = jnp.where(y == 0, outs[0].astype(F32), outs[1].astype(F32)).astype(BF)
    outs_ref[...] = jnp.where(y == 0, outs[1].astype(F32), outs[0].astype(F32)).astype(BF)


def column_specs():
    return [pl.BlockSpec((TB, CW), lambda i, meta, col=col: (i, 2 * col + meta[1])) for col in range(2)]


def emit(meta, x, pa, pb, g, fk, fr, vec):
    return pl.pallas_call(
        emit_kernel,
        out_shape=(jax.ShapeDtypeStruct((LEN, CW), BF),) * 2 + (jax.ShapeDtypeStruct((8, 2 * CW), F32),),
        grid_spec=pltpu.PrefetchScalarGridSpec(
            num_scalar_prefetch=1,
            grid=(NT,),
            in_specs=column_specs() * 4 + [rows_spec(2 * CW)] * 2 + [whole(vec.shape)],
            out_specs=(rows_spec(CW),) * 2 + (whole((8, 2 * CW)),),
        ),
        compiler_params=params(),
        cost_estimate=cost(1e7, 8e6),
        name="emit",
    )(meta, x, x, pa, pa, pb, pb, g, g, fk, fr, vec)


def final_kernel(meta, x_ref, ga_ref, gb_ref, gx0, gx1, vec_ref, gink_ref, gins_ref, sums_ref, isc):
    y, c = meta[0], meta[1]
    step = pl.program_id(0)

    @pl.when(step == 0)
    def _():
        sums_ref[...] = jnp.zeros_like(sums_ref)

    n1, inv = layer_norm(x_ref[...].astype(F32))
    gh1 = ga_ref[...].astype(F32) + gb_ref[...].astype(F32)
    gn = gh1 * (1.0 + vec_ref[8:9, :])
    m0 = jnp.mean(gn, axis=1, keepdims=True)
    m1 = jnp.mean(gn * n1, axis=1, keepdims=True)
    isc[...] = (gn - m0 - n1 * m1) * inv
    sums_ref[0:1, :] += jnp.sum(gh1, axis=0, keepdims=True)
    sums_ref[1:2, :] += jnp.sum(gh1 * n1, axis=0, keepdims=True)
    grads = [gx[...] + isc[:, pl.ds(pl.multiple_of((col * 2 + c) * CW, CW), CW)] for col, gx in ((0, gx0), (1, gx1))]
    gink_ref[...] = jnp.where(y == 0, grads[0], grads[1])
    gins_ref[...] = jnp.where(y == 0, grads[1], grads[0]).astype(BF)


def final(meta, x, ga, gb, gx, vec):
    return pl.pallas_call(
        final_kernel,
        out_shape=(
            jax.ShapeDtypeStruct((LEN, CW), F32),
            jax.ShapeDtypeStruct((LEN, CW), BF),
            jax.ShapeDtypeStruct((8, D), F32),
        ),
        grid_spec=pltpu.PrefetchScalarGridSpec(
            num_scalar_prefetch=1,
            grid=(NT,),
            in_specs=[rows_spec(D)] * 3 + column_specs() + [whole(vec.shape)],
            out_specs=(rows_spec(CW),) * 2 + (whole((8, D)),),
            scratch_shapes=[pltpu.VMEM((TB, D), F32)],
        ),
        compiler_params=params(),
        cost_estimate=cost(1e8, 12e6),
        name="final",
    )(meta, x, ga, gb, gx, gx, vec)


def turn(a, b, contract):
    return lax.dot_general(
        a.astype(BF), b.astype(BF), ((contract[:1], contract[1:]), ((), ())), preferred_element_type=F32
    )


def soap_kernel(parts, chained, *refs):
    grads_in, (w, m1, m2, lb, rb), outs = refs[:parts], refs[parts : parts + 5], refs[parts + 5 + chained :]
    grad = grads_in[0][0].astype(F32)
    for extra in grads_in[1:]:
        grad = grad + extra[0].astype(F32)
    left, right = lb[0], rb[0]
    turned = turn(turn(left, grad, (0, 0)), right, (1, 0))
    first = soap_first * m1[0] + (1.0 - soap_first) * turned
    second = soap_second * m2[0] + (1.0 - soap_second) * turned * turned
    direction = first * (1.0 / (1.0 - soap_first**STEP)) / (
        jnp.sqrt(second * (1.0 / (1.0 - soap_second**STEP))) + soap_epsilon
    )
    back = turn(turn(left, direction, (1, 0)), right, (1, 1))
    new = w[0] - soap_rate * (back + soap_decay * w[0])
    outs[0][0] = grad
    outs[1][0] = first
    outs[2][0] = second
    outs[3][0] = new
    outs[4][0] = new.astype(BF)


def soap(base, grads, state, chain):
    count, rows, _ = grads[0].shape
    total = state[0].shape[0]
    parts = len(grads)
    own = pl.BlockSpec((1, rows, CW), lambda i: (i, 0, 0))
    place = pl.BlockSpec((1, rows, CW), lambda i: (base + i, 0, 0))
    shape = jax.ShapeDtypeStruct((total, rows, CW), F32)
    return pl.pallas_call(
        functools.partial(soap_kernel, parts, len(chain)),
        out_shape=(shape,) * 4 + (jax.ShapeDtypeStruct((total, rows, CW), BF),),
        grid=(count,),
        in_specs=[own] * parts
        + [place] * 3
        + [
            pl.BlockSpec((1, rows, rows), lambda i: (base + i, 0, 0)),
            pl.BlockSpec((1, CW, CW), lambda i: (base + i, 0, 0)),
        ]
        + [ANY] * len(chain),
        out_specs=(place,) * 5,
        input_output_aliases={parts + 5 + i: i for i in range(len(chain))},
        compiler_params=params(),
        cost_estimate=cost(count * rows * CW * (rows + CW) * 24, count * rows * CW * 34),
        name="soap",
    )(*grads, *state, *chain)


def xor_pairs(size, step):
    return [(i, i ^ step) for i in range(size)]


def swap(v, axis):
    return lax.ppermute(v, axis, SWAP)


def after(value, *deps):
    return lax.optimization_barrier((value,) + deps)[0]


def true_blocks(own, got, y, c):
    blocks = jnp.stack([own, got], axis=1)
    blocks = jnp.where(c == 1, blocks[:, ::-1], blocks)
    return jnp.where(y == 1, blocks[::-1], blocks)


def side_by_side(blocks):
    return jnp.concatenate([blocks[0, 0], blocks[0, 1], blocks[1, 0], blocks[1, 1]], axis=-1)


def rotary_tables():
    half_dim = HEAD_DIM // 2
    places = jnp.arange(LEN, dtype=F32)
    frequencies = 10000.0 ** (-(jnp.arange(half_dim, dtype=F32) * 2.0 / HEAD_DIM))
    angles = places[:, None] * frequencies[None, :]
    pairs = jnp.tile(jnp.repeat(angles, 2, axis=1), (1, 2))
    odd = (jnp.arange(128) % 2 == 1)[None, :]
    cos, sin = jnp.cos(pairs), jnp.sin(pairs)
    return cos, jnp.where(odd, sin, 0.0), jnp.where(odd, 0.0, -sin)


LAST = ("x", "x", "y", "y", "x", "x", "y", "y")


def body(fast, block_in, out_grad, lengths, group_ids, time_embed, weights, first_moments, second_moments,
         owners, left_basis, right_basis, biases, bias_first, bias_second):
    highest = lax.Precision.HIGHEST
    n_dp = owners.shape[1]
    z, x, y, c = (lax.axis_index(name) for name in ("z", "x", "y", "c"))
    dp = z * 2 + x
    by_matrix = lambda v: jnp.transpose(v, (1, 0, 2))
    weights, first_moments, second_moments = map(by_matrix, (weights, first_moments, second_moments))
    rows = weights.shape[1]

    columns = jnp.arange(2, dtype=jnp.int32)[None, None, :]
    holder = owners[:, :, None]
    yr = jnp.bitwise_xor(columns, y)
    if fast:
        zr = jnp.bitwise_xor(holder // 2, z)
        xr = jnp.bitwise_xor(holder % 2, x)
        x_last = jnp.array([name == "x" for name in LAST] + [False] * 6)[:, None, None]
        slottab = jnp.where(x_last, xr * 8 + yr * 4, yr * 8 + xr * 4) + zr
    else:
        slottab = yr * n_dp + holder
    slottab = slottab.reshape(owners.shape[0], 2 * n_dp).astype(jnp.int32)
    codes = jnp.arange(2 * n_dp, dtype=jnp.int32)
    rowtab = jnp.sum(
        jnp.where(slottab[:, :, None] == codes[None, None, :], codes[None, :, None], 0), axis=1
    ).astype(jnp.int32)
    meta = jnp.stack([y, c, lengths[y]]).astype(jnp.int32)

    cond = jax.nn.silu(time_embed).astype(BF)
    own_rows = (owners[8:] == dp).astype(F32)
    condk = jnp.sum(
        own_rows[:, None, :, None] * cond.astype(F32).reshape(1, GROUPS, n_dp, rows), axis=2
    ).astype(BF)
    own_weights, mod_part = prep(weights, condk)

    def part(v, index):
        return lax.dynamic_slice_in_dim(v, index * LEN, LEN, 0)

    def z_stage(pieces):
        return [lax.ppermute(piece, "z", xor_pairs(4, s + 1)) for s, piece in enumerate(pieces)]

    def utterance_rows(index):
        hit = (jnp.arange(GROUPS) == group_ids[index]).astype(F32)
        mods = jnp.sum(mod_all * hit[None, :, None], axis=1) + biases[7:]
        return jnp.concatenate([biases[:7], mods, jnp.zeros((3, CW), F32)], axis=0)

    both_in = jnp.stack([block_in, out_grad])
    pair = lambda index: lax.dynamic_slice_in_dim(both_in, index * LEN, LEN, 1)
    rows_own = jnp.stack([pair(y), swap(pair(1 - y), "y")])
    if fast:
        piece = own_weights[None, :4]
        z_attn = [piece] + z_stage([piece] * 3)
        mod_all = mod_part + swap(mod_part, "x")
        for step in (1, 2):
            mod_all = mod_all + lax.ppermute(mod_all, "z", xor_pairs(4, step))
    else:
        mod_all = lax.psum(mod_part, ("z", "x"))
    vec_own = jnp.stack([utterance_rows(y), swap(utterance_rows(1 - y), "y")])
    vec_got = swap(vec_own, "c")
    if fast:
        four = jnp.concatenate(z_attn, axis=0)
        four, rows_own, vec_got = lax.optimization_barrier((four, rows_own, vec_got))
    rows_got = swap(rows_own, "c")
    if fast:
        a_got, b_got = swap(four[:, :2], "y"), swap(four[:, 2:], "x")
        piece = after(own_weights[None, 4:], four)
        z_feed = [piece] + z_stage([piece] * 3)
        a_got, b_got, rows_got = lax.optimization_barrier((a_got, b_got, rows_got))
        eight_a = jnp.concatenate([four[:, :2], a_got], axis=0)
        eight_b = jnp.concatenate([four[:, 2:], b_got], axis=0)
        w_attn = (eight_a, swap(eight_a, "x"), eight_b, swap(eight_b, "y"))
        z_feed, w_attn = lax.optimization_barrier((z_feed, w_attn))
        four = jnp.concatenate(z_feed, axis=0)
    else:
        gathered = [
            lax.all_gather(own_weights[None, 2 * i : 2 * i + 2], ("z", "x"), axis=0, tiled=True) for i in range(4)
        ]
        w_attn = (gathered[0], swap(gathered[0], "y"), gathered[1], swap(gathered[1], "y"))

    rows_both = true_blocks(rows_own, rows_got, y, c)
    xs = side_by_side(rows_both[:, :, 0])
    gs = side_by_side(rows_both[:, :, 1])
    vec = side_by_side(true_blocks(vec_own, vec_got, y, c))
    tables = rotary_tables()
    lane = jnp.arange(128)[None, :]
    padded = (jnp.arange(LEN, dtype=jnp.int32) >= meta[2])[:, None]
    kaug = jnp.where(lane < 3, 1.0, jnp.where((lane == 3) & padded, masked_score, 0.0)).astype(BF)

    if fast:
        c_got, d_got = swap(four[:, :2], "y"), swap(four[:, 2:], "x")
    h1, q, k, v = qkv(meta, rowtab, xs, vec, tables, w_attn)
    if fast:
        q, c_got, d_got = lax.optimization_barrier((q, c_got, d_got))
        eight_c = jnp.concatenate([four[:, :2], c_got], axis=0)
        eight_d = jnp.concatenate([four[:, 2:], d_got], axis=0)
        w_feed = (eight_c, swap(eight_c, "x"), eight_d, swap(eight_d, "y"))
    else:
        w_feed = (gathered[2], swap(gathered[2], "y"), gathered[3], swap(gathered[3], "y"))
    o, qaug, pa = attend(meta, rowtab, q, k, v, kaug, *w_attn[2:])
    pa, w_feed = lax.optimization_barrier((pa, w_feed))
    pb = swap(pa, "c")
    pfk, pfs, g2a, gb_feed, keep_c, send_c, keep_d, send_d = feed(
        meta, rowtab, slottab, xs, pa, pb, gs, vec, w_feed
    )
    g2b = swap(g2a, "c")

    def second_stage(keep, got, axis):
        total = keep.astype(F32) + got.astype(F32)
        if not fast:
            return lax.psum_scatter(total.astype(BF), ("z", "x"), scatter_dimension=0, tiled=True)[0], None
        return total[:4], swap(total[4:].astype(BF), axis)

    def third_stage(*states):
        if not fast:
            return [jnp.concatenate([state[0] for state in states], axis=0)]
        total = jnp.concatenate([keep + got.astype(F32) for keep, got in states], axis=1)
        low = total.astype(BF)
        return [total[0]] + z_stage([low[1], low[2], low[3]])

    first = lambda name: name if fast else "y"
    got_c, got_d = swap(send_c, first("x")), swap(send_d, "y")
    gx, go, sums_mid, keep_o, send_o = proj_back(
        meta, rowtab, slottab, xs, pa, pb, gs, g2a, g2b, o, vec, *w_attn[2:]
    )
    pfr = swap(after(pfs, g2b), "c")
    out_keep, out_send, sums_out = emit(meta, xs, pa, pb, gs, pfk, after(pfr, go), vec)
    go, got_c, got_d, out_send = lax.optimization_barrier((go, got_c, got_d, out_send))
    state_c = second_stage(keep_c, got_c, "y")
    state_d = second_stage(keep_d, got_d, "x")
    got_o = swap(send_o, "y")
    gq, gk, gv, gb_qkv = attend_back(q, k, v, go, o, qaug, kaug, tables)
    gq, state_c, state_d, got_o = lax.optimization_barrier((gq, state_c, state_d, got_o))
    grads_feed = third_stage(state_c, state_d)
    state_o = second_stage(keep_o, got_o, "x")
    out_got = swap(out_send, "y")
    g1a, keep_a, send_a, keep_v, send_v = qkv_back(meta, rowtab, slottab, h1, gq, gk, gv, w_attn)
    g1a, state_o, out_got, grads_feed = lax.optimization_barrier((g1a, state_o, out_got, grads_feed))
    g1b = swap(g1a, "c")
    got_a, got_v = swap(send_a, first("x")), swap(send_v, "y")
    gin_keep, gin_send, sums_end = final(meta, xs, g1a, g1b, gx, vec)
    gin_got = swap(gin_send, "y").astype(F32)

    def columns_of(v, col):
        return lax.dynamic_slice_in_dim(v, (col * 2 + c) * CW, CW, 1)

    tall = jnp.concatenate([sums_mid[3:4], gb_feed[:3], sums_end[:2], sums_mid[:3]], axis=0)
    hot = jnp.broadcast_to((jnp.arange(CW) == group_ids[y]).astype(F32)[None], (3, CW))
    local = jnp.stack(
        [
            jnp.concatenate(
                [
                    gb_qkv[:3, col * CW : (col + 1) * CW],
                    columns_of(tall, col),
                    sums_out[:1, col * CW : (col + 1) * CW],
                    hot,
                ],
                axis=0,
            )
            for col in range(2)
        ]
    )
    mine = jnp.where(y == 0, local[0], local[1])
    other = jnp.where(y == 0, local[1], local[0])
    vecs = jnp.stack([mine, swap(other, "y")])
    if fast:
        vecs = jnp.concatenate([vecs, swap(vecs, "x")], axis=0)
        for step in (1, 2):
            vecs = jnp.concatenate([vecs, lax.ppermute(vecs, "z", xor_pairs(4, step))], axis=0)
    else:
        vecs = lax.all_gather(vecs, ("z", "x"), axis=0, tiled=True)

    state = (weights, first_moments, second_moments, left_basis, right_basis)
    chain = soap(4, grads_feed, state, ())
    got_a, got_v, vecs, gin_got, chain = lax.optimization_barrier((got_a, got_v, vecs, gin_got, chain))
    state_a = second_stage(keep_a, got_a, "y")
    state_v = second_stage(keep_v, got_v, "x")
    bias_grad = jnp.sum(vecs[:, :13], axis=0)
    grouped = jnp.einsum("ug,ukc->kgc", vecs[:, 13, :GROUPS], vecs[:, 7:13], precision=highest)
    grads_mod = jnp.einsum("kgr,kgc->krc", condk.astype(F32), grouped, precision=highest)
    chain = soap(8, [grads_mod], state, chain)
    state_a, state_v, chain = lax.optimization_barrier((state_a, state_v, chain))
    grads_attn = third_stage(state_a, state_v, state_o)
    chain = soap(0, grads_attn, state, chain)

    def both(mine, other):
        return jnp.where(
            y == 0, jnp.concatenate([mine, other], axis=0), jnp.concatenate([other, mine], axis=0)
        )

    block_out = both(out_keep, out_got)
    input_grad = both(gin_keep, gin_got)
    bias_first_new = vector_first * bias_first + (1.0 - vector_first) * bias_grad
    bias_second_new = vector_second * bias_second + (1.0 - vector_second) * bias_grad * bias_grad
    new_biases = biases - vector_rate * (bias_first_new / (1.0 - vector_first**STEP)) / (
        jnp.sqrt(bias_second_new / (1.0 - vector_second**STEP)) + vector_epsilon
    )
    return (block_out, input_grad) + tuple(map(by_matrix, chain)) + (bias_first_new, bias_second_new, new_biases)


def solution(mesh):
    n_dp = mesh.shape["dp"]
    fine = Mesh(mesh.devices.reshape(n_dp // 2, 2, 2, 2), ("z", "x", "y", "c"))
    dp, mp = ("z", "x"), ("y", "c")
    return jax.shard_map(
        functools.partial(body, n_dp == 8),
        mesh=fine,
        in_specs=(
            P(dp, mp),
            P(dp, mp),
            P(dp),
            P(dp),
            P(),
            P(dp, None, mp),
            P(dp, None, mp),
            P(dp, None, mp),
            P(),
            P(None, dp, None),
            P(None, mp, None),
            P(None, mp),
            P(None, mp),
            P(None, mp),
        ),
        out_specs=(
            P(dp, mp),
            P(dp, mp),
            P(dp, None, mp),
            P(dp, None, mp),
            P(dp, None, mp),
            P(dp, None, mp),
            P(dp, None, mp),
            P(None, mp),
            P(None, mp),
            P(None, mp),
        ),
        check_vma=False,
    )
```

```python
import functools
import math

import jax
import jax.numpy as jnp
from jax import lax
from jax.experimental import pallas as pl
from jax.experimental.pallas import tpu as pltpu
from jax.sharding import Mesh
from jax.sharding import PartitionSpec as P

D = 1024
HEAD_DIM = 64
LEN = 1024
GROUPS = 8
STEP = 10
CW = 256
TB = 256
NT = LEN // TB
BF = jnp.bfloat16
F32 = jnp.float32
LOG2E = math.log2(math.e)
LN2 = math.log(2.0)

norm_epsilon = 1e-06
soap_first = 0.95
soap_second = 0.95
soap_epsilon = 1e-08
soap_rate = 0.05
soap_decay = 0.01
vector_first = 0.9
vector_second = 0.999
vector_epsilon = 1e-08
vector_rate = 0.1
masked_score = -1e30
VMEM_LIMIT = 60 * 1024 * 1024

SWAP = [(0, 1), (1, 0)]


def params(n=1):
    return pltpu.CompilerParams(
        dimension_semantics=("arbitrary",) * n, vmem_limit_bytes=VMEM_LIMIT
    )


def nt_dot(a, b):
    return lax.dot_general(a, b, (((1,), (1,)), ((), ())), preferred_element_type=F32)


def nn_dot(a, b):
    return lax.dot_general(a, b, (((1,), (0,)), ((), ())), preferred_element_type=F32)


def whole(shape):
    return pl.BlockSpec(shape, lambda *_: (0,) * len(shape))


def rows_spec(width):
    return pl.BlockSpec((TB, width), lambda i, *_: (i, 0))


ANY = pl.BlockSpec(memory_space=pl.ANY)


def cost(flops, nbytes, trans=0):
    return pl.CostEstimate(flops=int(flops), bytes_accessed=int(nbytes), transcendentals=int(trans))


def fetch_weights(rowcol, sources, dest, sem, start):
    for at, (mat, arrays, index) in enumerate(sources):
        n_dp, _, rows, _ = arrays[0].shape
        for side in range(2):

            def step(slot, carry, at=at, mat=mat, index=index, side=side, array=arrays[side], n_dp=n_dp, rows=rows):
                code = rowcol[mat, side * n_dp + slot]
                first = pl.multiple_of((code // 2) * rows, rows)
                copy = pltpu.make_async_copy(
                    array.at[slot, index], dest.at[at, code % 2, pl.ds(first, rows), :], sem
                )
                if start:
                    copy.start()
                else:
                    copy.wait()
                return carry

            lax.fori_loop(0, n_dp, step, 0, unroll=n_dp <= 8)


def store_grads(slottab, mat, col, staged, targets, index, sem, start, half=0):
    n_dp, _, rows, _ = targets[0].shape
    pitch = LEN // n_dp

    def step(block, carry):
        source = staged.at[pl.ds(pl.multiple_of(block * pitch + half * rows, rows), rows), :]
        if not start:
            pltpu.make_async_copy(source, targets[0].at[0, index], sem).wait()
            return carry
        code = slottab[mat, block * 2 + col]

        @pl.when(code < n_dp)
        def _():
            pltpu.make_async_copy(source, targets[0].at[code, index], sem).start()

        @pl.when(code >= n_dp)
        def _():
            pltpu.make_async_copy(source, targets[1].at[code - n_dp, index], sem).start()

        return carry

    lax.fori_loop(0, n_dp, step, 0, unroll=n_dp <= 8)


def layer_norm(x):
    mean = jnp.mean(x, axis=1, keepdims=True)
    centre = x - mean
    var = jnp.mean(centre * centre, axis=1, keepdims=True)
    inv = lax.rsqrt(var + norm_epsilon)
    return centre * inv, inv


def prep_kernel(w_ref, cond_ref, wp_ref, mod_ref):
    for k in range(8):
        wp_ref[k] = w_ref[k].astype(BF)
    for c in range(6):
        mod_ref[c] = nn_dot(cond_ref[c], w_ref[8 + c].astype(BF))


def prep(weights, condk):
    rows = weights.shape[1]
    return pl.pallas_call(
        prep_kernel,
        out_shape=(
            jax.ShapeDtypeStruct((8, rows, CW), BF),
            jax.ShapeDtypeStruct((6, GROUPS, CW), F32),
        ),
        grid=(1,),
        in_specs=[whole(weights.shape), whole(condk.shape)],
        out_specs=(whole((8, rows, CW)), whole((6, GROUPS, CW))),
        compiler_params=params(),
        cost_estimate=cost(2e6, weights.size * 6),
        name="prep",
    )(weights, condk)


def assemble_kernel(meta, own_ref, got_ref, x_ref, g_ref):
    y, c = meta[0], meta[1]
    for yr in range(2):
        for cr, ref in enumerate((own_ref, got_ref)):
            off = (jnp.bitwise_xor(y, yr) * 2 + jnp.bitwise_xor(c, cr)) * CW
            off = pl.ds(pl.multiple_of(off, CW), CW)
            x_ref[:, off] = ref[yr, 0]
            g_ref[:, off] = ref[yr, 1]


def assemble(meta, own, got):
    block = pl.BlockSpec((2, 2, TB, CW), lambda i, *_: (0, 0, i, 0))
    out = jax.ShapeDtypeStruct((LEN, D), BF)
    return pl.pallas_call(
        assemble_kernel,
        out_shape=(out, out),
        grid_spec=pltpu.PrefetchScalarGridSpec(
            num_scalar_prefetch=1,
            grid=(NT,),
            in_specs=[block, block],
            out_specs=(rows_spec(D), rows_spec(D)),
        ),
        compiler_params=params(),
        cost_estimate=cost(1e4, 8e6),
        name="assemble",
    )(meta, own, got)


def rope(x, ct, s1, s2, sign):
    width = x.shape[1]
    up = pltpu.roll(x, 1, 1)
    down = pltpu.roll(x, width - 1, 1)
    reps = width // 128
    ct = jnp.concatenate([ct] * reps, axis=1) if reps > 1 else ct
    s1 = jnp.concatenate([s1] * reps, axis=1) if reps > 1 else s1
    s2 = jnp.concatenate([s2] * reps, axis=1) if reps > 1 else s2
    turn = up * s1 + down * s2
    return x * ct + turn if sign > 0 else x * ct - turn


def qkv_sources(a0, a1, b0, b1):
    return ((0, (a0, a1), 0), (1, (a0, a1), 1), (2, (b0, b1), 0))


def qkv_kernel(
    meta, rowtab, x_ref, vec_ref, ct_ref, s1_ref, s2_ref, a0, a1, b0, b1, h1_ref, q_ref, k_ref, v_ref, wsc, sem
):
    @pl.when(pl.program_id(0) == 0)
    def _():
        fetch_weights(rowtab, qkv_sources(a0, a1, b0, b1), wsc, sem, True)

    n1, _ = layer_norm(x_ref[...].astype(F32))
    h1 = (n1 * (1.0 + vec_ref[8:9, :]) + vec_ref[7:8, :]).astype(BF)
    h1_ref[...] = h1

    @pl.when(pl.program_id(0) == 0)
    def _():
        fetch_weights(rowtab, qkv_sources(a0, a1, b0, b1), wsc, sem, False)

    c = meta[1]
    ct, s1, s2 = ct_ref[...], s1_ref[...], s2_ref[...]
    for col in range(2):
        off = pl.multiple_of((col * 2 + c) * CW, CW)
        for k, out in ((0, q_ref), (1, k_ref), (2, v_ref)):
            acc = nn_dot(h1, wsc[k, col]) + vec_ref[k : k + 1, pl.ds(off, CW)]
            if k < 2:
                acc = rope(acc, ct, s1, s2, 1.0)
            if k == 0:
                acc = acc * (LOG2E * HEAD_DIM**-0.5)
            out[:, col * CW : (col + 1) * CW] = acc.astype(BF)


def qkv(meta, rowtab, x, vec, tables, w_attn):
    half = 2 * CW
    return pl.pallas_call(
        qkv_kernel,
        out_shape=(jax.ShapeDtypeStruct((LEN, D), BF),) + (jax.ShapeDtypeStruct((LEN, half), BF),) * 3,
        grid_spec=pltpu.PrefetchScalarGridSpec(
            num_scalar_prefetch=2,
            grid=(NT,),
            in_specs=[rows_spec(D), whole(vec.shape)] + [rows_spec(128)] * 3 + [ANY] * 4,
            out_specs=(rows_spec(D),) + (rows_spec(half),) * 3,
            scratch_shapes=[pltpu.VMEM((3, 2, D, CW), BF), pltpu.SemaphoreType.DMA(())],
        ),
        compiler_params=params(),
        cost_estimate=cost(2 * LEN * D * 3 * half, 12e6),
        name="qkv",
    )(meta, rowtab, x, vec, *tables, *w_attn)


def lane_iota(rows):
    return lax.broadcasted_iota(jnp.int32, (rows, 128), 1)


def split3(v):
    hi = v.astype(BF).astype(F32)
    mid = (v - hi).astype(BF).astype(F32)
    return hi, mid, v - hi - mid


def attend_kernel(meta, rowtab, q_ref, k_ref, v_ref, kaug_ref, wa, wb, o_ref, qaug_ref, pa_ref, wsc, osc, sem):
    @pl.when(pl.program_id(0) == 0)
    def _():
        fetch_weights(rowtab, ((3, (wa, wb), 1),), wsc, sem, True)

    lane = lane_iota(TB)
    first = lane < HEAD_DIM
    mask_one = jnp.where(lane == 3, 1.0, 0.0).astype(BF)
    ones = jnp.ones((LEN, 128), BF)
    kaug = kaug_ref[...]

    def pair(p, carry):
        off = pl.multiple_of(p * 128, 128)
        q2 = q_ref[:, pl.ds(off, 128)]
        kcat = jnp.concatenate([k_ref[:, pl.ds(off, 128)], kaug], axis=1)
        vcat = jnp.concatenate([v_ref[:, pl.ds(off, 128)], ones], axis=1)
        outs = []
        for head in range(2):
            mine = first if head == 0 else jnp.logical_not(first)
            qm = jnp.where(mine, q2.astype(F32), 0.0).astype(BF)
            s = nt_dot(jnp.concatenate([qm, mask_one], axis=1), kcat)
            top = jnp.max(s, axis=1, keepdims=True)
            probs = jnp.exp2(s - top).astype(BF)
            acc = nn_dot(probs, vcat)
            total = acc[:, 128:256]
            outs.append(acc[:, :128] / total)
            lse = jnp.broadcast_to(top, (TB, 128)) + jnp.log(total) * LOG2E
            hi, mid, lo = split3(-lse)
            aug = jnp.where(lane == 0, hi, jnp.where(lane == 1, mid, jnp.where(lane == 2, lo, jnp.where(lane == 3, 1.0, 0.0))))
            qaug_ref[2 * p + head] = aug.astype(BF)
        osc[:, pl.ds(off, 128)] = jnp.where(first, outs[0], outs[1]).astype(BF)
        return carry

    lax.fori_loop(0, 4, pair, 0)
    o_ref[...] = osc[...]

    @pl.when(pl.program_id(0) == 0)
    def _():
        fetch_weights(rowtab, ((3, (wa, wb), 1),), wsc, sem, False)

    pa = nt_dot(osc[:, :CW], wsc[0, 0]) + nt_dot(osc[:, CW:], wsc[0, 1])
    pa_ref[...] = pa.astype(BF)


def attend(meta, rowtab, q, k, v, kaug, wa, wb):
    half = 2 * CW
    return pl.pallas_call(
        attend_kernel,
        out_shape=(
            jax.ShapeDtypeStruct((LEN, half), BF),
            jax.ShapeDtypeStruct((8, LEN, 128), BF),
            jax.ShapeDtypeStruct((LEN, D), BF),
        ),
        grid_spec=pltpu.PrefetchScalarGridSpec(
            num_scalar_prefetch=2,
            grid=(NT,),
            in_specs=[rows_spec(half), whole((LEN, half)), whole((LEN, half)), whole((LEN, 128)), ANY, ANY],
            out_specs=(rows_spec(half), pl.BlockSpec((8, TB, 128), lambda i, *_: (0, i, 0)), rows_spec(D)),
            scratch_shapes=[
                pltpu.VMEM((1, 2, D, CW), BF),
                pltpu.VMEM((TB, half), BF),
                pltpu.SemaphoreType.DMA(()),
            ],
        ),
        compiler_params=params(),
        cost_estimate=cost(12e9, 10e6, 8e6),
        name="attend",
    )(meta, rowtab, q, k, v, kaug, wa, wb)


def middle_rows(x, pa, pb, vec, valid):
    a = (pa.astype(F32) + pb.astype(F32) + vec[3:4, :]) * valid
    return a, x.astype(F32) + vec[9:10, :] * a


def valid_rows(start, rows, length):
    return (start + lax.broadcasted_iota(jnp.int32, (rows, 1), 0) < length).astype(F32)


def gelu_parts(v):
    c0 = math.sqrt(2.0 / math.pi)
    sq = v * v
    t = jnp.tanh(v * (c0 + (c0 * 0.044715) * sq))
    half = 0.5 * (1.0 + t)
    slope = half + (0.5 * v) * (1.0 - t * t) * (c0 + (3.0 * c0 * 0.044715) * sq)
    return v * half, slope


def fetch_flat(rowcol, mat, arrays, index, dest, lane, sem, start):
    n_dp, _, rows, _ = arrays[0].shape
    for side in range(2):

        def step(slot, carry, side=side):
            code = rowcol[mat, side * n_dp + slot]
            first = pl.multiple_of((code // 2) * rows, rows)
            to = pl.multiple_of(lane + (code % 2) * CW, CW)
            copy = pltpu.make_async_copy(
                arrays[side].at[slot, index], dest.at[pl.ds(first, rows), pl.ds(to, CW)], sem
            )
            if start:
                copy.start()
            else:
                copy.wait()
            return carry

        lax.fori_loop(0, n_dp, step, 0, unroll=n_dp <= 8)


def feed_kernel(
    meta, rowtab, slottab, x_ref, pa_ref, pb_ref, g_ref, vec_ref, c0, c1, d0, d1,
    pfk_ref, pfs_ref, pg_ref, n2_ref, inv_ref, gb_ref, gck_ref, gcs_ref, gdk_ref, gds_ref,
    w_in, w_out, h2t, gft, zsc, ghsc, fsc, stage, sem_in, sem_out, gsem,
):
    c, length = meta[1], meta[2]
    step = pl.program_id(0)

    def weights(start):
        for e in range(2):
            fetch_flat(rowtab, 4 + e, (c0, c1), e, w_in, e * 2 * CW, sem_in, start)
        for e in range(2):
            fetch_flat(rowtab, 6 + e, (d0, d1), e, w_out, e * 2 * CW, sem_out, start)

    @pl.when(step == 0)
    def _():
        weights(True)
        gb_ref[...] = jnp.zeros_like(gb_ref)

    _, x1 = middle_rows(x_ref[...], pa_ref[...], pb_ref[...], vec_ref, valid_rows(step * TB, TB, length))
    n2, inv = layer_norm(x1)
    n2_ref[...] = n2.astype(BF)
    inv_ref[...] = jnp.broadcast_to(inv, (TB, 128))
    hh = (n2 * (1.0 + vec_ref[11:12, :]) + vec_ref[10:11, :]).astype(BF)
    gg = (vec_ref[12:13, :] * g_ref[...].astype(F32)).astype(BF)
    at = pl.ds(pl.multiple_of(step * TB, TB), TB)
    h2t[:, at] = hh.T
    gft[:, at] = gg.T
    gb_ref[2:3, :] += jnp.sum(gg.astype(F32), axis=0, keepdims=True)

    @pl.when(step == 0)
    def _():
        weights(False)

    for block in range(4):
        e, col = block // 2, block % 2
        here = slice(block * CW, (block + 1) * CW)
        off = pl.multiple_of((col * 2 + c) * CW, CW)
        z, slope = gelu_parts(nn_dot(hh, w_in[:, here]) + vec_ref[4 + e : 5 + e, pl.ds(off, CW)])
        zsc[at, here] = z.astype(BF)
        ghb = (nn_dot(gg, w_out[:, here]) * slope).astype(BF)
        ghsc[at, here] = ghb
        gb_ref[e : e + 1, pl.ds(off, CW)] += jnp.sum(ghb.astype(F32), axis=0, keepdims=True)
    fsc[...] = nt_dot(zsc[at, :], w_out[...]).astype(BF)
    pg_ref[...] = nt_dot(ghsc[at, :], w_in[...]).astype(BF)
    for block in range(2):
        mine = pl.ds(pl.multiple_of((block * 2 + c) * CW, CW), CW)
        theirs = pl.ds(pl.multiple_of((block * 2 + 1 - c) * CW, CW), CW)
        pfk_ref[:, block * CW : (block + 1) * CW] = fsc[:, mine]
        pfs_ref[:, block * CW : (block + 1) * CW] = fsc[:, theirs]

    @pl.when(step == NT - 1)
    def _():
        targets = ((gck_ref, gcs_ref), (gdk_ref, gds_ref))
        for which, (lhs, rhs) in enumerate(((h2t, ghsc), (gft, zsc))):
            for block in range(4):
                e, col = block // 2, block % 2
                here = slice(block * CW, (block + 1) * CW)
                for r in range(NT):
                    part = slice(r * TB, (r + 1) * TB)
                    stage[which, block, part, :] = nn_dot(lhs[part, :], rhs[:, here]).astype(BF)
                store_grads(slottab, 4 + 2 * which + e, col, stage.at[which, block], targets[which], e, gsem, True)
        for which in range(2):
            for block in range(4):
                store_grads(slottab, 4, 0, stage.at[which, block], targets[which], 0, gsem, False)


def feed(meta, rowtab, slottab, x, pa, pb, g, vec, w_feed):
    grads = jax.ShapeDtypeStruct(w_feed[0].shape, BF)
    part = jax.ShapeDtypeStruct((LEN, 2 * CW), BF)
    whole_rows = jax.ShapeDtypeStruct((LEN, D), BF)
    square = pltpu.VMEM((D, D), BF)
    return pl.pallas_call(
        feed_kernel,
        out_shape=(
            part, part, whole_rows, whole_rows,
            jax.ShapeDtypeStruct((LEN, 128), F32), jax.ShapeDtypeStruct((8, D), F32),
        ) + (grads,) * 4,
        grid_spec=pltpu.PrefetchScalarGridSpec(
            num_scalar_prefetch=3,
            grid=(NT,),
            in_specs=[rows_spec(D)] * 4 + [whole(vec.shape)] + [ANY] * 4,
            out_specs=(
                rows_spec(2 * CW), rows_spec(2 * CW), rows_spec(D), rows_spec(D), rows_spec(128), whole((8, D)),
            ) + (ANY,) * 4,
            scratch_shapes=[square] * 6
            + [
                pltpu.VMEM((TB, D), BF),
                pltpu.VMEM((2, 4, D, CW), BF),
                pltpu.SemaphoreType.DMA(()),
                pltpu.SemaphoreType.DMA(()),
                pltpu.SemaphoreType.DMA(()),
            ],
        ),
        compiler_params=params(),
        cost_estimate=cost(2 * LEN * D * D * 6, 24e6, 1e6),
        name="feed",
    )(meta, rowtab, slottab, x, pa, pb, g, vec, *w_feed)


def proj_back_kernel(
    meta, rowtab, slottab, n2_ref, inv_ref, pa0, pa1, pb0, pb1, g_ref, ga_ref, gb_ref, o_ref, vec_ref, wa, wb,
    gx_ref, go_ref, sums_ref, acol_ref, keep_ref, send_ref, wsc, wacc, gxs, stage, sem, gsem,
):
    c, length = meta[1], meta[2]
    step = pl.program_id(0)

    @pl.when(step == 0)
    def _():
        fetch_flat(rowtab, 3, (wa, wb), 1, wsc, 0, sem, True)
        sums_ref[...] = jnp.zeros_like(sums_ref)
        acol_ref[...] = jnp.zeros_like(acol_ref)

    valid = valid_rows(step * TB, TB, length)
    n2 = n2_ref[...].astype(F32)
    inv = inv_ref[:, 0:1]
    gh2 = ga_ref[...].astype(F32) + gb_ref[...].astype(F32)
    gn = gh2 * (1.0 + vec_ref[11:12, :])
    ghn = gh2 * n2
    m0 = jnp.mean(gn, axis=1, keepdims=True)
    m1 = jnp.mean(gn * n2, axis=1, keepdims=True)
    gx = g_ref[...].astype(F32) + (gn - m0 - n2 * m1) * inv
    gxs[...] = gx
    gatt = (vec_ref[9:10, :] * gx * valid).astype(BF)
    sums_ref[1:2, :] += jnp.sum(gh2, axis=0, keepdims=True)
    sums_ref[2:3, :] += jnp.sum(ghn, axis=0, keepdims=True)
    sums_ref[3:4, :] += jnp.sum(gatt.astype(F32), axis=0, keepdims=True)
    for col, (pa, pb) in enumerate(((pa0, pb0), (pa1, pb1))):
        off = pl.ds(pl.multiple_of((col * 2 + c) * CW, CW), CW)
        here = slice(col * CW, (col + 1) * CW)
        a = (pa[...].astype(F32) + pb[...].astype(F32) + vec_ref[3:4, off]) * valid
        mine = gxs[:, off]
        gx_ref[:, here] = mine
        acol_ref[0:1, here] += jnp.sum(mine * a, axis=0, keepdims=True)

    @pl.when(step == 0)
    def _():
        fetch_flat(rowtab, 3, (wa, wb), 1, wsc, 0, sem, False)

    go_ref[...] = nn_dot(gatt, wsc[...]).astype(BF)
    part = nn_dot(gatt.T, o_ref[...])

    @pl.when(step == 0)
    def _():
        wacc[...] = part

    @pl.when(step > 0)
    def _():
        wacc[...] += part

    @pl.when(step == NT - 1)
    def _():
        for col in range(2):
            stage[col] = wacc[:, col * CW : (col + 1) * CW].astype(BF)
            store_grads(slottab, 3, col, stage.at[col], (keep_ref, send_ref), 0, gsem, True)
        for col in range(2):
            store_grads(slottab, 3, col, stage.at[col], (keep_ref, send_ref), 0, gsem, False)


def proj_back(meta, rowtab, slottab, n2, inv, pa, pb, g, ga, gb, o, vec, wa, wb):
    grads = jax.ShapeDtypeStruct(wa.shape[:1] + (1,) + wa.shape[2:], BF)
    half = 2 * CW
    return pl.pallas_call(
        proj_back_kernel,
        out_shape=(
            jax.ShapeDtypeStruct((LEN, half), F32),
            jax.ShapeDtypeStruct((LEN, half), BF),
            jax.ShapeDtypeStruct((8, D), F32),
            jax.ShapeDtypeStruct((8, half), F32),
            grads,
            grads,
        ),
        grid_spec=pltpu.PrefetchScalarGridSpec(
            num_scalar_prefetch=3,
            grid=(NT,),
            in_specs=[rows_spec(D), rows_spec(128)]
            + column_specs() * 2
            + [rows_spec(D)] * 3
            + [rows_spec(half), whole(vec.shape), ANY, ANY],
            out_specs=(rows_spec(half), rows_spec(half), whole((8, D)), whole((8, half)), ANY, ANY),
            scratch_shapes=[
                pltpu.VMEM((D, half), BF),
                pltpu.VMEM((D, half), F32),
                pltpu.VMEM((TB, D), F32),
                pltpu.VMEM((2, D, CW), BF),
                pltpu.SemaphoreType.DMA(()),
                pltpu.SemaphoreType.DMA(()),
            ],
        ),
        compiler_params=params(),
        cost_estimate=cost(2 * LEN * D * half * 2, 20e6),
        name="proj_back",
    )(meta, rowtab, slottab, n2, inv, pa, pa, pb, pb, g, ga, gb, o, vec, wa, wb)


HALVES = ((0, 0, 0, 0), (0, 1, 0, 1), (1, 0, 0, 2), (1, 1, 1, 0), (2, 0, 1, 1), (2, 1, 1, 2))


def attend_back_kernel(
    rowtab, slottab, q_ref, k_ref, v_ref, go_ref, o_ref, qaug_ref, kaug_ref, ct_ref, s1_ref, s2_ref, h1_ref,
    a0, a1, b0, b1,
    gb_ref, pg_ref, gxk_ref, gxs_ref, gyk_ref, gys_ref,
    qcat, gocat, kt, gqt, gall, h1, h1t, wsc, stage, pgsc, hsem, wsem, gsem, psem,
):
    pair = pl.program_id(0)

    @pl.when(pair == 0)
    def _():
        pltpu.make_async_copy(h1_ref, h1, hsem).start()
        for k, arrays, index in qkv_sources(a0, a1, b0, b1):
            fetch_flat(rowtab, k, arrays, index, wsc.at[k], 0, wsem, True)

    lane = lane_iota(LEN)
    first = lane < HEAD_DIM
    lane_kb = lane_iota(TB)
    first_kb = lane_kb < HEAD_DIM
    vaug = jnp.where(lane_kb < 3, 1.0, 0.0).astype(BF)
    go2 = go_ref[...].astype(F32)
    q2 = q_ref[...].astype(F32)
    dots = go2 * o_ref[...].astype(F32)
    for head in range(2):
        mine = first if head == 0 else jnp.logical_not(first)
        qcat[head, :, :128] = jnp.where(mine, q2, 0.0).astype(BF)
        qcat[head, :, 128:] = qaug_ref[head]
        gocat[head, :, :128] = jnp.where(mine, go2, 0.0).astype(BF)
        inner = jnp.sum(jnp.where(mine, dots, 0.0), axis=1, keepdims=True)
        hi, mid, lo = split3(-jnp.broadcast_to(inner, (LEN, 128)))
        aug = jnp.where(lane == 0, hi, jnp.where(lane == 1, mid, jnp.where(lane == 2, lo, 0.0)))
        gocat[head, :, 128:] = aug.astype(BF)
    kt[...] = k_ref[...].T
    gqt[...] = jnp.zeros_like(gqt)
    gb_ref[...] = jnp.zeros_like(gb_ref)
    here = pl.ds(pl.multiple_of(pair * 128, 128), 128)

    for kb in range(NT):
        at = slice(kb * TB, (kb + 1) * TB)
        kcat = jnp.concatenate([k_ref[at, :], kaug_ref[at, :]], axis=1)
        vcat = jnp.concatenate([v_ref[at, :], vaug], axis=1)
        gvs, gks = [], []
        for head in range(2):
            pt = jnp.exp2(nt_dot(kcat, qcat[head]))
            gpt = nt_dot(vcat, gocat[head])
            gst = (pt * gpt).astype(BF)
            gvs.append(nn_dot(pt.astype(BF), go_ref[...]))
            gks.append(nn_dot(gst, q_ref[...]))
            rows = slice(head * HEAD_DIM, (head + 1) * HEAD_DIM)
            gqt[rows, :] += nn_dot(kt[rows, at], gst)
        gv = jnp.where(first_kb, gvs[0], gvs[1]).astype(BF)
        gk = jnp.where(first_kb, gks[0], gks[1]) * LN2
        gk = rope(gk, ct_ref[at, :], s1_ref[at, :], s2_ref[at, :], -1.0).astype(BF)
        gall[1, at, here] = gk
        gall[2, at, here] = gv
        gb_ref[1:2, :] += jnp.sum(gk.astype(F32), axis=0, keepdims=True)
        gb_ref[2:3, :] += jnp.sum(gv.astype(F32), axis=0, keepdims=True)
    gq = gqt[...].T * (HEAD_DIM**-0.5)
    gq = rope(gq, ct_ref[...], s1_ref[...], s2_ref[...], -1.0).astype(BF)
    gall[0, :, here] = gq
    gb_ref[0:1, :] += jnp.sum(gq.astype(F32), axis=0, keepdims=True)

    @pl.when(pair == 3)
    def _():
        pltpu.make_async_copy(h1_ref, h1, hsem).wait()

        def flip(i, carry):
            part = pl.ds(pl.multiple_of(i * TB, TB), TB)
            h1t[:, part] = h1[part, :].T
            return carry

        lax.fori_loop(0, NT, flip, 0)
        targets = ((gxk_ref, gxs_ref), (gyk_ref, gys_ref))

        def stores(k, start):
            for mat, half, way, index in HALVES:
                if mat == k:
                    for col in range(2):
                        store_grads(
                            slottab, 14 * way + k, col, stage.at[k, col], targets[way], index, gsem, start, half
                        )

        for k in range(3):

            def rows(i, carry, k=k):
                part = pl.ds(pl.multiple_of(i * TB, TB), TB)
                grad = nn_dot(h1t[part, :], gall[k]).astype(BF)
                stage[k, 0, part, :] = grad[:, :CW]
                stage[k, 1, part, :] = grad[:, CW:]
                return carry

            lax.fori_loop(0, NT, rows, 0)
            stores(k, True)
        for k, arrays, index in qkv_sources(a0, a1, b0, b1):
            fetch_flat(rowtab, k, arrays, index, wsc.at[k], 0, wsem, False)

        def rows(i, carry):
            part = pl.ds(pl.multiple_of(i * TB, TB), TB)
            acc = nt_dot(gall[0, part, :], wsc[0])
            for k in (1, 2):
                acc += nt_dot(gall[k, part, :], wsc[k])
            pgsc[part, :] = acc.astype(BF)
            pltpu.make_async_copy(pgsc.at[part, :], pg_ref.at[part, :], psem).start()
            return carry

        lax.fori_loop(0, NT, rows, 0)
        pltpu.make_async_copy(pgsc, pg_ref, psem).wait()
        for k in range(3):
            stores(k, False)


def attend_back(rowtab, slottab, q, k, v, go, o, qaug, kaug, tables, h1, w_attn):
    n_dp, _, rows, _ = w_attn[0].shape
    half = 2 * CW
    pair = pl.BlockSpec((LEN, 128), lambda i, *_: (0, i))
    grads = jax.ShapeDtypeStruct((n_dp, 3, rows // 2, CW), BF)
    return pl.pallas_call(
        attend_back_kernel,
        out_shape=(jax.ShapeDtypeStruct((8, half), F32), jax.ShapeDtypeStruct((LEN, D), BF)) + (grads,) * 4,
        grid_spec=pltpu.PrefetchScalarGridSpec(
            num_scalar_prefetch=2,
            grid=(4,),
            in_specs=[pair] * 5
            + [pl.BlockSpec((2, LEN, 128), lambda i, *_: (i, 0, 0))]
            + [whole((LEN, 128))] * 4
            + [ANY] * 5,
            out_specs=(pl.BlockSpec((8, 128), lambda i, *_: (0, i)),) + (ANY,) * 5,
            scratch_shapes=[
                pltpu.VMEM((2, LEN, 256), BF),
                pltpu.VMEM((2, LEN, 256), BF),
                pltpu.VMEM((128, LEN), BF),
                pltpu.VMEM((128, LEN), F32),
                pltpu.VMEM((3, LEN, half), BF),
                pltpu.VMEM((LEN, D), BF),
                pltpu.VMEM((D, LEN), BF),
                pltpu.VMEM((3, D, half), BF),
                pltpu.VMEM((3, 2, D, CW), BF),
                pltpu.VMEM((LEN, D), BF),
                pltpu.SemaphoreType.DMA(()),
                pltpu.SemaphoreType.DMA(()),
                pltpu.SemaphoreType.DMA(()),
                pltpu.SemaphoreType.DMA(()),
            ],
        ),
        compiler_params=params(),
        cost_estimate=cost(40e9, 20e6, 8e6),
        name="attend_back",
    )(rowtab, slottab, q, k, v, go, o, qaug, kaug, *tables, h1, *w_attn)


def emit_kernel(meta, x0, x1, pa0, pa1, pb0, pb1, g0, g1, fk_ref, fr_ref, vec_ref, outk_ref, outs_ref, sums_ref):
    y, c, length = meta[0], meta[1], meta[2]
    step = pl.program_id(0)

    @pl.when(step == 0)
    def _():
        sums_ref[...] = jnp.zeros_like(sums_ref)

    valid = valid_rows(step * TB, TB, length)
    outs = []
    for col, (x, pa, pb, g) in enumerate(((x0, pa0, pb0, g0), (x1, pa1, pb1, g1))):
        off = pl.ds(pl.multiple_of((col * 2 + c) * CW, CW), CW)
        here = slice(col * CW, (col + 1) * CW)
        a = (pa[...].astype(F32) + pb[...].astype(F32) + vec_ref[3:4, off]) * valid
        middle = x[...].astype(F32) + vec_ref[9:10, off] * a
        f = fk_ref[:, here].astype(F32) + fr_ref[:, here].astype(F32) + vec_ref[6:7, off]
        outs.append((middle + vec_ref[12:13, off] * f).astype(BF))
        sums_ref[0:1, here] += jnp.sum(g[...].astype(F32) * f, axis=0, keepdims=True)
    outk_ref[...] = jnp.where(y == 0, outs[0].astype(F32), outs[1].astype(F32)).astype(BF)
    outs_ref[...] = jnp.where(y == 0, outs[1].astype(F32), outs[0].astype(F32)).astype(BF)


def column_specs():
    return [pl.BlockSpec((TB, CW), lambda i, meta, *_, col=col: (i, 2 * col + meta[1])) for col in range(2)]


def emit(meta, x, pa, pb, g, fk, fr, vec):
    return pl.pallas_call(
        emit_kernel,
        out_shape=(jax.ShapeDtypeStruct((LEN, CW), BF),) * 2 + (jax.ShapeDtypeStruct((8, 2 * CW), F32),),
        grid_spec=pltpu.PrefetchScalarGridSpec(
            num_scalar_prefetch=1,
            grid=(NT,),
            in_specs=column_specs() * 4 + [rows_spec(2 * CW)] * 2 + [whole(vec.shape)],
            out_specs=(rows_spec(CW),) * 2 + (whole((8, 2 * CW)),),
        ),
        compiler_params=params(),
        cost_estimate=cost(1e7, 8e6),
        name="emit",
    )(meta, x, x, pa, pa, pb, pb, g, g, fk, fr, vec)


def final_kernel(meta, x_ref, ga_ref, gb_ref, gx_ref, vec_ref, gink_ref, gins_ref, sums_ref, isc):
    y, c = meta[0], meta[1]
    step = pl.program_id(0)

    @pl.when(step == 0)
    def _():
        sums_ref[...] = jnp.zeros_like(sums_ref)

    n1, inv = layer_norm(x_ref[...].astype(F32))
    gh1 = ga_ref[...].astype(F32) + gb_ref[...].astype(F32)
    gn = gh1 * (1.0 + vec_ref[8:9, :])
    m0 = jnp.mean(gn, axis=1, keepdims=True)
    m1 = jnp.mean(gn * n1, axis=1, keepdims=True)
    isc[...] = (gn - m0 - n1 * m1) * inv
    sums_ref[0:1, :] += jnp.sum(gh1, axis=0, keepdims=True)
    sums_ref[1:2, :] += jnp.sum(gh1 * n1, axis=0, keepdims=True)
    grads = [
        gx_ref[:, col * CW : (col + 1) * CW] + isc[:, pl.ds(pl.multiple_of((col * 2 + c) * CW, CW), CW)]
        for col in range(2)
    ]
    gink_ref[...] = jnp.where(y == 0, grads[0], grads[1])
    gins_ref[...] = jnp.where(y == 0, grads[1], grads[0]).astype(BF)


def final(meta, x, ga, gb, gx, vec):
    return pl.pallas_call(
        final_kernel,
        out_shape=(
            jax.ShapeDtypeStruct((LEN, CW), F32),
            jax.ShapeDtypeStruct((LEN, CW), BF),
            jax.ShapeDtypeStruct((8, D), F32),
        ),
        grid_spec=pltpu.PrefetchScalarGridSpec(
            num_scalar_prefetch=1,
            grid=(NT,),
            in_specs=[rows_spec(D)] * 3 + [rows_spec(2 * CW), whole(vec.shape)],
            out_specs=(rows_spec(CW),) * 2 + (whole((8, D)),),
            scratch_shapes=[pltpu.VMEM((TB, D), F32)],
        ),
        compiler_params=params(),
        cost_estimate=cost(1e8, 12e6),
        name="final",
    )(meta, x, ga, gb, gx, vec)


def collect_kernel(meta, qkv_ref, feed_ref, mid_ref, gate_ref, out_ref, end_ref, hot_ref, res_ref):
    y, c = meta[0], meta[1]
    for side in range(2):
        col = jnp.bitwise_xor(y, side)
        tall = pl.ds(pl.multiple_of((col * 2 + c) * CW, CW), CW)
        short = pl.ds(pl.multiple_of(col * CW, CW), CW)
        res_ref[side, 0:3, :] = qkv_ref[0:3, short]
        res_ref[side, 3:4, :] = mid_ref[3:4, tall]
        res_ref[side, 4:7, :] = feed_ref[0:3, tall]
        res_ref[side, 7:9, :] = end_ref[0:2, tall]
        res_ref[side, 9:10, :] = gate_ref[0:1, short]
        res_ref[side, 10:12, :] = mid_ref[1:3, tall]
        res_ref[side, 12:13, :] = out_ref[0:1, short]
        res_ref[side, 13:16, :] = hot_ref[...]


def collect(meta, *parts):
    return pl.pallas_call(
        collect_kernel,
        out_shape=jax.ShapeDtypeStruct((2, 16, CW), F32),
        grid_spec=pltpu.PrefetchScalarGridSpec(
            num_scalar_prefetch=1,
            grid=(1,),
            in_specs=[whole(v.shape) for v in parts],
            out_specs=whole((2, 16, CW)),
        ),
        compiler_params=params(),
        cost_estimate=cost(1e4, 2e5),
        name="collect",
    )(meta, *parts)


def turn(a, b, contract):
    return lax.dot_general(
        a.astype(BF), b.astype(BF), ((contract[:1], contract[1:]), ((), ())), preferred_element_type=F32
    )


def soap_kernel(parts, chained, *refs):
    grads_in, (w, m1, m2, lb, rb), outs = refs[:parts], refs[parts : parts + 5], refs[parts + 5 + chained :]
    both = range(2)
    grad = [grads_in[0][i].astype(F32) for i in both]
    for extra in grads_in[1:]:
        grad = [grad[i] + extra[i].astype(F32) for i in both]
    left, right = [lb[i].astype(BF) for i in both], [rb[i].astype(BF) for i in both]
    turned = [turn(left[i], grad[i], (0, 0)) for i in both]
    turned = [turn(turned[i], right[i], (1, 0)) for i in both]
    first = [soap_first * m1[i] + (1.0 - soap_first) * turned[i] for i in both]
    second = [soap_second * m2[i] + (1.0 - soap_second) * turned[i] * turned[i] for i in both]
    back = [
        first[i]
        * (1.0 / (1.0 - soap_first**STEP))
        / (jnp.sqrt(second[i] * (1.0 / (1.0 - soap_second**STEP))) + soap_epsilon)
        for i in both
    ]
    back = [turn(left[i], back[i], (1, 0)) for i in both]
    back = [turn(back[i], right[i], (1, 1)) for i in both]
    for i in both:
        new = w[i] - soap_rate * (back[i] + soap_decay * w[i])
        outs[0][i] = grad[i]
        outs[1][i] = first[i]
        outs[2][i] = second[i]
        outs[3][i] = new
        outs[4][i] = new.astype(BF)


def soap(base, grads, state, chain):
    count, rows, _ = grads[0].shape
    total = state[0].shape[0]
    parts = len(grads)
    own = pl.BlockSpec((2, rows, CW), lambda i: (i, 0, 0))
    place = pl.BlockSpec((2, rows, CW), lambda i: (base // 2 + i, 0, 0))
    shape = jax.ShapeDtypeStruct((total, rows, CW), F32)
    return pl.pallas_call(
        functools.partial(soap_kernel, parts, len(chain)),
        out_shape=(shape,) * 4 + (jax.ShapeDtypeStruct((total, rows, CW), BF),),
        grid=(count // 2,),
        in_specs=[own] * parts
        + [place] * 3
        + [
            pl.BlockSpec((2, rows, rows), lambda i: (base // 2 + i, 0, 0)),
            pl.BlockSpec((2, CW, CW), lambda i: (base // 2 + i, 0, 0)),
        ]
        + [ANY] * len(chain),
        out_specs=(place,) * 5,
        input_output_aliases={parts + 5 + i: i for i in range(len(chain))},
        compiler_params=params(),
        cost_estimate=cost(count * rows * CW * (rows + CW) * 24, count * rows * CW * 34),
        name="soap",
    )(*grads, *state, *chain)


def xor_pairs(size, step):
    return [(i, i ^ step) for i in range(size)]


def swap(v, axis):
    return lax.ppermute(v, axis, SWAP)


def after(value, *deps):
    return lax.optimization_barrier((value,) + deps)[0]


def true_blocks(own, got, y, c):
    blocks = jnp.stack([own, got], axis=1)
    blocks = jnp.where(c == 1, blocks[:, ::-1], blocks)
    return jnp.where(y == 1, blocks[::-1], blocks)


def side_by_side(blocks):
    return jnp.concatenate([blocks[0, 0], blocks[0, 1], blocks[1, 0], blocks[1, 1]], axis=-1)


def rotary_tables(start):
    half_dim = HEAD_DIM // 2
    places = jnp.arange(LEN, dtype=F32) + start
    frequencies = 10000.0 ** (-(jnp.arange(half_dim, dtype=F32) * 2.0 / HEAD_DIM))
    angles = places[:, None] * frequencies[None, :]
    pairs = jnp.tile(jnp.repeat(angles, 2, axis=1), (1, 2))
    odd = (jnp.arange(128) % 2 == 1)[None, :]
    cos, sin = jnp.cos(pairs), jnp.sin(pairs)
    return cos, jnp.where(odd, sin, 0.0), jnp.where(odd, 0.0, -sin)


LAST = ("x", "x", "y", "y", "x", "x", "y", "y")


def body(fast, block_in, out_grad, lengths, group_ids, time_embed, weights, first_moments, second_moments,
         owners, left_basis, right_basis, biases, bias_first, bias_second):
    highest = lax.Precision.HIGHEST
    n_dp = owners.shape[1]
    z, x, y, c = (lax.axis_index(name) for name in ("z", "x", "y", "c"))
    dp = z * 2 + x
    by_matrix = lambda v: jnp.transpose(v, (1, 0, 2))
    weights, first_moments, second_moments = map(by_matrix, (weights, first_moments, second_moments))
    rows = weights.shape[1]

    def placement(start):
        columns = jnp.arange(2, dtype=jnp.int32)[None, None, :]
        holder = owners[:, :, None] + start
        yr = jnp.bitwise_xor(columns, y)
        if fast:
            zr = jnp.bitwise_xor(holder // 2, z)
            xr = jnp.bitwise_xor(holder % 2, x)
            by_x, by_y = xr * 8 + yr * 4 + zr, yr * 8 + xr * 4 + zr
        else:
            by_x = by_y = yr * n_dp + holder
        flat = lambda v: v.reshape(owners.shape[0], 2 * n_dp).astype(jnp.int32)
        by_x, by_y = flat(by_x), flat(by_y)
        x_last = jnp.array([name == "x" for name in LAST] + [False] * 6)[:, None]
        slottab = jnp.where(x_last, by_x, by_y)
        codes = jnp.arange(2 * n_dp, dtype=jnp.int32)
        rowtab = jnp.sum(
            jnp.where(slottab[:, :, None] == codes[None, None, :], codes[None, :, None], 0), axis=1
        ).astype(jnp.int32)
        meta = jnp.stack([y, c, lengths[y] + start]).astype(jnp.int32)
        return slottab, jnp.concatenate([by_x, by_y], axis=0), rowtab, meta

    cond = jax.nn.silu(time_embed).astype(BF)
    own_rows = (owners[8:] == dp).astype(F32)
    condk = jnp.sum(
        own_rows[:, None, :, None] * cond.astype(F32).reshape(1, GROUPS, n_dp, rows), axis=2
    ).astype(BF)
    own_weights, mod_part = prep(weights, condk)

    def part(v, index):
        return lax.dynamic_slice_in_dim(v, index * LEN, LEN, 0)

    def z_stage(pieces):
        return [lax.ppermute(piece, "z", xor_pairs(4, s + 1)) for s, piece in enumerate(pieces)]

    def utterance_rows(index):
        hit = (jnp.arange(GROUPS) == group_ids[index]).astype(F32)
        mods = jnp.sum(mod_all * hit[None, :, None], axis=1) + biases[7:]
        return jnp.concatenate([biases[:7], mods, jnp.zeros((3, CW), F32)], axis=0)

    both_in = jnp.stack([block_in, out_grad])
    pair = lambda index: lax.dynamic_slice_in_dim(both_in, index * LEN, LEN, 1)
    rows_own = jnp.stack([pair(y), swap(pair(1 - y), "y")])
    if fast:
        piece = own_weights[None, :4]
        z_attn = [piece] + z_stage([piece] * 3)
        mod_all = mod_part + swap(mod_part, "x")
        for step in (1, 2):
            mod_all = mod_all + lax.ppermute(mod_all, "z", xor_pairs(4, step))
    else:
        mod_all = lax.psum(mod_part, ("z", "x"))
    vec_own = jnp.stack([utterance_rows(y), swap(utterance_rows(1 - y), "y")])
    vec_got = swap(vec_own, "c")
    late = mod_all[0, 0, 0] * 0.0
    slottab, bothtab, rowtab, meta = placement(late.astype(jnp.int32))
    tables = rotary_tables(late)
    lane = jnp.arange(128)[None, :]
    padded = (jnp.arange(LEN, dtype=jnp.int32) >= meta[2])[:, None]
    kaug = jnp.where(lane < 3, 1.0, jnp.where((lane == 3) & padded, masked_score, 0.0)).astype(BF)
    if fast:
        four = jnp.concatenate(z_attn, axis=0)
        four, rows_own, vec_got, slottab, bothtab, rowtab, meta, tables, kaug = lax.optimization_barrier(
            (four, rows_own, vec_got, slottab, bothtab, rowtab, meta, tables, kaug)
        )
    rows_got = swap(rows_own, "c")
    xs, gs = assemble(meta, rows_own, rows_got)
    vec = side_by_side(true_blocks(vec_own, vec_got, y, c))
    if fast:
        a_got, b_got = swap(four[:, :2], "y"), swap(four[:, 2:], "x")
        piece = after(own_weights[None, 4:], four)
        z_feed = [piece] + z_stage([piece] * 3)
        a_got, b_got, xs, gs, vec = lax.optimization_barrier((a_got, b_got, xs, gs, vec))
        eight_a = jnp.concatenate([four[:, :2], a_got], axis=0)
        eight_b = jnp.concatenate([four[:, 2:], b_got], axis=0)
        w_attn = (eight_a, swap(eight_a, "x"), eight_b, swap(eight_b, "y"))
        z_feed, w_attn = lax.optimization_barrier((z_feed, w_attn))
        four = jnp.concatenate(z_feed, axis=0)
    else:
        gathered = [
            lax.all_gather(own_weights[None, 2 * i : 2 * i + 2], ("z", "x"), axis=0, tiled=True) for i in range(4)
        ]
        w_attn = (gathered[0], swap(gathered[0], "y"), gathered[1], swap(gathered[1], "y"))

    if fast:
        c_got, d_got = swap(four[:, :2], "y"), swap(four[:, 2:], "x")
    h1, q, k, v = qkv(meta, rowtab, xs, vec, tables, w_attn)
    if fast:
        q, c_got, d_got = lax.optimization_barrier((q, c_got, d_got))
        eight_c = jnp.concatenate([four[:, :2], c_got], axis=0)
        eight_d = jnp.concatenate([four[:, 2:], d_got], axis=0)
        w_feed = (eight_c, swap(eight_c, "x"), eight_d, swap(eight_d, "y"))
    else:
        w_feed = (gathered[2], swap(gathered[2], "y"), gathered[3], swap(gathered[3], "y"))
    o, qaug, pa = attend(meta, rowtab, q, k, v, kaug, *w_attn[2:])
    pa, w_feed = lax.optimization_barrier((pa, w_feed))
    pb = swap(pa, "c")
    pfk, pfs, g2a, n2, inv2, gb_feed, keep_c, send_c, keep_d, send_d = feed(
        meta, rowtab, slottab, xs, pa, pb, gs, vec, w_feed
    )
    g2b = swap(g2a, "c")

    def second_stage(keep, got, axis):
        total = keep.astype(F32) + got.astype(F32)
        if not fast:
            return lax.psum_scatter(total.astype(BF), ("z", "x"), scatter_dimension=0, tiled=True)[0], None
        return total[:4], swap(total[4:].astype(BF), axis)

    def third_stage(*states):
        if not fast:
            return [jnp.concatenate([state[0] for state in states], axis=0)]
        total = jnp.concatenate([keep + got.astype(F32) for keep, got in states], axis=1)
        low = total.astype(BF)
        return [total[0]] + z_stage([low[1], low[2], low[3]])

    first = lambda name: name if fast else "y"
    got_c, got_d = swap(send_c, first("x")), swap(send_d, "y")
    pfr = swap(after(pfs, g2b), "c")
    gx, go, sums_mid, sum_gate, keep_o, send_o = proj_back(
        meta, rowtab, slottab, n2, inv2, pa, pb, gs, g2a, g2b, o, vec, *w_attn[2:]
    )
    out_keep, out_send, sums_out = emit(meta, xs, pa, pb, gs, pfk, pfr, after(vec, go))
    go, got_c, got_d, out_send = lax.optimization_barrier((go, got_c, got_d, out_send))
    state_c = second_stage(keep_c, got_c, "y")
    state_d = second_stage(keep_d, got_d, "x")
    got_o, out_got = swap(send_o, "y"), swap(out_send, "y")
    gb_qkv, g1a, keep_x, send_x, keep_y, send_y = attend_back(
        rowtab, bothtab, q, k, v, go, o, qaug, kaug, tables, h1, w_attn
    )
    g1a, state_c, state_d, got_o, out_got = lax.optimization_barrier((g1a, state_c, state_d, got_o, out_got))
    g1b = swap(g1a, "c")
    got_x, got_y = swap(send_x, first("x")), swap(send_y, "y")
    state_o = second_stage(keep_o, after(got_o, g1b), "x")
    grads_feed = third_stage(state_c, state_d)
    gin_keep, gin_send, sums_end = final(meta, xs, g1a, g1b, gx, vec)
    got_x, got_y, gin_keep, gin_send, sums_end, state_o = lax.optimization_barrier(
        (got_x, got_y, gin_keep, gin_send, sums_end, state_o)
    )
    state_x = second_stage(keep_x, got_x, "y")
    state_y = second_stage(keep_y, got_y, "x")

    hot = jnp.broadcast_to((jnp.arange(CW) == group_ids[y]).astype(F32)[None], (3, CW))
    vecs = collect(meta, gb_qkv, gb_feed, sums_mid, sum_gate, sums_out, sums_end, hot)[None]
    if fast:
        for step in (1, 2):
            vecs = jnp.concatenate([vecs, lax.ppermute(vecs, "z", xor_pairs(4, step))], axis=0)
        state_x, state_y, vecs = lax.optimization_barrier((state_x, state_y, vecs))
        vecs = jnp.concatenate([vecs, swap(vecs, "x")], axis=0)
    else:
        vecs = lax.all_gather(vecs, ("z", "x"), axis=0, tiled=True)
    vecs = jnp.concatenate([vecs[:, 0], swap(vecs[:, 1], "y")], axis=0)

    state = (weights, first_moments, second_moments, left_basis, right_basis)
    chain = soap(4, after(grads_feed, got_x), state, ())
    halves = lambda v: v.reshape(v.shape[0], 2, rows // 2, CW)
    if fast:
        state_o = tuple(map(halves, state_o))
    else:
        state_o = (halves(state_o[0])[0], None)
    grads_attn = [v.reshape(4, rows, CW) for v in third_stage(state_x, state_y, state_o)]
    gin_got = swap(gin_send, "y").astype(F32)
    bias_grad = jnp.sum(vecs[:, :13], axis=0)
    grouped = jnp.einsum("ug,ukc->kgc", vecs[:, 13, :GROUPS], vecs[:, 7:13], precision=highest)
    grads_mod = jnp.einsum("kgr,kgc->krc", condk.astype(F32), grouped, precision=highest)
    chain = soap(8, [grads_mod], state, chain)
    chain = soap(0, grads_attn, state, after(chain, grads_attn))

    def both(mine, other):
        return jnp.where(
            y == 0, jnp.concatenate([mine, other], axis=0), jnp.concatenate([other, mine], axis=0)
        )

    block_out = both(out_keep, out_got)
    input_grad = both(gin_keep, gin_got)
    bias_first_new = vector_first * bias_first + (1.0 - vector_first) * bias_grad
    bias_second_new = vector_second * bias_second + (1.0 - vector_second) * bias_grad * bias_grad
    new_biases = biases - vector_rate * (bias_first_new / (1.0 - vector_first**STEP)) / (
        jnp.sqrt(bias_second_new / (1.0 - vector_second**STEP)) + vector_epsilon
    )
    return (block_out, input_grad) + tuple(map(by_matrix, chain)) + (bias_first_new, bias_second_new, new_biases)


def solution(mesh):
    n_dp = mesh.shape["dp"]
    fine = Mesh(mesh.devices.reshape(n_dp // 2, 2, 2, 2), ("z", "x", "y", "c"))
    dp, mp = ("z", "x"), ("y", "c")
    return jax.shard_map(
        functools.partial(body, n_dp == 8),
        mesh=fine,
        in_specs=(
            P(dp, mp),
            P(dp, mp),
            P(dp),
            P(dp),
            P(),
            P(dp, None, mp),
            P(dp, None, mp),
            P(dp, None, mp),
            P(),
            P(None, dp, None),
            P(None, mp, None),
            P(None, mp),
            P(None, mp),
            P(None, mp),
        ),
        out_specs=(
            P(dp, mp),
            P(dp, mp),
            P(dp, None, mp),
            P(dp, None, mp),
            P(dp, None, mp),
            P(dp, None, mp),
            P(dp, None, mp),
            P(None, mp),
            P(None, mp),
            P(None, mp),
        ),
        check_vma=False,
    )
```

```python
import functools
import math

import jax
import jax.numpy as jnp
from jax import lax
from jax.experimental import pallas as pl
from jax.experimental.pallas import tpu as pltpu
from jax.sharding import Mesh
from jax.sharding import PartitionSpec as P

D = 1024
HEAD_DIM = 64
LEN = 1024
GROUPS = 8
STEP = 10
CW = 256
TB = 256
KB = 512
SHARE = 1000
NT = LEN // TB
BF = jnp.bfloat16
F32 = jnp.float32
LOG2E = math.log2(math.e)
LN2 = math.log(2.0)

norm_epsilon = 1e-06
soap_first = 0.95
soap_second = 0.95
soap_epsilon = 1e-08
soap_rate = 0.05
soap_decay = 0.01
vector_first = 0.9
vector_second = 0.999
vector_epsilon = 1e-08
vector_rate = 0.1
masked_score = -1e30
VMEM_LIMIT = 60 * 1024 * 1024

SWAP = [(0, 1), (1, 0)]


def params(n=1):
    return pltpu.CompilerParams(
        dimension_semantics=("arbitrary",) * n, vmem_limit_bytes=VMEM_LIMIT
    )


def nt_dot(a, b):
    return lax.dot_general(a, b, (((1,), (1,)), ((), ())), preferred_element_type=F32)


def nn_dot(a, b):
    return lax.dot_general(a, b, (((1,), (0,)), ((), ())), preferred_element_type=F32)


def whole(shape):
    return pl.BlockSpec(shape, lambda *_: (0,) * len(shape))


def rows_spec(width):
    return pl.BlockSpec((TB, width), lambda i, *_: (i, 0))


ANY = pl.BlockSpec(memory_space=pl.ANY)


def cost(flops, nbytes, trans=0):
    return pl.CostEstimate(flops=int(flops) // SHARE, bytes_accessed=int(nbytes) // SHARE, transcendentals=int(trans) // SHARE)


def fetch_weights(rowcol, sources, dest, sem, start):
    for at, (mat, arrays, index) in enumerate(sources):
        n_dp, _, rows, _ = arrays[0].shape
        for side in range(2):

            def step(slot, carry, at=at, mat=mat, index=index, side=side, array=arrays[side], n_dp=n_dp, rows=rows):
                code = rowcol[mat, side * n_dp + slot]
                first = pl.multiple_of((code // 2) * rows, rows)
                copy = pltpu.make_async_copy(
                    array.at[slot, index], dest.at[at, code % 2, pl.ds(first, rows), :], sem
                )
                if start:
                    copy.start()
                else:
                    copy.wait()
                return carry

            lax.fori_loop(0, n_dp, step, 0, unroll=n_dp <= 8)


def store_grads(slottab, mat, col, staged, targets, index, sem, start, half=0):
    n_dp, _, rows, _ = targets[0].shape
    pitch = LEN // n_dp

    def step(block, carry):
        source = staged.at[pl.ds(pl.multiple_of(block * pitch + half * rows, rows), rows), :]
        if not start:
            pltpu.make_async_copy(source, targets[0].at[0, index], sem).wait()
            return carry
        code = slottab[mat, block * 2 + col]

        @pl.when(code < n_dp)
        def _():
            pltpu.make_async_copy(source, targets[0].at[code, index], sem).start()

        @pl.when(code >= n_dp)
        def _():
            pltpu.make_async_copy(source, targets[1].at[code - n_dp, index], sem).start()

        return carry

    lax.fori_loop(0, n_dp, step, 0, unroll=n_dp <= 8)


def layer_norm(x):
    mean = jnp.mean(x, axis=1, keepdims=True)
    centre = x - mean
    var = jnp.mean(centre * centre, axis=1, keepdims=True)
    inv = lax.rsqrt(var + norm_epsilon)
    return centre * inv, inv


def prep_kernel(w_ref, cond_ref, wp_ref, mod_ref):
    for k in range(8):
        wp_ref[k] = w_ref[k].astype(BF)
    for c in range(6):
        mod_ref[c] = nn_dot(cond_ref[c], w_ref[8 + c].astype(BF))


def prep(weights, condk):
    rows = weights.shape[1]
    return pl.pallas_call(
        prep_kernel,
        out_shape=(
            jax.ShapeDtypeStruct((8, rows, CW), BF),
            jax.ShapeDtypeStruct((6, GROUPS, CW), F32),
        ),
        grid=(1,),
        in_specs=[whole(weights.shape), whole(condk.shape)],
        out_specs=(whole((8, rows, CW)), whole((6, GROUPS, CW))),
        compiler_params=params(),
        cost_estimate=cost(2e6, weights.size * 6),
        name="prep",
    )(weights, condk)


def assemble_kernel(meta, *refs):
    y, c = meta[0], meta[1]
    x_ref, g_ref = refs[4:]
    for yr in range(2):
        for cr in range(2):
            off = (jnp.bitwise_xor(y, yr) * 2 + jnp.bitwise_xor(c, cr)) * CW
            off = pl.ds(pl.multiple_of(off, CW), CW)
            x_ref[:, off] = refs[yr * 2 + cr][0]
            g_ref[:, off] = refs[yr * 2 + cr][1]


def assemble(meta, *pieces):
    block = pl.BlockSpec((2, TB, CW), lambda i, *_: (0, i, 0))
    out = jax.ShapeDtypeStruct((LEN, D), BF)
    return pl.pallas_call(
        assemble_kernel,
        out_shape=(out, out),
        grid_spec=pltpu.PrefetchScalarGridSpec(
            num_scalar_prefetch=1,
            grid=(NT,),
            in_specs=[block] * 4,
            out_specs=(rows_spec(D), rows_spec(D)),
        ),
        compiler_params=params(),
        cost_estimate=cost(1e4, 8e6),
        name="assemble",
    )(meta, *pieces)


def rope(x, ct, s1, s2, sign):
    width = x.shape[1]
    up = pltpu.roll(x, 1, 1)
    down = pltpu.roll(x, width - 1, 1)
    reps = width // 128
    ct = jnp.concatenate([ct] * reps, axis=1) if reps > 1 else ct
    s1 = jnp.concatenate([s1] * reps, axis=1) if reps > 1 else s1
    s2 = jnp.concatenate([s2] * reps, axis=1) if reps > 1 else s2
    turn = up * s1 + down * s2
    return x * ct + turn if sign > 0 else x * ct - turn


def qkv_sources(a0, a1, b0, b1):
    return ((0, (a0, a1), 0), (1, (a0, a1), 1), (2, (b0, b1), 0))


def qkv_kernel(
    meta, rowtab, x_ref, vec_ref, ct_ref, s1_ref, s2_ref, a0, a1, b0, b1, h1_ref, q_ref, k_ref, v_ref, wsc, sem
):
    @pl.when(pl.program_id(0) == 0)
    def _():
        fetch_weights(rowtab, qkv_sources(a0, a1, b0, b1), wsc, sem, True)

    n1, _ = layer_norm(x_ref[...].astype(F32))
    h1 = (n1 * (1.0 + vec_ref[8:9, :]) + vec_ref[7:8, :]).astype(BF)
    h1_ref[...] = h1

    @pl.when(pl.program_id(0) == 0)
    def _():
        fetch_weights(rowtab, qkv_sources(a0, a1, b0, b1), wsc, sem, False)

    c = meta[1]
    ct, s1, s2 = ct_ref[...], s1_ref[...], s2_ref[...]
    for col in range(2):
        off = pl.multiple_of((col * 2 + c) * CW, CW)
        for k, out in ((0, q_ref), (1, k_ref), (2, v_ref)):
            acc = nn_dot(h1, wsc[k, col]) + vec_ref[k : k + 1, pl.ds(off, CW)]
            if k < 2:
                acc = rope(acc, ct, s1, s2, 1.0)
            if k == 0:
                acc = acc * (LOG2E * HEAD_DIM**-0.5)
            out[:, col * CW : (col + 1) * CW] = acc.astype(BF)


def qkv(meta, rowtab, x, vec, tables, w_attn):
    half = 2 * CW
    return pl.pallas_call(
        qkv_kernel,
        out_shape=(jax.ShapeDtypeStruct((LEN, D), BF),) + (jax.ShapeDtypeStruct((LEN, half), BF),) * 3,
        grid_spec=pltpu.PrefetchScalarGridSpec(
            num_scalar_prefetch=2,
            grid=(NT,),
            in_specs=[rows_spec(D), whole(vec.shape)] + [rows_spec(128)] * 3 + [ANY] * 4,
            out_specs=(rows_spec(D),) + (rows_spec(half),) * 3,
            scratch_shapes=[pltpu.VMEM((3, 2, D, CW), BF), pltpu.SemaphoreType.DMA(())],
        ),
        compiler_params=params(),
        cost_estimate=cost(2 * LEN * D * 3 * half, 12e6),
        name="qkv",
    )(meta, rowtab, x, vec, *tables, *w_attn)


def lane_iota(rows):
    return lax.broadcasted_iota(jnp.int32, (rows, 128), 1)


def split3(v):
    hi = v.astype(BF).astype(F32)
    mid = (v - hi).astype(BF).astype(F32)
    return hi, mid, v - hi - mid


def attend_kernel(meta, rowtab, q_ref, k_ref, v_ref, kaug_ref, wa, wb, o_ref, qaug_ref, pa_ref, wsc, osc, sem):
    @pl.when(pl.program_id(0) == 0)
    def _():
        fetch_weights(rowtab, ((3, (wa, wb), 1),), wsc, sem, True)

    lane = lane_iota(TB)
    first = lane < HEAD_DIM
    mask_one = jnp.where(lane == 3, 1.0, 0.0).astype(BF)
    ones = jnp.ones((LEN, 128), BF)
    kaug = kaug_ref[...]

    def pair(p, carry):
        off = pl.multiple_of(p * 128, 128)
        q2 = q_ref[:, pl.ds(off, 128)]
        kcat = jnp.concatenate([k_ref[:, pl.ds(off, 128)], kaug], axis=1)
        vcat = jnp.concatenate([v_ref[:, pl.ds(off, 128)], ones], axis=1)
        outs = []
        for head in range(2):
            mine = first if head == 0 else jnp.logical_not(first)
            qm = jnp.where(mine, q2.astype(F32), 0.0).astype(BF)
            s = nt_dot(jnp.concatenate([qm, mask_one], axis=1), kcat)
            top = jnp.max(s, axis=1, keepdims=True)
            probs = jnp.exp2(s - top).astype(BF)
            acc = nn_dot(probs, vcat)
            total = acc[:, 128:256]
            outs.append(acc[:, :128] / total)
            lse = jnp.broadcast_to(top, (TB, 128)) + jnp.log(total) * LOG2E
            hi, mid, lo = split3(-lse)
            aug = jnp.where(lane == 0, hi, jnp.where(lane == 1, mid, jnp.where(lane == 2, lo, jnp.where(lane == 3, 1.0, 0.0))))
            qaug_ref[2 * p + head] = aug.astype(BF)
        osc[:, pl.ds(off, 128)] = jnp.where(first, outs[0], outs[1]).astype(BF)
        return carry

    lax.fori_loop(0, 4, pair, 0, unroll=True)
    o_ref[...] = osc[...]

    @pl.when(pl.program_id(0) == 0)
    def _():
        fetch_weights(rowtab, ((3, (wa, wb), 1),), wsc, sem, False)

    pa = nt_dot(osc[:, :CW], wsc[0, 0]) + nt_dot(osc[:, CW:], wsc[0, 1])
    pa_ref[...] = pa.astype(BF)


def attend(meta, rowtab, q, k, v, kaug, wa, wb):
    half = 2 * CW
    return pl.pallas_call(
        attend_kernel,
        out_shape=(
            jax.ShapeDtypeStruct((LEN, half), BF),
            jax.ShapeDtypeStruct((8, LEN, 128), BF),
            jax.ShapeDtypeStruct((LEN, D), BF),
        ),
        grid_spec=pltpu.PrefetchScalarGridSpec(
            num_scalar_prefetch=2,
            grid=(NT,),
            in_specs=[rows_spec(half), whole((LEN, half)), whole((LEN, half)), whole((LEN, 128)), ANY, ANY],
            out_specs=(rows_spec(half), pl.BlockSpec((8, TB, 128), lambda i, *_: (0, i, 0)), rows_spec(D)),
            scratch_shapes=[
                pltpu.VMEM((1, 2, D, CW), BF),
                pltpu.VMEM((TB, half), BF),
                pltpu.SemaphoreType.DMA(()),
            ],
        ),
        compiler_params=params(),
        cost_estimate=cost(12e9, 10e6, 8e6),
        name="attend",
    )(meta, rowtab, q, k, v, kaug, wa, wb)


def middle_rows(x, pa, pb, vec, valid):
    a = (pa.astype(F32) + pb.astype(F32) + vec[3:4, :]) * valid
    return a, x.astype(F32) + vec[9:10, :] * a


def valid_rows(start, rows, length):
    return (start + lax.broadcasted_iota(jnp.int32, (rows, 1), 0) < length).astype(F32)


def gelu_parts(v):
    c0 = math.sqrt(2.0 / math.pi)
    sq = v * v
    t = jnp.tanh(v * (c0 + (c0 * 0.044715) * sq))
    half = 0.5 * (1.0 + t)
    slope = half + (0.5 * v) * (1.0 - t * t) * (c0 + (3.0 * c0 * 0.044715) * sq)
    return v * half, slope


def fetch_flat(rowcol, mat, arrays, index, dest, lane, sem, start):
    n_dp, _, rows, _ = arrays[0].shape
    for side in range(2):

        def step(slot, carry, side=side):
            code = rowcol[mat, side * n_dp + slot]
            first = pl.multiple_of((code // 2) * rows, rows)
            to = pl.multiple_of(lane + (code % 2) * CW, CW)
            copy = pltpu.make_async_copy(
                arrays[side].at[slot, index], dest.at[pl.ds(first, rows), pl.ds(to, CW)], sem
            )
            if start:
                copy.start()
            else:
                copy.wait()
            return carry

        lax.fori_loop(0, n_dp, step, 0, unroll=n_dp <= 8)


def feed_kernel(
    meta, rowtab, slottab, x_ref, pa_ref, pb_ref, g_ref, vec_ref, c0, c1, d0, d1,
    pfk_ref, pfs_ref, pg_ref, n2_ref, inv_ref, gb_ref, gck_ref, gcs_ref, gdk_ref, gds_ref,
    w_in, w_out, h2t, gft, zsc, ghsc, fsc, stage, sem_in, sem_out, gsem,
):
    c, length = meta[1], meta[2]
    step = pl.program_id(0)

    def weights(start):
        for e in range(2):
            fetch_flat(rowtab, 4 + e, (c0, c1), e, w_in, e * 2 * CW, sem_in, start)
        for e in range(2):
            fetch_flat(rowtab, 6 + e, (d0, d1), e, w_out, e * 2 * CW, sem_out, start)

    @pl.when(step == 0)
    def _():
        weights(True)
        gb_ref[...] = jnp.zeros_like(gb_ref)

    _, x1 = middle_rows(x_ref[...], pa_ref[...], pb_ref[...], vec_ref, valid_rows(step * TB, TB, length))
    n2, inv = layer_norm(x1)
    n2_ref[...] = n2.astype(BF)
    inv_ref[...] = jnp.broadcast_to(inv, (TB, 128))
    hh = (n2 * (1.0 + vec_ref[11:12, :]) + vec_ref[10:11, :]).astype(BF)
    gg = (vec_ref[12:13, :] * g_ref[...].astype(F32)).astype(BF)
    at = pl.ds(pl.multiple_of(step * TB, TB), TB)
    h2t[:, at] = hh.T
    gft[:, at] = gg.T
    gb_ref[2:3, :] += jnp.sum(gg.astype(F32), axis=0, keepdims=True)

    @pl.when(step == 0)
    def _():
        weights(False)

    for block in range(4):
        e, col = block // 2, block % 2
        here = slice(block * CW, (block + 1) * CW)
        off = pl.multiple_of((col * 2 + c) * CW, CW)
        z, slope = gelu_parts(nn_dot(hh, w_in[:, here]) + vec_ref[4 + e : 5 + e, pl.ds(off, CW)])
        zsc[at, here] = z.astype(BF)
        ghb = (nn_dot(gg, w_out[:, here]) * slope).astype(BF)
        ghsc[at, here] = ghb
        gb_ref[e : e + 1, pl.ds(off, CW)] += jnp.sum(ghb.astype(F32), axis=0, keepdims=True)
    fsc[...] = nt_dot(zsc[at, :], w_out[...]).astype(BF)
    pg_ref[...] = nt_dot(ghsc[at, :], w_in[...]).astype(BF)
    for block in range(2):
        mine = pl.ds(pl.multiple_of((block * 2 + c) * CW, CW), CW)
        theirs = pl.ds(pl.multiple_of((block * 2 + 1 - c) * CW, CW), CW)
        pfk_ref[:, block * CW : (block + 1) * CW] = fsc[:, mine]
        pfs_ref[:, block * CW : (block + 1) * CW] = fsc[:, theirs]

    @pl.when(step == NT - 1)
    def _():
        targets = ((gck_ref, gcs_ref), (gdk_ref, gds_ref))
        for which, (lhs, rhs) in enumerate(((h2t, ghsc), (gft, zsc))):
            for block in range(4):
                e, col = block // 2, block % 2
                here = slice(block * CW, (block + 1) * CW)
                for r in range(NT):
                    part = slice(r * TB, (r + 1) * TB)
                    stage[which, block, part, :] = nn_dot(lhs[part, :], rhs[:, here]).astype(BF)
                store_grads(slottab, 4 + 2 * which + e, col, stage.at[which, block], targets[which], e, gsem, True)
        for which in range(2):
            for block in range(4):
                store_grads(slottab, 4, 0, stage.at[which, block], targets[which], 0, gsem, False)


def feed(meta, rowtab, slottab, x, pa, pb, g, vec, w_feed):
    grads = jax.ShapeDtypeStruct(w_feed[0].shape, BF)
    part = jax.ShapeDtypeStruct((LEN, 2 * CW), BF)
    whole_rows = jax.ShapeDtypeStruct((LEN, D), BF)
    square = pltpu.VMEM((D, D), BF)
    return pl.pallas_call(
        feed_kernel,
        out_shape=(
            part, part, whole_rows, whole_rows,
            jax.ShapeDtypeStruct((LEN, 128), F32), jax.ShapeDtypeStruct((8, D), F32),
        ) + (grads,) * 4,
        grid_spec=pltpu.PrefetchScalarGridSpec(
            num_scalar_prefetch=3,
            grid=(NT,),
            in_specs=[rows_spec(D)] * 4 + [whole(vec.shape)] + [ANY] * 4,
            out_specs=(
                rows_spec(2 * CW), rows_spec(2 * CW), rows_spec(D), rows_spec(D), rows_spec(128), whole((8, D)),
            ) + (ANY,) * 4,
            scratch_shapes=[square] * 6
            + [
                pltpu.VMEM((TB, D), BF),
                pltpu.VMEM((2, 4, D, CW), BF),
                pltpu.SemaphoreType.DMA(()),
                pltpu.SemaphoreType.DMA(()),
                pltpu.SemaphoreType.DMA(()),
            ],
        ),
        compiler_params=params(),
        cost_estimate=cost(2 * LEN * D * D * 6, 24e6, 1e6),
        name="feed",
    )(meta, rowtab, slottab, x, pa, pb, g, vec, *w_feed)


def proj_back_kernel(
    meta, rowtab, slottab, n2_ref, inv_ref, pa0, pa1, pb0, pb1, g_ref, ga_ref, gb_ref, o_ref, vec_ref, wa, wb,
    gx_ref, go_ref, sums_ref, acol_ref, keep_ref, send_ref, wsc, wacc, gxs, stage, sem, gsem,
):
    c, length = meta[1], meta[2]
    step = pl.program_id(0)

    @pl.when(step == 0)
    def _():
        fetch_flat(rowtab, 3, (wa, wb), 1, wsc, 0, sem, True)
        sums_ref[...] = jnp.zeros_like(sums_ref)
        acol_ref[...] = jnp.zeros_like(acol_ref)

    valid = valid_rows(step * TB, TB, length)
    n2 = n2_ref[...].astype(F32)
    inv = inv_ref[:, 0:1]
    gh2 = ga_ref[...].astype(F32) + gb_ref[...].astype(F32)
    gn = gh2 * (1.0 + vec_ref[11:12, :])
    ghn = gh2 * n2
    m0 = jnp.mean(gn, axis=1, keepdims=True)
    m1 = jnp.mean(gn * n2, axis=1, keepdims=True)
    gx = g_ref[...].astype(F32) + (gn - m0 - n2 * m1) * inv
    gxs[...] = gx
    gatt = (vec_ref[9:10, :] * gx * valid).astype(BF)
    sums_ref[1:2, :] += jnp.sum(gh2, axis=0, keepdims=True)
    sums_ref[2:3, :] += jnp.sum(ghn, axis=0, keepdims=True)
    sums_ref[3:4, :] += jnp.sum(gatt.astype(F32), axis=0, keepdims=True)
    for col, (pa, pb) in enumerate(((pa0, pb0), (pa1, pb1))):
        off = pl.ds(pl.multiple_of((col * 2 + c) * CW, CW), CW)
        here = slice(col * CW, (col + 1) * CW)
        a = (pa[...].astype(F32) + pb[...].astype(F32) + vec_ref[3:4, off]) * valid
        mine = gxs[:, off]
        gx_ref[:, here] = mine
        acol_ref[0:1, here] += jnp.sum(mine * a, axis=0, keepdims=True)

    @pl.when(step == 0)
    def _():
        fetch_flat(rowtab, 3, (wa, wb), 1, wsc, 0, sem, False)

    go_ref[...] = nn_dot(gatt, wsc[...]).astype(BF)
    part = nn_dot(gatt.T, o_ref[...])

    @pl.when(step == 0)
    def _():
        wacc[...] = part

    @pl.when(step > 0)
    def _():
        wacc[...] += part

    @pl.when(step == NT - 1)
    def _():
        for col in range(2):
            stage[col] = wacc[:, col * CW : (col + 1) * CW].astype(BF)
            store_grads(slottab, 3, col, stage.at[col], (keep_ref, send_ref), 0, gsem, True)
        for col in range(2):
            store_grads(slottab, 3, col, stage.at[col], (keep_ref, send_ref), 0, gsem, False)


def proj_back(meta, rowtab, slottab, n2, inv, pa, pb, g, ga, gb, o, vec, wa, wb):
    grads = jax.ShapeDtypeStruct(wa.shape[:1] + (1,) + wa.shape[2:], BF)
    half = 2 * CW
    return pl.pallas_call(
        proj_back_kernel,
        out_shape=(
            jax.ShapeDtypeStruct((LEN, half), F32),
            jax.ShapeDtypeStruct((LEN, half), BF),
            jax.ShapeDtypeStruct((8, D), F32),
            jax.ShapeDtypeStruct((8, half), F32),
            grads,
            grads,
        ),
        grid_spec=pltpu.PrefetchScalarGridSpec(
            num_scalar_prefetch=3,
            grid=(NT,),
            in_specs=[rows_spec(D), rows_spec(128)]
            + column_specs() * 2
            + [rows_spec(D)] * 3
            + [rows_spec(half), whole(vec.shape), ANY, ANY],
            out_specs=(rows_spec(half), rows_spec(half), whole((8, D)), whole((8, half)), ANY, ANY),
            scratch_shapes=[
                pltpu.VMEM((D, half), BF),
                pltpu.VMEM((D, half), F32),
                pltpu.VMEM((TB, D), F32),
                pltpu.VMEM((2, D, CW), BF),
                pltpu.SemaphoreType.DMA(()),
                pltpu.SemaphoreType.DMA(()),
            ],
        ),
        compiler_params=params(),
        cost_estimate=cost(2 * LEN * D * half * 2, 20e6),
        name="proj_back",
    )(meta, rowtab, slottab, n2, inv, pa, pa, pb, pb, g, ga, gb, o, vec, wa, wb)


HALVES = ((0, 0, 0, 0), (0, 1, 0, 1), (1, 0, 0, 2), (1, 1, 1, 0), (2, 0, 1, 1), (2, 1, 1, 2))


def attend_back_kernel(
    rowtab, slottab, q_ref, k_ref, v_ref, go_ref, o_ref, qaug_ref, kaug_ref, ct_ref, s1_ref, s2_ref, h1_ref,
    a0, a1, b0, b1,
    gb_ref, pg_ref, gxk_ref, gxs_ref, gyk_ref, gys_ref,
    qcat, gocat, kt, gqt, gall, h1, h1t, wsc, stage, pgsc, hsem, wsem, gsem, psem,
):
    pair = pl.program_id(0)

    @pl.when(pair == 0)
    def _():
        pltpu.make_async_copy(h1_ref, h1, hsem).start()
        for k, arrays, index in qkv_sources(a0, a1, b0, b1):
            fetch_flat(rowtab, k, arrays, index, wsc.at[k], 0, wsem, True)

    lane = lane_iota(LEN)
    first = lane < HEAD_DIM
    lane_kb = lane_iota(KB)
    first_kb = lane_kb < HEAD_DIM
    vaug = jnp.where(lane_kb < 3, 1.0, 0.0).astype(BF)
    go2 = go_ref[...].astype(F32)
    q2 = q_ref[...].astype(F32)
    dots = go2 * o_ref[...].astype(F32)
    for head in range(2):
        mine = first if head == 0 else jnp.logical_not(first)
        qcat[head, :, :128] = jnp.where(mine, q2, 0.0).astype(BF)
        qcat[head, :, 128:] = qaug_ref[head]
        gocat[head, :, :128] = jnp.where(mine, go2, 0.0).astype(BF)
        inner = jnp.sum(jnp.where(mine, dots, 0.0), axis=1, keepdims=True)
        hi, mid, lo = split3(-jnp.broadcast_to(inner, (LEN, 128)))
        aug = jnp.where(lane == 0, hi, jnp.where(lane == 1, mid, jnp.where(lane == 2, lo, 0.0)))
        gocat[head, :, 128:] = aug.astype(BF)
    kt[...] = k_ref[...].T
    gqt[...] = jnp.zeros_like(gqt)
    gb_ref[...] = jnp.zeros_like(gb_ref)
    here = pl.ds(pl.multiple_of(pair * 128, 128), 128)

    for kb in range(LEN // KB):
        at = slice(kb * KB, (kb + 1) * KB)
        kcat = jnp.concatenate([k_ref[at, :], kaug_ref[at, :]], axis=1)
        vcat = jnp.concatenate([v_ref[at, :], vaug], axis=1)
        gvs, gks = [], []
        for head in range(2):
            pt = jnp.exp2(nt_dot(kcat, qcat[head]))
            gpt = nt_dot(vcat, gocat[head])
            gst = (pt * gpt).astype(BF)
            gvs.append(nn_dot(pt.astype(BF), go_ref[...]))
            gks.append(nn_dot(gst, q_ref[...]))
            rows = slice(head * HEAD_DIM, (head + 1) * HEAD_DIM)
            gqt[rows, :] += nn_dot(kt[rows, at], gst)
        gv = jnp.where(first_kb, gvs[0], gvs[1]).astype(BF)
        gk = jnp.where(first_kb, gks[0], gks[1]) * LN2
        gk = rope(gk, ct_ref[at, :], s1_ref[at, :], s2_ref[at, :], -1.0).astype(BF)
        gall[1, at, here] = gk
        gall[2, at, here] = gv
        gb_ref[1:2, :] += jnp.sum(gk.astype(F32), axis=0, keepdims=True)
        gb_ref[2:3, :] += jnp.sum(gv.astype(F32), axis=0, keepdims=True)
    gq = gqt[...].T * (HEAD_DIM**-0.5)
    gq = rope(gq, ct_ref[...], s1_ref[...], s2_ref[...], -1.0).astype(BF)
    gall[0, :, here] = gq
    gb_ref[0:1, :] += jnp.sum(gq.astype(F32), axis=0, keepdims=True)

    @pl.when(pair == 3)
    def _():
        pltpu.make_async_copy(h1_ref, h1, hsem).wait()

        def flip(i, carry):
            part = pl.ds(pl.multiple_of(i * TB, TB), TB)
            h1t[:, part] = h1[part, :].T
            return carry

        lax.fori_loop(0, NT, flip, 0)
        targets = ((gxk_ref, gxs_ref), (gyk_ref, gys_ref))

        def stores(k, start):
            for mat, half, way, index in HALVES:
                if mat == k:
                    for col in range(2):
                        store_grads(
                            slottab, 14 * way + k, col, stage.at[k, col], targets[way], index, gsem, start, half
                        )

        for k in range(3):

            def rows(i, carry, k=k):
                part = pl.ds(pl.multiple_of(i * TB, TB), TB)
                grad = nn_dot(h1t[part, :], gall[k]).astype(BF)
                stage[k, 0, part, :] = grad[:, :CW]
                stage[k, 1, part, :] = grad[:, CW:]
                return carry

            lax.fori_loop(0, NT, rows, 0)
            stores(k, True)
        for k, arrays, index in qkv_sources(a0, a1, b0, b1):
            fetch_flat(rowtab, k, arrays, index, wsc.at[k], 0, wsem, False)

        def rows(i, carry):
            part = pl.ds(pl.multiple_of(i * TB, TB), TB)
            acc = nt_dot(gall[0, part, :], wsc[0])
            for k in (1, 2):
                acc += nt_dot(gall[k, part, :], wsc[k])
            pgsc[part, :] = acc.astype(BF)
            pltpu.make_async_copy(pgsc.at[part, :], pg_ref.at[part, :], psem).start()
            return carry

        lax.fori_loop(0, NT, rows, 0)
        pltpu.make_async_copy(pgsc, pg_ref, psem).wait()
        for k in range(3):
            stores(k, False)


def attend_back(rowtab, slottab, q, k, v, go, o, qaug, kaug, tables, h1, w_attn):
    n_dp, _, rows, _ = w_attn[0].shape
    half = 2 * CW
    pair = pl.BlockSpec((LEN, 128), lambda i, *_: (0, i))
    grads = jax.ShapeDtypeStruct((n_dp, 3, rows // 2, CW), BF)
    return pl.pallas_call(
        attend_back_kernel,
        out_shape=(jax.ShapeDtypeStruct((8, half), F32), jax.ShapeDtypeStruct((LEN, D), BF)) + (grads,) * 4,
        grid_spec=pltpu.PrefetchScalarGridSpec(
            num_scalar_prefetch=2,
            grid=(4,),
            in_specs=[pair] * 5
            + [pl.BlockSpec((2, LEN, 128), lambda i, *_: (i, 0, 0))]
            + [whole((LEN, 128))] * 4
            + [ANY] * 5,
            out_specs=(pl.BlockSpec((8, 128), lambda i, *_: (0, i)),) + (ANY,) * 5,
            scratch_shapes=[
                pltpu.VMEM((2, LEN, 256), BF),
                pltpu.VMEM((2, LEN, 256), BF),
                pltpu.VMEM((128, LEN), BF),
                pltpu.VMEM((128, LEN), F32),
                pltpu.VMEM((3, LEN, half), BF),
                pltpu.VMEM((LEN, D), BF),
                pltpu.VMEM((D, LEN), BF),
                pltpu.VMEM((3, D, half), BF),
                pltpu.VMEM((3, 2, D, CW), BF),
                pltpu.VMEM((LEN, D), BF),
                pltpu.SemaphoreType.DMA(()),
                pltpu.SemaphoreType.DMA(()),
                pltpu.SemaphoreType.DMA(()),
                pltpu.SemaphoreType.DMA(()),
            ],
        ),
        compiler_params=params(),
        cost_estimate=cost(40e9, 20e6, 8e6),
        name="attend_back",
    )(rowtab, slottab, q, k, v, go, o, qaug, kaug, *tables, h1, *w_attn)


def emit_kernel(meta, x0, x1, pa0, pa1, pb0, pb1, g0, g1, fk_ref, fr_ref, vec_ref, outk_ref, outs_ref, sums_ref):
    y, c, length = meta[0], meta[1], meta[2]
    step = pl.program_id(0)

    @pl.when(step == 0)
    def _():
        sums_ref[...] = jnp.zeros_like(sums_ref)

    valid = valid_rows(step * TB, TB, length)
    outs = []
    for col, (x, pa, pb, g) in enumerate(((x0, pa0, pb0, g0), (x1, pa1, pb1, g1))):
        off = pl.ds(pl.multiple_of((col * 2 + c) * CW, CW), CW)
        here = slice(col * CW, (col + 1) * CW)
        a = (pa[...].astype(F32) + pb[...].astype(F32) + vec_ref[3:4, off]) * valid
        middle = x[...].astype(F32) + vec_ref[9:10, off] * a
        f = fk_ref[:, here].astype(F32) + fr_ref[:, here].astype(F32) + vec_ref[6:7, off]
        outs.append((middle + vec_ref[12:13, off] * f).astype(BF))
        sums_ref[0:1, here] += jnp.sum(g[...].astype(F32) * f, axis=0, keepdims=True)
    outk_ref[...] = jnp.where(y == 0, outs[0].astype(F32), outs[1].astype(F32)).astype(BF)
    outs_ref[...] = jnp.where(y == 0, outs[1].astype(F32), outs[0].astype(F32)).astype(BF)


def column_specs():
    return [pl.BlockSpec((TB, CW), lambda i, meta, *_, col=col: (i, 2 * col + meta[1])) for col in range(2)]


def emit(meta, x, pa, pb, g, fk, fr, vec):
    return pl.pallas_call(
        emit_kernel,
        out_shape=(jax.ShapeDtypeStruct((LEN, CW), BF),) * 2 + (jax.ShapeDtypeStruct((8, 2 * CW), F32),),
        grid_spec=pltpu.PrefetchScalarGridSpec(
            num_scalar_prefetch=1,
            grid=(NT,),
            in_specs=column_specs() * 4 + [rows_spec(2 * CW)] * 2 + [whole(vec.shape)],
            out_specs=(rows_spec(CW),) * 2 + (whole((8, 2 * CW)),),
        ),
        compiler_params=params(),
        cost_estimate=cost(1e7, 8e6),
        name="emit",
    )(meta, x, x, pa, pa, pb, pb, g, g, fk, fr, vec)


def final_kernel(meta, x_ref, ga_ref, gb_ref, gx_ref, vec_ref, gink_ref, gins_ref, sums_ref, isc):
    y, c = meta[0], meta[1]
    step = pl.program_id(0)

    @pl.when(step == 0)
    def _():
        sums_ref[...] = jnp.zeros_like(sums_ref)

    n1, inv = layer_norm(x_ref[...].astype(F32))
    gh1 = ga_ref[...].astype(F32) + gb_ref[...].astype(F32)
    gn = gh1 * (1.0 + vec_ref[8:9, :])
    m0 = jnp.mean(gn, axis=1, keepdims=True)
    m1 = jnp.mean(gn * n1, axis=1, keepdims=True)
    isc[...] = (gn - m0 - n1 * m1) * inv
    sums_ref[0:1, :] += jnp.sum(gh1, axis=0, keepdims=True)
    sums_ref[1:2, :] += jnp.sum(gh1 * n1, axis=0, keepdims=True)
    grads = [
        gx_ref[:, col * CW : (col + 1) * CW] + isc[:, pl.ds(pl.multiple_of((col * 2 + c) * CW, CW), CW)]
        for col in range(2)
    ]
    gink_ref[...] = jnp.where(y == 0, grads[0], grads[1])
    gins_ref[...] = jnp.where(y == 0, grads[1], grads[0]).astype(BF)


def final(meta, x, ga, gb, gx, vec):
    return pl.pallas_call(
        final_kernel,
        out_shape=(
            jax.ShapeDtypeStruct((LEN, CW), F32),
            jax.ShapeDtypeStruct((LEN, CW), BF),
            jax.ShapeDtypeStruct((8, D), F32),
        ),
        grid_spec=pltpu.PrefetchScalarGridSpec(
            num_scalar_prefetch=1,
            grid=(NT,),
            in_specs=[rows_spec(D)] * 3 + [rows_spec(2 * CW), whole(vec.shape)],
            out_specs=(rows_spec(CW),) * 2 + (whole((8, D)),),
            scratch_shapes=[pltpu.VMEM((TB, D), F32)],
        ),
        compiler_params=params(),
        cost_estimate=cost(1e8, 12e6),
        name="final",
    )(meta, x, ga, gb, gx, vec)


def collect_kernel(meta, qkv_ref, feed_ref, mid_ref, gate_ref, out_ref, end_ref, hot_ref, res_ref):
    y, c = meta[0], meta[1]
    for side in range(2):
        col = jnp.bitwise_xor(y, side)
        tall = pl.ds(pl.multiple_of((col * 2 + c) * CW, CW), CW)
        short = pl.ds(pl.multiple_of(col * CW, CW), CW)
        res_ref[side, 0:3, :] = qkv_ref[0:3, short]
        res_ref[side, 3:4, :] = mid_ref[3:4, tall]
        res_ref[side, 4:7, :] = feed_ref[0:3, tall]
        res_ref[side, 7:9, :] = end_ref[0:2, tall]
        res_ref[side, 9:10, :] = gate_ref[0:1, short]
        res_ref[side, 10:12, :] = mid_ref[1:3, tall]
        res_ref[side, 12:13, :] = out_ref[0:1, short]
        res_ref[side, 13:16, :] = hot_ref[...]


def collect(meta, *parts):
    return pl.pallas_call(
        collect_kernel,
        out_shape=jax.ShapeDtypeStruct((2, 16, CW), F32),
        grid_spec=pltpu.PrefetchScalarGridSpec(
            num_scalar_prefetch=1,
            grid=(1,),
            in_specs=[whole(v.shape) for v in parts],
            out_specs=whole((2, 16, CW)),
        ),
        compiler_params=params(),
        cost_estimate=cost(1e4, 2e5),
        name="collect",
    )(meta, *parts)


def turn(a, b, contract):
    return lax.dot_general(
        a.astype(BF), b.astype(BF), ((contract[:1], contract[1:]), ((), ())), preferred_element_type=F32
    )


def soap_kernel(parts, chained, *refs):
    grads_in, (w, m1, m2, lb, rb), outs = refs[:parts], refs[parts : parts + 5], refs[parts + 5 + chained :]
    both = range(2)
    grad = [grads_in[0][i].astype(F32) for i in both]
    for extra in grads_in[1:]:
        grad = [grad[i] + extra[i].astype(F32) for i in both]
    left, right = [lb[i].astype(BF) for i in both], [rb[i].astype(BF) for i in both]
    turned = [turn(left[i], grad[i], (0, 0)) for i in both]
    turned = [turn(turned[i], right[i], (1, 0)) for i in both]
    first = [soap_first * m1[i] + (1.0 - soap_first) * turned[i] for i in both]
    second = [soap_second * m2[i] + (1.0 - soap_second) * turned[i] * turned[i] for i in both]
    back = [
        first[i]
        * (1.0 / (1.0 - soap_first**STEP))
        / (jnp.sqrt(second[i] * (1.0 / (1.0 - soap_second**STEP))) + soap_epsilon)
        for i in both
    ]
    back = [turn(left[i], back[i], (1, 0)) for i in both]
    back = [turn(back[i], right[i], (1, 1)) for i in both]
    for i in both:
        new = w[i] - soap_rate * (back[i] + soap_decay * w[i])
        outs[0][i] = grad[i]
        outs[1][i] = first[i]
        outs[2][i] = second[i]
        outs[3][i] = new
        outs[4][i] = new.astype(BF)


def soap(base, grads, state, chain):
    count, rows, _ = grads[0].shape
    total = state[0].shape[0]
    parts = len(grads)
    own = pl.BlockSpec((2, rows, CW), lambda i: (i, 0, 0))
    place = pl.BlockSpec((2, rows, CW), lambda i: (base // 2 + i, 0, 0))
    shape = jax.ShapeDtypeStruct((total, rows, CW), F32)
    return pl.pallas_call(
        functools.partial(soap_kernel, parts, len(chain)),
        out_shape=(shape,) * 4 + (jax.ShapeDtypeStruct((total, rows, CW), BF),),
        grid=(count // 2,),
        in_specs=[own] * parts
        + [place] * 3
        + [
            pl.BlockSpec((2, rows, rows), lambda i: (base // 2 + i, 0, 0)),
            pl.BlockSpec((2, CW, CW), lambda i: (base // 2 + i, 0, 0)),
        ]
        + [ANY] * len(chain),
        out_specs=(place,) * 5,
        input_output_aliases={parts + 5 + i: i for i in range(len(chain))},
        compiler_params=params(),
        cost_estimate=cost(count * rows * CW * (rows + CW) * 24, count * rows * CW * 34),
        name="soap",
    )(*grads, *state, *chain)


def xor_pairs(size, step):
    return [(i, i ^ step) for i in range(size)]


def swap(v, axis):
    return lax.ppermute(v, axis, SWAP)


def after(value, *deps):
    return lax.optimization_barrier((value,) + deps)[0]


def true_blocks(own, got, y, c):
    blocks = jnp.stack([own, got], axis=1)
    blocks = jnp.where(c == 1, blocks[:, ::-1], blocks)
    return jnp.where(y == 1, blocks[::-1], blocks)


def side_by_side(blocks):
    return jnp.concatenate([blocks[0, 0], blocks[0, 1], blocks[1, 0], blocks[1, 1]], axis=-1)


def tables_kernel(meta, freq_ref, ct_ref, s1_ref, s2_ref, kaug_ref):
    place = pl.program_id(0) * TB + lax.broadcasted_iota(jnp.int32, (TB, 128), 0)
    lane = lane_iota(TB)
    angles = place.astype(F32) * freq_ref[0:1, :]
    sin = jnp.sin(angles)
    odd = lane % 2 == 1
    ct_ref[...] = jnp.cos(angles)
    s1_ref[...] = jnp.where(odd, sin, 0.0)
    s2_ref[...] = jnp.where(odd, 0.0, -sin)
    masked = jnp.where((lane == 3) & (place >= meta[2]), masked_score, 0.0)
    kaug_ref[...] = jnp.where(lane < 3, 1.0, masked).astype(BF)


def small_tables(meta):
    half_dim = HEAD_DIM // 2
    frequencies = 10000.0 ** (-(jnp.arange(half_dim, dtype=F32) * 2.0 / HEAD_DIM))
    freq = jnp.broadcast_to(jnp.tile(jnp.repeat(frequencies, 2), 2)[None], (8, 128))
    table = jax.ShapeDtypeStruct((LEN, 128), F32)
    out = pl.pallas_call(
        tables_kernel,
        out_shape=(table,) * 3 + (jax.ShapeDtypeStruct((LEN, 128), BF),),
        grid_spec=pltpu.PrefetchScalarGridSpec(
            num_scalar_prefetch=1,
            grid=(NT,),
            in_specs=[whole((8, 128))],
            out_specs=(rows_spec(128),) * 4,
        ),
        compiler_params=params(),
        cost_estimate=cost(1e7, 2e6),
        name="tables",
    )(meta, freq)
    return out[:3], out[3]


LAST = ("x", "x", "y", "y", "x", "x", "y", "y")


def body(fast, block_in, out_grad, lengths, group_ids, time_embed, weights, first_moments, second_moments,
         owners, left_basis, right_basis, biases, bias_first, bias_second):
    highest = lax.Precision.HIGHEST
    n_dp = owners.shape[1]
    z, x, y, c = (lax.axis_index(name) for name in ("z", "x", "y", "c"))
    dp = z * 2 + x
    by_matrix = lambda v: jnp.transpose(v, (1, 0, 2))
    weights, first_moments, second_moments = map(by_matrix, (weights, first_moments, second_moments))
    rows = weights.shape[1]

    def placement(start):
        columns = jnp.arange(2, dtype=jnp.int32)[None, None, :]
        holder = owners[:, :, None] + start
        yr = jnp.bitwise_xor(columns, y)
        if fast:
            zr = jnp.bitwise_xor(holder // 2, z)
            xr = jnp.bitwise_xor(holder % 2, x)
            by_x, by_y = xr * 8 + yr * 4 + zr, yr * 8 + xr * 4 + zr
        else:
            by_x = by_y = yr * n_dp + holder
        flat = lambda v: v.reshape(owners.shape[0], 2 * n_dp).astype(jnp.int32)
        by_x, by_y = flat(by_x), flat(by_y)
        x_last = jnp.array([name == "x" for name in LAST] + [False] * 6)[:, None]
        slottab = jnp.where(x_last, by_x, by_y)
        codes = jnp.arange(2 * n_dp, dtype=jnp.int32)
        rowtab = jnp.sum(
            jnp.where(slottab[:, :, None] == codes[None, None, :], codes[None, :, None], 0), axis=1
        ).astype(jnp.int32)
        return slottab, jnp.concatenate([by_x, by_y], axis=0), rowtab

    meta = jnp.stack([y, c, lengths[y]]).astype(jnp.int32)

    cond = jax.nn.silu(time_embed).astype(BF)
    own_rows = (owners[8:] == dp).astype(F32)
    condk = jnp.sum(
        own_rows[:, None, :, None] * cond.astype(F32).reshape(1, GROUPS, n_dp, rows), axis=2
    ).astype(BF)
    own_weights, mod_part = prep(weights, condk)

    def part(v, index):
        return lax.dynamic_slice_in_dim(v, index * LEN, LEN, 0)

    def z_stage(pieces):
        return [lax.ppermute(piece, "z", xor_pairs(4, s + 1)) for s, piece in enumerate(pieces)]

    def utterance_rows(index):
        hit = (jnp.arange(GROUPS) == group_ids[index]).astype(F32)
        mods = jnp.sum(mod_all * hit[None, :, None], axis=1) + biases[7:]
        return jnp.concatenate([biases[:7], mods, jnp.zeros((3, CW), F32)], axis=0)

    both_in = jnp.stack(after([block_in, out_grad], own_weights))
    pair = lambda index: lax.dynamic_slice_in_dim(both_in, index * LEN, LEN, 1)
    rows_mine, rows_other = pair(y), swap(pair(1 - y), "y")
    if fast:
        mod_one = mod_part + swap(mod_part, "x")
        late = (mod_one[0, 0, 0] * 0.0).astype(jnp.int32)
    else:
        mod_all = lax.psum(mod_part, ("z", "x"))
        late = 0
    slottab, bothtab, rowtab = placement(late)
    tables, kaug = small_tables(meta + late)
    if fast:
        piece = own_weights[None, :2]
        z_a = [piece] + z_stage([piece] * 3)
        piece = after(own_weights[None, 2:4], z_a)
        z_b = [piece] + z_stage([piece] * 3)
        mod_one, slottab, bothtab, rowtab, tables, kaug = lax.optimization_barrier(
            (mod_one, slottab, bothtab, rowtab, tables, kaug)
        )
        mod_two = mod_one + lax.ppermute(mod_one, "z", xor_pairs(4, 1))
        mod_all = mod_two + lax.ppermute(mod_two, "z", xor_pairs(4, 2))
        z_a, z_b, rows_other, mod_all = lax.optimization_barrier((z_a, z_b, rows_other, mod_all))
        four_a, four_b = jnp.concatenate(z_a, axis=0), jnp.concatenate(z_b, axis=0)
    rows_mine = after(rows_mine, rows_other)
    xs, gs = assemble(meta, rows_mine, swap(rows_mine, "c"), rows_other, swap(rows_other, "c"))
    vec_own = jnp.stack([utterance_rows(y), swap(utterance_rows(1 - y), "y")])
    if fast:
        a_got, b_got = swap(four_a, "y"), swap(four_b, "x")
        a_got, b_got, xs, gs, vec_own = lax.optimization_barrier((a_got, b_got, xs, gs, vec_own))
        eight_a = jnp.concatenate([four_a, a_got], axis=0)
        eight_b = jnp.concatenate([four_b, b_got], axis=0)
        w_attn = (eight_a, swap(eight_a, "x"), eight_b, swap(eight_b, "y"))
        piece = after(own_weights[None, 4:], a_got)
        z_feed = [piece] + z_stage([piece] * 3)
        z_feed, w_attn = lax.optimization_barrier((z_feed, w_attn))
        four = jnp.concatenate(z_feed, axis=0)
        four_c, four_d = four[:, :2], four[:, 2:]
    else:
        gathered = [
            lax.all_gather(own_weights[None, 2 * i : 2 * i + 2], ("z", "x"), axis=0, tiled=True) for i in range(4)
        ]
        w_attn = (gathered[0], swap(gathered[0], "y"), gathered[1], swap(gathered[1], "y"))
    vec = side_by_side(true_blocks(vec_own, swap(vec_own, "c"), y, c))

    if fast:
        c_got, d_got = swap(four_c, "y"), swap(four_d, "x")
    h1, q, k, v = qkv(meta, rowtab, xs, vec, tables, w_attn)
    if fast:
        q, c_got, d_got = lax.optimization_barrier((q, c_got, d_got))
        eight_c = jnp.concatenate([four_c, c_got], axis=0)
        eight_d = jnp.concatenate([four_d, d_got], axis=0)
        w_feed = (eight_c, swap(eight_c, "x"), eight_d, swap(eight_d, "y"))
    else:
        w_feed = (gathered[2], swap(gathered[2], "y"), gathered[3], swap(gathered[3], "y"))
    o, qaug, pa = attend(meta, rowtab, q, k, v, kaug, *w_attn[2:])
    pa, w_feed = lax.optimization_barrier((pa, w_feed))
    pb = swap(pa, "c")
    pfk, pfs, g2a, n2, inv2, gb_feed, keep_c, send_c, keep_d, send_d = feed(
        meta, rowtab, slottab, xs, pa, pb, gs, vec, w_feed
    )
    g2b = swap(g2a, "c")

    def added(keep, got):
        total = keep.astype(F32) + got.astype(F32)
        return (total[:4], total[4:].astype(BF)) if fast else (total.astype(BF), None)

    def sent(total, low, axis):
        if not fast:
            return lax.psum_scatter(total, ("z", "x"), scatter_dimension=0, tiled=True)[0], None
        return total, swap(low, axis)

    def second_stage(keep, got, axis):
        return sent(*added(keep, got), axis)

    def third_stage(*states):
        if not fast:
            return [jnp.concatenate([state[0] for state in states], axis=0)]
        total = jnp.concatenate([keep + got.astype(F32) for keep, got in states], axis=1)
        low = total.astype(BF)
        return [total[0]] + z_stage([low[1], low[2], low[3]])

    first = lambda name: name if fast else "y"
    got_c, got_d = swap(send_c, first("x")), swap(send_d, "y")
    pfr = swap(after(pfs, g2b), "c")
    gx, go, sums_mid, sum_gate, keep_o, send_o = proj_back(
        meta, rowtab, slottab, n2, inv2, pa, pb, gs, g2a, g2b, o, vec, *w_attn[2:]
    )
    out_keep, out_send, sums_out = emit(meta, xs, pa, pb, gs, pfk, pfr, after(vec, go))
    go, got_c, got_d, out_send = lax.optimization_barrier((go, got_c, got_d, out_send))
    state_c = second_stage(keep_c, got_c, "y")
    state_d = second_stage(keep_d, got_d, "x")
    got_o, out_got = swap(send_o, "y"), swap(out_send, "y")
    gb_qkv, g1a, keep_x, send_x, keep_y, send_y = attend_back(
        rowtab, bothtab, q, k, v, go, o, qaug, kaug, tables, h1, w_attn
    )
    g1a, state_c, state_d, got_o, out_got = lax.optimization_barrier((g1a, state_c, state_d, got_o, out_got))
    g1b = swap(g1a, "c")
    got_x, got_y = swap(send_x, first("x")), swap(send_y, "y")
    grads_feed = third_stage(state_c, state_d)
    gin_keep, gin_send, sums_end = final(meta, xs, g1a, g1b, gx, vec)
    got_x, got_y, gin_keep, gin_send, sums_end = lax.optimization_barrier(
        (got_x, got_y, gin_keep, gin_send, sums_end)
    )
    halves = lambda v: v.reshape(n_dp, 2, rows // 2, CW)
    joined = lambda v, w: jnp.concatenate([v, halves(w)], axis=1)
    state_x = second_stage(keep_x, got_x, "y")
    state_y = second_stage(joined(keep_y, keep_o), joined(got_y, got_o), "x")

    hot = jnp.broadcast_to((jnp.arange(CW) == group_ids[y]).astype(F32)[None], (3, CW))
    vecs = collect(meta, gb_qkv, gb_feed, sums_mid, sum_gate, sums_out, sums_end, hot)[None]
    if fast:
        vecs = jnp.concatenate([vecs] + z_stage([vecs] * 3), axis=0)
        state_x, state_y, vecs = lax.optimization_barrier((state_x, state_y, vecs))
        out_keep = after(out_keep, vecs)
        same, cross = vecs[:, 0], vecs[:, 1]
        corner = lax.ppermute(cross, ("x", "y"), [(0, 3), (1, 2), (2, 1), (3, 0)])
        vecs = jnp.concatenate([same, swap(same, "x"), swap(cross, "y"), corner], axis=0)
    else:
        vecs = lax.all_gather(vecs, ("z", "x"), axis=0, tiled=True)
        vecs = jnp.concatenate([vecs[:, 0], swap(vecs[:, 1], "y")], axis=0)

    state = (weights, first_moments, second_moments, left_basis, right_basis)
    chain = soap(4, after(grads_feed, got_x), state, ())
    grads_attn = [v.reshape(4, rows, CW) for v in third_stage(state_x, state_y)]
    gin_got = swap(after(gin_send, vecs), "y").astype(F32)
    bias_grad = jnp.sum(vecs[:, :13], axis=0)
    grouped = jnp.einsum("ug,ukc->kgc", vecs[:, 13, :GROUPS], vecs[:, 7:13], precision=highest)
    grads_mod = jnp.einsum("kgr,kgc->krc", condk.astype(F32), grouped, precision=highest)
    chain = soap(8, [grads_mod], state, chain)
    chain = soap(0, grads_attn, state, after(chain, grads_attn))

    def both(mine, other):
        return jnp.where(
            y == 0, jnp.concatenate([mine, other], axis=0), jnp.concatenate([other, mine], axis=0)
        )

    block_out = both(out_keep, out_got)
    input_grad = both(gin_keep, gin_got)
    bias_first_new = vector_first * bias_first + (1.0 - vector_first) * bias_grad
    bias_second_new = vector_second * bias_second + (1.0 - vector_second) * bias_grad * bias_grad
    new_biases = biases - vector_rate * (bias_first_new / (1.0 - vector_first**STEP)) / (
        jnp.sqrt(bias_second_new / (1.0 - vector_second**STEP)) + vector_epsilon
    )
    return (block_out, input_grad) + tuple(map(by_matrix, chain)) + (bias_first_new, bias_second_new, new_biases)


def solution(mesh):
    n_dp = mesh.shape["dp"]
    fine = Mesh(mesh.devices.reshape(n_dp // 2, 2, 2, 2), ("z", "x", "y", "c"))
    dp, mp = ("z", "x"), ("y", "c")
    return jax.shard_map(
        functools.partial(body, n_dp == 8),
        mesh=fine,
        in_specs=(
            P(dp, mp),
            P(dp, mp),
            P(dp),
            P(dp),
            P(),
            P(dp, None, mp),
            P(dp, None, mp),
            P(dp, None, mp),
            P(),
            P(None, dp, None),
            P(None, mp, None),
            P(None, mp),
            P(None, mp),
            P(None, mp),
        ),
        out_specs=(
            P(dp, mp),
            P(dp, mp),
            P(dp, None, mp),
            P(dp, None, mp),
            P(dp, None, mp),
            P(dp, None, mp),
            P(dp, None, mp),
            P(None, mp),
            P(None, mp),
            P(None, mp),
        ),
        check_vma=False,
    )
```

```python
import functools
import math

import jax
import jax.numpy as jnp
from jax import lax
from jax.experimental import pallas as pl
from jax.experimental.pallas import tpu as pltpu
from jax.sharding import Mesh
from jax.sharding import PartitionSpec as P

D = 1024
HEAD_DIM = 64
LEN = 1024
GROUPS = 8
STEP = 10
CW = 256
TB = 256
KB = 512
SHARE = 1000
NT = LEN // TB
BF = jnp.bfloat16
F32 = jnp.float32
LOG2E = math.log2(math.e)
LN2 = math.log(2.0)

norm_epsilon = 1e-06
soap_first = 0.95
soap_second = 0.95
soap_epsilon = 1e-08
soap_rate = 0.05
soap_decay = 0.01
vector_first = 0.9
vector_second = 0.999
vector_epsilon = 1e-08
vector_rate = 0.1
masked_score = -1e30

SWAP = [(0, 1), (1, 0)]


def params(megabytes):
    return pltpu.CompilerParams(dimension_semantics=("arbitrary",), vmem_limit_bytes=megabytes * 1024 * 1024)


def nt_dot(a, b):
    return lax.dot_general(a, b, (((1,), (1,)), ((), ())), preferred_element_type=F32)


def nn_dot(a, b):
    return lax.dot_general(a, b, (((1,), (0,)), ((), ())), preferred_element_type=F32)


def whole(shape):
    return pl.BlockSpec(shape, lambda *_: (0,) * len(shape))


def rows_spec(width):
    return pl.BlockSpec((TB, width), lambda i, *_: (i, 0))


ANY = pl.BlockSpec(memory_space=pl.ANY)


def cost(flops, nbytes, trans=0):
    return pl.CostEstimate(flops=int(flops) // SHARE, bytes_accessed=int(nbytes) // SHARE, transcendentals=int(trans) // SHARE)


def fetch_weights(rowcol, sources, dest, sem, start):
    for at, (mat, arrays, index) in enumerate(sources):
        n_dp, _, rows, _ = arrays[0].shape
        for side in range(2):

            def step(slot, carry, at=at, mat=mat, index=index, side=side, array=arrays[side], n_dp=n_dp, rows=rows):
                code = rowcol[mat, side * n_dp + slot]
                first = pl.multiple_of((code // 2) * rows, rows)
                copy = pltpu.make_async_copy(
                    array.at[slot, index], dest.at[at, code % 2, pl.ds(first, rows), :], sem
                )
                if start:
                    copy.start()
                else:
                    copy.wait()
                return carry

            lax.fori_loop(0, n_dp, step, 0, unroll=n_dp <= 8)


def store_grads(slottab, mat, col, staged, targets, index, sem, start, half=0):
    n_dp, _, rows, _ = targets[0].shape
    pitch = LEN // n_dp

    def step(block, carry):
        source = staged.at[pl.ds(pl.multiple_of(block * pitch + half * rows, rows), rows), :]
        if not start:
            pltpu.make_async_copy(source, targets[0].at[0, index], sem).wait()
            return carry
        code = slottab[mat, block * 2 + col]

        @pl.when(code < n_dp)
        def _():
            pltpu.make_async_copy(source, targets[0].at[code, index], sem).start()

        @pl.when(code >= n_dp)
        def _():
            pltpu.make_async_copy(source, targets[1].at[code - n_dp, index], sem).start()

        return carry

    lax.fori_loop(0, n_dp, step, 0, unroll=n_dp <= 8)


def layer_norm(x):
    mean = jnp.mean(x, axis=1, keepdims=True)
    centre = x - mean
    var = jnp.mean(centre * centre, axis=1, keepdims=True)
    inv = lax.rsqrt(var + norm_epsilon)
    return centre * inv, inv


def prep_kernel(w_ref, cond_ref, wp_ref, mod_ref):
    for k in range(8):
        wp_ref[k] = w_ref[k].astype(BF)
    for c in range(6):
        mod_ref[c] = nn_dot(cond_ref[c], w_ref[8 + c].astype(BF))


def prep(weights, condk):
    rows = weights.shape[1]
    return pl.pallas_call(
        prep_kernel,
        out_shape=(
            jax.ShapeDtypeStruct((8, rows, CW), BF),
            jax.ShapeDtypeStruct((6, GROUPS, CW), F32),
        ),
        grid=(1,),
        in_specs=[whole(weights.shape), whole(condk.shape)],
        out_specs=(whole((8, rows, CW)), whole((6, GROUPS, CW))),
        compiler_params=params(12),
        cost_estimate=cost(2e6, weights.size * 6),
        name="prep",
    )(weights, condk)


def assemble_kernel(meta, *refs):
    y, c = meta[0], meta[1]
    x_ref, g_ref = refs[4:]
    for yr in range(2):
        for cr in range(2):
            off = (jnp.bitwise_xor(y, yr) * 2 + jnp.bitwise_xor(c, cr)) * CW
            off = pl.ds(pl.multiple_of(off, CW), CW)
            x_ref[:, off] = refs[yr * 2 + cr][0]
            g_ref[:, off] = refs[yr * 2 + cr][1]


def assemble(meta, *pieces):
    block = pl.BlockSpec((2, TB, CW), lambda i, *_: (0, i, 0))
    out = jax.ShapeDtypeStruct((LEN, D), BF)
    return pl.pallas_call(
        assemble_kernel,
        out_shape=(out, out),
        grid_spec=pltpu.PrefetchScalarGridSpec(
            num_scalar_prefetch=1,
            grid=(NT,),
            in_specs=[block] * 4,
            out_specs=(rows_spec(D), rows_spec(D)),
        ),
        compiler_params=params(12),
        cost_estimate=cost(1e4, 8e6),
        name="assemble",
    )(meta, *pieces)


def rope(x, ct, s1, s2, sign):
    width = x.shape[1]
    up = pltpu.roll(x, 1, 1)
    down = pltpu.roll(x, width - 1, 1)
    reps = width // 128
    ct = jnp.concatenate([ct] * reps, axis=1) if reps > 1 else ct
    s1 = jnp.concatenate([s1] * reps, axis=1) if reps > 1 else s1
    s2 = jnp.concatenate([s2] * reps, axis=1) if reps > 1 else s2
    turn = up * s1 + down * s2
    return x * ct + turn if sign > 0 else x * ct - turn


def qkv_sources(a0, a1, b0, b1):
    return ((0, (a0, a1), 0), (1, (a0, a1), 1), (2, (b0, b1), 0))


def qkv_kernel(
    meta, rowtab, x_ref, vec_ref, ct_ref, s1_ref, s2_ref, a0, a1, b0, b1, h1_ref, q_ref, k_ref, v_ref, wsc, sem
):
    @pl.when(pl.program_id(0) == 0)
    def _():
        fetch_weights(rowtab, qkv_sources(a0, a1, b0, b1), wsc, sem, True)

    n1, _ = layer_norm(x_ref[...].astype(F32))
    h1 = (n1 * (1.0 + vec_ref[8:9, :]) + vec_ref[7:8, :]).astype(BF)
    h1_ref[...] = h1

    @pl.when(pl.program_id(0) == 0)
    def _():
        fetch_weights(rowtab, qkv_sources(a0, a1, b0, b1), wsc, sem, False)

    c = meta[1]
    ct, s1, s2 = ct_ref[...], s1_ref[...], s2_ref[...]
    for col in range(2):
        off = pl.multiple_of((col * 2 + c) * CW, CW)
        for k, out in ((0, q_ref), (1, k_ref), (2, v_ref)):
            acc = nn_dot(h1, wsc[k, col]) + vec_ref[k : k + 1, pl.ds(off, CW)]
            if k < 2:
                acc = rope(acc, ct, s1, s2, 1.0)
            if k == 0:
                acc = acc * (LOG2E * HEAD_DIM**-0.5)
            out[:, col * CW : (col + 1) * CW] = acc.astype(BF)


def qkv(meta, rowtab, x, vec, tables, w_attn):
    half = 2 * CW
    return pl.pallas_call(
        qkv_kernel,
        out_shape=(jax.ShapeDtypeStruct((LEN, D), BF),) + (jax.ShapeDtypeStruct((LEN, half), BF),) * 3,
        grid_spec=pltpu.PrefetchScalarGridSpec(
            num_scalar_prefetch=2,
            grid=(NT,),
            in_specs=[rows_spec(D), whole(vec.shape)] + [rows_spec(128)] * 3 + [ANY] * 4,
            out_specs=(rows_spec(D),) + (rows_spec(half),) * 3,
            scratch_shapes=[pltpu.VMEM((3, 2, D, CW), BF), pltpu.SemaphoreType.DMA(())],
        ),
        compiler_params=params(20),
        cost_estimate=cost(2 * LEN * D * 3 * half, 12e6),
        name="qkv",
    )(meta, rowtab, x, vec, *tables, *w_attn)


def lane_iota(rows):
    return lax.broadcasted_iota(jnp.int32, (rows, 128), 1)


def split3(v):
    hi = v.astype(BF).astype(F32)
    mid = (v - hi).astype(BF).astype(F32)
    return hi, mid, v - hi - mid


def attend_kernel(meta, rowtab, q_ref, k_ref, v_ref, kaug_ref, wa, wb, o_ref, qaug_ref, pa_ref, wsc, osc, sem):
    @pl.when(pl.program_id(0) == 0)
    def _():
        fetch_weights(rowtab, ((3, (wa, wb), 1),), wsc, sem, True)

    lane = lane_iota(TB)
    first = lane < HEAD_DIM
    mask_one = jnp.where(lane == 3, 1.0, 0.0).astype(BF)
    ones = jnp.ones((LEN, 128), BF)
    kaug = kaug_ref[...]

    def pair(p, carry):
        off = pl.multiple_of(p * 128, 128)
        q2 = q_ref[:, pl.ds(off, 128)]
        kcat = jnp.concatenate([k_ref[:, pl.ds(off, 128)], kaug], axis=1)
        vcat = jnp.concatenate([v_ref[:, pl.ds(off, 128)], ones], axis=1)
        outs = []
        for head in range(2):
            mine = first if head == 0 else jnp.logical_not(first)
            qm = jnp.where(mine, q2.astype(F32), 0.0).astype(BF)
            s = nt_dot(jnp.concatenate([qm, mask_one], axis=1), kcat)
            top = jnp.max(s, axis=1, keepdims=True)
            probs = jnp.exp2(s - top).astype(BF)
            acc = nn_dot(probs, vcat)
            total = acc[:, 128:256]
            outs.append(acc[:, :128] / total)
            lse = jnp.broadcast_to(top, (TB, 128)) + jnp.log(total) * LOG2E
            hi, mid, lo = split3(-lse)
            aug = jnp.where(lane == 0, hi, jnp.where(lane == 1, mid, jnp.where(lane == 2, lo, jnp.where(lane == 3, 1.0, 0.0))))
            qaug_ref[2 * p + head] = aug.astype(BF)
        osc[:, pl.ds(off, 128)] = jnp.where(first, outs[0], outs[1]).astype(BF)
        return carry

    lax.fori_loop(0, 4, pair, 0, unroll=True)
    o_ref[...] = osc[...]

    @pl.when(pl.program_id(0) == 0)
    def _():
        fetch_weights(rowtab, ((3, (wa, wb), 1),), wsc, sem, False)

    pa = nt_dot(osc[:, :CW], wsc[0, 0]) + nt_dot(osc[:, CW:], wsc[0, 1])
    pa_ref[...] = pa.astype(BF)


def attend(meta, rowtab, q, k, v, kaug, wa, wb):
    half = 2 * CW
    return pl.pallas_call(
        attend_kernel,
        out_shape=(
            jax.ShapeDtypeStruct((LEN, half), BF),
            jax.ShapeDtypeStruct((8, LEN, 128), BF),
            jax.ShapeDtypeStruct((LEN, D), BF),
        ),
        grid_spec=pltpu.PrefetchScalarGridSpec(
            num_scalar_prefetch=2,
            grid=(NT,),
            in_specs=[rows_spec(half), whole((LEN, half)), whole((LEN, half)), whole((LEN, 128)), ANY, ANY],
            out_specs=(rows_spec(half), pl.BlockSpec((8, TB, 128), lambda i, *_: (0, i, 0)), rows_spec(D)),
            scratch_shapes=[
                pltpu.VMEM((1, 2, D, CW), BF),
                pltpu.VMEM((TB, half), BF),
                pltpu.SemaphoreType.DMA(()),
            ],
        ),
        compiler_params=params(60),
        cost_estimate=cost(12e9, 10e6, 8e6),
        name="attend",
    )(meta, rowtab, q, k, v, kaug, wa, wb)


def middle_rows(x, pa, pb, vec, valid):
    a = (pa.astype(F32) + pb.astype(F32) + vec[3:4, :]) * valid
    return a, x.astype(F32) + vec[9:10, :] * a


def valid_rows(start, rows, length):
    return (start + lax.broadcasted_iota(jnp.int32, (rows, 1), 0) < length).astype(F32)


def gelu_parts(v):
    c0 = math.sqrt(2.0 / math.pi)
    sq = v * v
    t = jnp.tanh(v * (c0 + (c0 * 0.044715) * sq))
    half = 0.5 * (1.0 + t)
    slope = half + (0.5 * v) * (1.0 - t * t) * (c0 + (3.0 * c0 * 0.044715) * sq)
    return v * half, slope


def fetch_flat(rowcol, mat, arrays, index, dest, lane, sem, start):
    n_dp, _, rows, _ = arrays[0].shape
    for side in range(2):

        def step(slot, carry, side=side):
            code = rowcol[mat, side * n_dp + slot]
            first = pl.multiple_of((code // 2) * rows, rows)
            to = pl.multiple_of(lane + (code % 2) * CW, CW)
            copy = pltpu.make_async_copy(
                arrays[side].at[slot, index], dest.at[pl.ds(first, rows), pl.ds(to, CW)], sem
            )
            if start:
                copy.start()
            else:
                copy.wait()
            return carry

        lax.fori_loop(0, n_dp, step, 0, unroll=n_dp <= 8)


def feed_kernel(
    meta, rowtab, slottab, x_ref, pa_ref, pb_ref, g_ref, vec_ref, c0, c1, d0, d1,
    pfk_ref, pfs_ref, pg_ref, n2_ref, inv_ref, gb_ref, gck_ref, gcs_ref, gdk_ref, gds_ref,
    w_in, w_out, h2t, gft, zsc, ghsc, fsc, stage, sem_in, sem_out, gsem,
):
    c, length = meta[1], meta[2]
    step = pl.program_id(0)

    def weights(start):
        for e in range(2):
            fetch_flat(rowtab, 4 + e, (c0, c1), e, w_in, e * 2 * CW, sem_in, start)
        for e in range(2):
            fetch_flat(rowtab, 6 + e, (d0, d1), e, w_out, e * 2 * CW, sem_out, start)

    @pl.when(step == 0)
    def _():
        weights(True)
        gb_ref[...] = jnp.zeros_like(gb_ref)

    _, x1 = middle_rows(x_ref[...], pa_ref[...], pb_ref[...], vec_ref, valid_rows(step * TB, TB, length))
    n2, inv = layer_norm(x1)
    n2_ref[...] = n2.astype(BF)
    inv_ref[...] = jnp.broadcast_to(inv, (TB, 128))
    hh = (n2 * (1.0 + vec_ref[11:12, :]) + vec_ref[10:11, :]).astype(BF)
    gg = (vec_ref[12:13, :] * g_ref[...].astype(F32)).astype(BF)
    at = pl.ds(pl.multiple_of(step * TB, TB), TB)
    h2t[:, at] = hh.T
    gft[:, at] = gg.T
    gb_ref[2:3, :] += jnp.sum(gg.astype(F32), axis=0, keepdims=True)

    @pl.when(step == 0)
    def _():
        weights(False)

    for block in range(4):
        e, col = block // 2, block % 2
        here = slice(block * CW, (block + 1) * CW)
        off = pl.multiple_of((col * 2 + c) * CW, CW)
        z, slope = gelu_parts(nn_dot(hh, w_in[:, here]) + vec_ref[4 + e : 5 + e, pl.ds(off, CW)])
        zsc[at, here] = z.astype(BF)
        ghb = (nn_dot(gg, w_out[:, here]) * slope).astype(BF)
        ghsc[at, here] = ghb
        gb_ref[e : e + 1, pl.ds(off, CW)] += jnp.sum(ghb.astype(F32), axis=0, keepdims=True)
    fsc[...] = nt_dot(zsc[at, :], w_out[...]).astype(BF)
    pg_ref[...] = nt_dot(ghsc[at, :], w_in[...]).astype(BF)
    for block in range(2):
        mine = pl.ds(pl.multiple_of((block * 2 + c) * CW, CW), CW)
        theirs = pl.ds(pl.multiple_of((block * 2 + 1 - c) * CW, CW), CW)
        pfk_ref[:, block * CW : (block + 1) * CW] = fsc[:, mine]
        pfs_ref[:, block * CW : (block + 1) * CW] = fsc[:, theirs]

    @pl.when(step == NT - 1)
    def _():
        targets = ((gck_ref, gcs_ref), (gdk_ref, gds_ref))
        for which, (lhs, rhs) in enumerate(((h2t, ghsc), (gft, zsc))):
            for block in range(4):
                e, col = block // 2, block % 2
                here = slice(block * CW, (block + 1) * CW)
                for r in range(NT):
                    part = slice(r * TB, (r + 1) * TB)
                    stage[which, block, part, :] = nn_dot(lhs[part, :], rhs[:, here]).astype(BF)
                store_grads(slottab, 4 + 2 * which + e, col, stage.at[which, block], targets[which], e, gsem, True)
        for which in range(2):
            for block in range(4):
                store_grads(slottab, 4, 0, stage.at[which, block], targets[which], 0, gsem, False)


def feed(meta, rowtab, slottab, x, pa, pb, g, vec, w_feed):
    grads = jax.ShapeDtypeStruct(w_feed[0].shape, BF)
    part = jax.ShapeDtypeStruct((LEN, 2 * CW), BF)
    whole_rows = jax.ShapeDtypeStruct((LEN, D), BF)
    square = pltpu.VMEM((D, D), BF)
    return pl.pallas_call(
        feed_kernel,
        out_shape=(
            part, part, whole_rows, whole_rows,
            jax.ShapeDtypeStruct((LEN, 128), F32), jax.ShapeDtypeStruct((8, D), F32),
        ) + (grads,) * 4,
        grid_spec=pltpu.PrefetchScalarGridSpec(
            num_scalar_prefetch=3,
            grid=(NT,),
            in_specs=[rows_spec(D)] * 4 + [whole(vec.shape)] + [ANY] * 4,
            out_specs=(
                rows_spec(2 * CW), rows_spec(2 * CW), rows_spec(D), rows_spec(D), rows_spec(128), whole((8, D)),
            ) + (ANY,) * 4,
            scratch_shapes=[square] * 6
            + [
                pltpu.VMEM((TB, D), BF),
                pltpu.VMEM((2, 4, D, CW), BF),
                pltpu.SemaphoreType.DMA(()),
                pltpu.SemaphoreType.DMA(()),
                pltpu.SemaphoreType.DMA(()),
            ],
        ),
        compiler_params=params(60),
        cost_estimate=cost(2 * LEN * D * D * 6, 24e6, 1e6),
        name="feed",
    )(meta, rowtab, slottab, x, pa, pb, g, vec, *w_feed)


def proj_back_kernel(
    meta, rowtab, slottab, n2_ref, inv_ref, pa0, pa1, pb0, pb1, g_ref, ga_ref, gb_ref, o_ref, vec_ref, wa, wb,
    gx_ref, go_ref, sums_ref, acol_ref, keep_ref, send_ref, wsc, wacc, gxs, stage, sem, gsem,
):
    c, length = meta[1], meta[2]
    step = pl.program_id(0)

    @pl.when(step == 0)
    def _():
        fetch_flat(rowtab, 3, (wa, wb), 1, wsc, 0, sem, True)
        sums_ref[...] = jnp.zeros_like(sums_ref)
        acol_ref[...] = jnp.zeros_like(acol_ref)

    valid = valid_rows(step * TB, TB, length)
    n2 = n2_ref[...].astype(F32)
    inv = inv_ref[:, 0:1]
    gh2 = ga_ref[...].astype(F32) + gb_ref[...].astype(F32)
    gn = gh2 * (1.0 + vec_ref[11:12, :])
    ghn = gh2 * n2
    m0 = jnp.mean(gn, axis=1, keepdims=True)
    m1 = jnp.mean(gn * n2, axis=1, keepdims=True)
    gx = g_ref[...].astype(F32) + (gn - m0 - n2 * m1) * inv
    gxs[...] = gx
    gatt = (vec_ref[9:10, :] * gx * valid).astype(BF)
    sums_ref[1:2, :] += jnp.sum(gh2, axis=0, keepdims=True)
    sums_ref[2:3, :] += jnp.sum(ghn, axis=0, keepdims=True)
    sums_ref[3:4, :] += jnp.sum(gatt.astype(F32), axis=0, keepdims=True)
    for col, (pa, pb) in enumerate(((pa0, pb0), (pa1, pb1))):
        off = pl.ds(pl.multiple_of((col * 2 + c) * CW, CW), CW)
        here = slice(col * CW, (col + 1) * CW)
        a = (pa[...].astype(F32) + pb[...].astype(F32) + vec_ref[3:4, off]) * valid
        mine = gxs[:, off]
        gx_ref[:, here] = mine
        acol_ref[0:1, here] += jnp.sum(mine * a, axis=0, keepdims=True)

    @pl.when(step == 0)
    def _():
        fetch_flat(rowtab, 3, (wa, wb), 1, wsc, 0, sem, False)

    go_ref[...] = nn_dot(gatt, wsc[...]).astype(BF)
    part = nn_dot(gatt.T, o_ref[...])

    @pl.when(step == 0)
    def _():
        wacc[...] = part

    @pl.when(step > 0)
    def _():
        wacc[...] += part

    @pl.when(step == NT - 1)
    def _():
        for col in range(2):
            stage[col] = wacc[:, col * CW : (col + 1) * CW].astype(BF)
            store_grads(slottab, 3, col, stage.at[col], (keep_ref, send_ref), 0, gsem, True)
        for col in range(2):
            store_grads(slottab, 3, col, stage.at[col], (keep_ref, send_ref), 0, gsem, False)


def proj_back(meta, rowtab, slottab, n2, inv, pa, pb, g, ga, gb, o, vec, wa, wb):
    grads = jax.ShapeDtypeStruct(wa.shape[:1] + (1,) + wa.shape[2:], BF)
    half = 2 * CW
    return pl.pallas_call(
        proj_back_kernel,
        out_shape=(
            jax.ShapeDtypeStruct((LEN, half), F32),
            jax.ShapeDtypeStruct((LEN, half), BF),
            jax.ShapeDtypeStruct((8, D), F32),
            jax.ShapeDtypeStruct((8, half), F32),
            grads,
            grads,
        ),
        grid_spec=pltpu.PrefetchScalarGridSpec(
            num_scalar_prefetch=3,
            grid=(NT,),
            in_specs=[rows_spec(D), rows_spec(128)]
            + column_specs() * 2
            + [rows_spec(D)] * 3
            + [rows_spec(half), whole(vec.shape), ANY, ANY],
            out_specs=(rows_spec(half), rows_spec(half), whole((8, D)), whole((8, half)), ANY, ANY),
            scratch_shapes=[
                pltpu.VMEM((D, half), BF),
                pltpu.VMEM((D, half), F32),
                pltpu.VMEM((TB, D), F32),
                pltpu.VMEM((2, D, CW), BF),
                pltpu.SemaphoreType.DMA(()),
                pltpu.SemaphoreType.DMA(()),
            ],
        ),
        compiler_params=params(60),
        cost_estimate=cost(2 * LEN * D * half * 2, 20e6),
        name="proj_back",
    )(meta, rowtab, slottab, n2, inv, pa, pa, pb, pb, g, ga, gb, o, vec, wa, wb)


HALVES = ((0, 0, 0, 0), (0, 1, 0, 1), (1, 0, 0, 2), (1, 1, 1, 0), (2, 0, 1, 1), (2, 1, 1, 2))


def attend_back_kernel(
    rowtab, slottab, q_ref, k_ref, v_ref, go_ref, o_ref, qaug_ref, kaug_ref, ct_ref, s1_ref, s2_ref, h1_ref,
    a0, a1, b0, b1,
    gb_ref, pg_ref, gxk_ref, gxs_ref, gyk_ref, gys_ref,
    qcat, gocat, kt, gqt, gall, h1, h1t, wsc, stage, pgsc, hsem, wsem, gsem, psem,
):
    pair = pl.program_id(0)

    @pl.when(pair == 0)
    def _():
        pltpu.make_async_copy(h1_ref, h1, hsem).start()
        for k, arrays, index in qkv_sources(a0, a1, b0, b1):
            fetch_flat(rowtab, k, arrays, index, wsc.at[k], 0, wsem, True)

    lane = lane_iota(LEN)
    first = lane < HEAD_DIM
    lane_kb = lane_iota(KB)
    first_kb = lane_kb < HEAD_DIM
    vaug = jnp.where(lane_kb < 3, 1.0, 0.0).astype(BF)
    go2 = go_ref[...].astype(F32)
    q2 = q_ref[...].astype(F32)
    dots = go2 * o_ref[...].astype(F32)
    for head in range(2):
        mine = first if head == 0 else jnp.logical_not(first)
        qcat[head, :, :128] = jnp.where(mine, q2, 0.0).astype(BF)
        qcat[head, :, 128:] = qaug_ref[head]
        gocat[head, :, :128] = jnp.where(mine, go2, 0.0).astype(BF)
        inner = jnp.sum(jnp.where(mine, dots, 0.0), axis=1, keepdims=True)
        hi, mid, lo = split3(-jnp.broadcast_to(inner, (LEN, 128)))
        aug = jnp.where(lane == 0, hi, jnp.where(lane == 1, mid, jnp.where(lane == 2, lo, 0.0)))
        gocat[head, :, 128:] = aug.astype(BF)
    kt[...] = k_ref[...].T
    gqt[...] = jnp.zeros_like(gqt)
    gb_ref[...] = jnp.zeros_like(gb_ref)
    here = pl.ds(pl.multiple_of(pair * 128, 128), 128)

    for kb in range(LEN // KB):
        at = slice(kb * KB, (kb + 1) * KB)
        kcat = jnp.concatenate([k_ref[at, :], kaug_ref[at, :]], axis=1)
        vcat = jnp.concatenate([v_ref[at, :], vaug], axis=1)
        gvs, gks = [], []
        for head in range(2):
            pt = jnp.exp2(nt_dot(kcat, qcat[head]))
            gpt = nt_dot(vcat, gocat[head])
            gst = (pt * gpt).astype(BF)
            gvs.append(nn_dot(pt.astype(BF), go_ref[...]))
            gks.append(nn_dot(gst, q_ref[...]))
            rows = slice(head * HEAD_DIM, (head + 1) * HEAD_DIM)
            gqt[rows, :] += nn_dot(kt[rows, at], gst)
        gv = jnp.where(first_kb, gvs[0], gvs[1]).astype(BF)
        gk = jnp.where(first_kb, gks[0], gks[1]) * LN2
        gk = rope(gk, ct_ref[at, :], s1_ref[at, :], s2_ref[at, :], -1.0).astype(BF)
        gall[1, at, here] = gk
        gall[2, at, here] = gv
        gb_ref[1:2, :] += jnp.sum(gk.astype(F32), axis=0, keepdims=True)
        gb_ref[2:3, :] += jnp.sum(gv.astype(F32), axis=0, keepdims=True)
    gq = gqt[...].T * (HEAD_DIM**-0.5)
    gq = rope(gq, ct_ref[...], s1_ref[...], s2_ref[...], -1.0).astype(BF)
    gall[0, :, here] = gq
    gb_ref[0:1, :] += jnp.sum(gq.astype(F32), axis=0, keepdims=True)

    @pl.when(pair == 3)
    def _():
        pltpu.make_async_copy(h1_ref, h1, hsem).wait()

        def flip(i, carry):
            part = pl.ds(pl.multiple_of(i * TB, TB), TB)
            h1t[:, part] = h1[part, :].T
            return carry

        lax.fori_loop(0, NT, flip, 0)
        targets = ((gxk_ref, gxs_ref), (gyk_ref, gys_ref))

        def stores(k, start):
            for mat, half, way, index in HALVES:
                if mat == k:
                    for col in range(2):
                        store_grads(
                            slottab, 14 * way + k, col, stage.at[k, col], targets[way], index, gsem, start, half
                        )

        for k in range(3):

            def rows(i, carry, k=k):
                part = pl.ds(pl.multiple_of(i * TB, TB), TB)
                grad = nn_dot(h1t[part, :], gall[k]).astype(BF)
                stage[k, 0, part, :] = grad[:, :CW]
                stage[k, 1, part, :] = grad[:, CW:]
                return carry

            lax.fori_loop(0, NT, rows, 0)
            stores(k, True)
        for k, arrays, index in qkv_sources(a0, a1, b0, b1):
            fetch_flat(rowtab, k, arrays, index, wsc.at[k], 0, wsem, False)

        def rows(i, carry):
            part = pl.ds(pl.multiple_of(i * TB, TB), TB)
            acc = nt_dot(gall[0, part, :], wsc[0])
            for k in (1, 2):
                acc += nt_dot(gall[k, part, :], wsc[k])
            pgsc[part, :] = acc.astype(BF)
            pltpu.make_async_copy(pgsc.at[part, :], pg_ref.at[part, :], psem).start()
            return carry

        lax.fori_loop(0, NT, rows, 0)
        pltpu.make_async_copy(pgsc, pg_ref, psem).wait()
        for k in range(3):
            stores(k, False)


def attend_back(rowtab, slottab, q, k, v, go, o, qaug, kaug, tables, h1, w_attn):
    n_dp, _, rows, _ = w_attn[0].shape
    half = 2 * CW
    pair = pl.BlockSpec((LEN, 128), lambda i, *_: (0, i))
    grads = jax.ShapeDtypeStruct((n_dp, 3, rows // 2, CW), BF)
    return pl.pallas_call(
        attend_back_kernel,
        out_shape=(jax.ShapeDtypeStruct((8, half), F32), jax.ShapeDtypeStruct((LEN, D), BF)) + (grads,) * 4,
        grid_spec=pltpu.PrefetchScalarGridSpec(
            num_scalar_prefetch=2,
            grid=(4,),
            in_specs=[pair] * 5
            + [pl.BlockSpec((2, LEN, 128), lambda i, *_: (i, 0, 0))]
            + [whole((LEN, 128))] * 4
            + [ANY] * 5,
            out_specs=(pl.BlockSpec((8, 128), lambda i, *_: (0, i)),) + (ANY,) * 5,
            scratch_shapes=[
                pltpu.VMEM((2, LEN, 256), BF),
                pltpu.VMEM((2, LEN, 256), BF),
                pltpu.VMEM((128, LEN), BF),
                pltpu.VMEM((128, LEN), F32),
                pltpu.VMEM((3, LEN, half), BF),
                pltpu.VMEM((LEN, D), BF),
                pltpu.VMEM((D, LEN), BF),
                pltpu.VMEM((3, D, half), BF),
                pltpu.VMEM((3, 2, D, CW), BF),
                pltpu.VMEM((LEN, D), BF),
                pltpu.SemaphoreType.DMA(()),
                pltpu.SemaphoreType.DMA(()),
                pltpu.SemaphoreType.DMA(()),
                pltpu.SemaphoreType.DMA(()),
            ],
        ),
        compiler_params=params(60),
        cost_estimate=cost(40e9, 20e6, 8e6),
        name="attend_back",
    )(rowtab, slottab, q, k, v, go, o, qaug, kaug, *tables, h1, *w_attn)


def emit_kernel(meta, x0, x1, pa0, pa1, pb0, pb1, g0, g1, fk_ref, fr_ref, vec_ref, outk_ref, outs_ref, sums_ref):
    y, c, length = meta[0], meta[1], meta[2]
    step = pl.program_id(0)

    @pl.when(step == 0)
    def _():
        sums_ref[...] = jnp.zeros_like(sums_ref)

    valid = valid_rows(step * TB, TB, length)
    outs = []
    for col, (x, pa, pb, g) in enumerate(((x0, pa0, pb0, g0), (x1, pa1, pb1, g1))):
        off = pl.ds(pl.multiple_of((col * 2 + c) * CW, CW), CW)
        here = slice(col * CW, (col + 1) * CW)
        a = (pa[...].astype(F32) + pb[...].astype(F32) + vec_ref[3:4, off]) * valid
        middle = x[...].astype(F32) + vec_ref[9:10, off] * a
        f = fk_ref[:, here].astype(F32) + fr_ref[:, here].astype(F32) + vec_ref[6:7, off]
        outs.append((middle + vec_ref[12:13, off] * f).astype(BF))
        sums_ref[0:1, here] += jnp.sum(g[...].astype(F32) * f, axis=0, keepdims=True)
    outk_ref[...] = jnp.where(y == 0, outs[0].astype(F32), outs[1].astype(F32)).astype(BF)
    outs_ref[...] = jnp.where(y == 0, outs[1].astype(F32), outs[0].astype(F32)).astype(BF)


def column_specs():
    return [pl.BlockSpec((TB, CW), lambda i, meta, *_, col=col: (i, 2 * col + meta[1])) for col in range(2)]


def emit(meta, x, pa, pb, g, fk, fr, vec):
    return pl.pallas_call(
        emit_kernel,
        out_shape=(jax.ShapeDtypeStruct((LEN, CW), BF),) * 2 + (jax.ShapeDtypeStruct((8, 2 * CW), F32),),
        grid_spec=pltpu.PrefetchScalarGridSpec(
            num_scalar_prefetch=1,
            grid=(NT,),
            in_specs=column_specs() * 4 + [rows_spec(2 * CW)] * 2 + [whole(vec.shape)],
            out_specs=(rows_spec(CW),) * 2 + (whole((8, 2 * CW)),),
        ),
        compiler_params=params(60),
        cost_estimate=cost(1e7, 8e6),
        name="emit",
    )(meta, x, x, pa, pa, pb, pb, g, g, fk, fr, vec)


def final_kernel(meta, x_ref, ga_ref, gb_ref, gx_ref, vec_ref, gink_ref, gins_ref, sums_ref, isc):
    y, c = meta[0], meta[1]
    step = pl.program_id(0)

    @pl.when(step == 0)
    def _():
        sums_ref[...] = jnp.zeros_like(sums_ref)

    n1, inv = layer_norm(x_ref[...].astype(F32))
    gh1 = ga_ref[...].astype(F32) + gb_ref[...].astype(F32)
    gn = gh1 * (1.0 + vec_ref[8:9, :])
    m0 = jnp.mean(gn, axis=1, keepdims=True)
    m1 = jnp.mean(gn * n1, axis=1, keepdims=True)
    isc[...] = (gn - m0 - n1 * m1) * inv
    sums_ref[0:1, :] += jnp.sum(gh1, axis=0, keepdims=True)
    sums_ref[1:2, :] += jnp.sum(gh1 * n1, axis=0, keepdims=True)
    grads = [
        gx_ref[:, col * CW : (col + 1) * CW] + isc[:, pl.ds(pl.multiple_of((col * 2 + c) * CW, CW), CW)]
        for col in range(2)
    ]
    gink_ref[...] = jnp.where(y == 0, grads[0], grads[1])
    gins_ref[...] = jnp.where(y == 0, grads[1], grads[0]).astype(BF)


def final(meta, x, ga, gb, gx, vec):
    return pl.pallas_call(
        final_kernel,
        out_shape=(
            jax.ShapeDtypeStruct((LEN, CW), F32),
            jax.ShapeDtypeStruct((LEN, CW), BF),
            jax.ShapeDtypeStruct((8, D), F32),
        ),
        grid_spec=pltpu.PrefetchScalarGridSpec(
            num_scalar_prefetch=1,
            grid=(NT,),
            in_specs=[rows_spec(D)] * 3 + [rows_spec(2 * CW), whole(vec.shape)],
            out_specs=(rows_spec(CW),) * 2 + (whole((8, D)),),
            scratch_shapes=[pltpu.VMEM((TB, D), F32)],
        ),
        compiler_params=params(14),
        cost_estimate=cost(1e8, 12e6),
        name="final",
    )(meta, x, ga, gb, gx, vec)


def collect_kernel(meta, qkv_ref, feed_ref, mid_ref, gate_ref, out_ref, end_ref, hot_ref, res_ref):
    y, c = meta[0], meta[1]
    for side in range(2):
        col = jnp.bitwise_xor(y, side)
        tall = pl.ds(pl.multiple_of((col * 2 + c) * CW, CW), CW)
        short = pl.ds(pl.multiple_of(col * CW, CW), CW)
        res_ref[side, 0:3, :] = qkv_ref[0:3, short]
        res_ref[side, 3:4, :] = mid_ref[3:4, tall]
        res_ref[side, 4:7, :] = feed_ref[0:3, tall]
        res_ref[side, 7:9, :] = end_ref[0:2, tall]
        res_ref[side, 9:10, :] = gate_ref[0:1, short]
        res_ref[side, 10:12, :] = mid_ref[1:3, tall]
        res_ref[side, 12:13, :] = out_ref[0:1, short]
        res_ref[side, 13:16, :] = hot_ref[...]


def collect(meta, *parts):
    return pl.pallas_call(
        collect_kernel,
        out_shape=jax.ShapeDtypeStruct((2, 16, CW), F32),
        grid_spec=pltpu.PrefetchScalarGridSpec(
            num_scalar_prefetch=1,
            grid=(1,),
            in_specs=[whole(v.shape) for v in parts],
            out_specs=whole((2, 16, CW)),
        ),
        compiler_params=params(8),
        cost_estimate=cost(1e4, 2e5),
        name="collect",
    )(meta, *parts)


def turn(a, b, contract):
    return lax.dot_general(
        a.astype(BF), b.astype(BF), ((contract[:1], contract[1:]), ((), ())), preferred_element_type=F32
    )


def soap_kernel(parts, chained, *refs):
    grads_in, (w, m1, m2, lb, rb), outs = refs[:parts], refs[parts : parts + 5], refs[parts + 5 + chained :]
    both = range(2)
    grad = [grads_in[0][i].astype(F32) for i in both]
    for extra in grads_in[1:]:
        grad = [grad[i] + extra[i].astype(F32) for i in both]
    left, right = [lb[i].astype(BF) for i in both], [rb[i].astype(BF) for i in both]
    turned = [turn(left[i], grad[i], (0, 0)) for i in both]
    turned = [turn(turned[i], right[i], (1, 0)) for i in both]
    first = [soap_first * m1[i] + (1.0 - soap_first) * turned[i] for i in both]
    second = [soap_second * m2[i] + (1.0 - soap_second) * turned[i] * turned[i] for i in both]
    back = [
        first[i]
        * (1.0 / (1.0 - soap_first**STEP))
        / (jnp.sqrt(second[i] * (1.0 / (1.0 - soap_second**STEP))) + soap_epsilon)
        for i in both
    ]
    back = [turn(left[i], back[i], (1, 0)) for i in both]
    back = [turn(back[i], right[i], (1, 1)) for i in both]
    for i in both:
        new = w[i] - soap_rate * (back[i] + soap_decay * w[i])
        outs[0][i] = grad[i]
        outs[1][i] = first[i]
        outs[2][i] = second[i]
        outs[3][i] = new
        outs[4][i] = new.astype(BF)


def soap(base, grads, state, chain):
    count, rows, _ = grads[0].shape
    total = state[0].shape[0]
    parts = len(grads)
    own = pl.BlockSpec((2, rows, CW), lambda i: (i, 0, 0))
    place = pl.BlockSpec((2, rows, CW), lambda i: (base // 2 + i, 0, 0))
    shape = jax.ShapeDtypeStruct((total, rows, CW), F32)
    return pl.pallas_call(
        functools.partial(soap_kernel, parts, len(chain)),
        out_shape=(shape,) * 4 + (jax.ShapeDtypeStruct((total, rows, CW), BF),),
        grid=(count // 2,),
        in_specs=[own] * parts
        + [place] * 3
        + [
            pl.BlockSpec((2, rows, rows), lambda i: (base // 2 + i, 0, 0)),
            pl.BlockSpec((2, CW, CW), lambda i: (base // 2 + i, 0, 0)),
        ]
        + [ANY] * len(chain),
        out_specs=(place,) * 5,
        input_output_aliases={parts + 5 + i: i for i in range(len(chain))},
        compiler_params=params(12),
        cost_estimate=cost(count * rows * CW * (rows + CW) * 24, count * rows * CW * 34),
        name="soap",
    )(*grads, *state, *chain)


def xor_pairs(size, step):
    return [(i, i ^ step) for i in range(size)]


def swap(v, axis):
    return lax.ppermute(v, axis, SWAP)


def after(value, *deps):
    return lax.optimization_barrier((value,) + deps)[0]


def true_blocks(own, got, y, c):
    blocks = jnp.stack([own, got], axis=1)
    blocks = jnp.where(c == 1, blocks[:, ::-1], blocks)
    return jnp.where(y == 1, blocks[::-1], blocks)


def side_by_side(blocks):
    return jnp.concatenate([blocks[0, 0], blocks[0, 1], blocks[1, 0], blocks[1, 1]], axis=-1)


def tables_kernel(meta, freq_ref, ct_ref, s1_ref, s2_ref, kaug_ref):
    place = pl.program_id(0) * TB + lax.broadcasted_iota(jnp.int32, (TB, 128), 0)
    lane = lane_iota(TB)
    angles = place.astype(F32) * freq_ref[0:1, :]
    sin = jnp.sin(angles)
    odd = lane % 2 == 1
    ct_ref[...] = jnp.cos(angles)
    s1_ref[...] = jnp.where(odd, sin, 0.0)
    s2_ref[...] = jnp.where(odd, 0.0, -sin)
    masked = jnp.where((lane == 3) & (place >= meta[2]), masked_score, 0.0)
    kaug_ref[...] = jnp.where(lane < 3, 1.0, masked).astype(BF)


def small_tables(meta):
    half_dim = HEAD_DIM // 2
    frequencies = 10000.0 ** (-(jnp.arange(half_dim, dtype=F32) * 2.0 / HEAD_DIM))
    freq = jnp.broadcast_to(jnp.tile(jnp.repeat(frequencies, 2), 2)[None], (8, 128))
    table = jax.ShapeDtypeStruct((LEN, 128), F32)
    out = pl.pallas_call(
        tables_kernel,
        out_shape=(table,) * 3 + (jax.ShapeDtypeStruct((LEN, 128), BF),),
        grid_spec=pltpu.PrefetchScalarGridSpec(
            num_scalar_prefetch=1,
            grid=(NT,),
            in_specs=[whole((8, 128))],
            out_specs=(rows_spec(128),) * 4,
        ),
        compiler_params=params(8),
        cost_estimate=cost(1e7, 2e6),
        name="tables",
    )(meta, freq)
    return out[:3], out[3]


LAST = ("x", "x", "y", "y", "x", "x", "y", "y")


def body(fast, block_in, out_grad, lengths, group_ids, time_embed, weights, first_moments, second_moments,
         owners, left_basis, right_basis, biases, bias_first, bias_second):
    highest = lax.Precision.HIGHEST
    n_dp = owners.shape[1]
    z, x, y, c = (lax.axis_index(name) for name in ("z", "x", "y", "c"))
    dp = z * 2 + x
    by_matrix = lambda v: jnp.transpose(v, (1, 0, 2))
    weights, first_moments, second_moments = map(by_matrix, (weights, first_moments, second_moments))
    rows = weights.shape[1]

    def placement(start):
        columns = jnp.arange(2, dtype=jnp.int32)[None, None, :]
        holder = owners[:, :, None] + start
        yr = jnp.bitwise_xor(columns, y)
        if fast:
            zr = jnp.bitwise_xor(holder // 2, z)
            xr = jnp.bitwise_xor(holder % 2, x)
            by_x, by_y = xr * 8 + yr * 4 + zr, yr * 8 + xr * 4 + zr
        else:
            by_x = by_y = yr * n_dp + holder
        flat = lambda v: v.reshape(owners.shape[0], 2 * n_dp).astype(jnp.int32)
        by_x, by_y = flat(by_x), flat(by_y)
        x_last = jnp.array([name == "x" for name in LAST] + [False] * 6)[:, None]
        slottab = jnp.where(x_last, by_x, by_y)
        codes = jnp.arange(2 * n_dp, dtype=jnp.int32)
        rowtab = jnp.sum(
            jnp.where(slottab[:, :, None] == codes[None, None, :], codes[None, :, None], 0), axis=1
        ).astype(jnp.int32)
        return slottab, jnp.concatenate([by_x, by_y], axis=0), rowtab

    meta = jnp.stack([y, c, lengths[y]]).astype(jnp.int32)

    cond = jax.nn.silu(time_embed).astype(BF)
    own_rows = (owners[8:] == dp).astype(F32)
    condk = jnp.sum(
        own_rows[:, None, :, None] * cond.astype(F32).reshape(1, GROUPS, n_dp, rows), axis=2
    ).astype(BF)
    own_weights, mod_part = prep(weights, condk)

    def part(v, index):
        return lax.dynamic_slice_in_dim(v, index * LEN, LEN, 0)

    def z_stage(pieces):
        return [lax.ppermute(piece, "z", xor_pairs(4, s + 1)) for s, piece in enumerate(pieces)]

    def utterance_rows(index):
        hit = (jnp.arange(GROUPS) == group_ids[index]).astype(F32)
        mods = jnp.sum(mod_all * hit[None, :, None], axis=1) + biases[7:]
        return jnp.concatenate([biases[:7], mods, jnp.zeros((3, CW), F32)], axis=0)

    both_in = jnp.stack(after([block_in, out_grad], own_weights))
    pair = lambda index: lax.dynamic_slice_in_dim(both_in, index * LEN, LEN, 1)
    rows_mine, rows_other = pair(y), swap(pair(1 - y), "y")
    if fast:
        mod_one = mod_part + swap(mod_part, "x")
        late = (mod_one[0, 0, 0] * 0.0).astype(jnp.int32)
    else:
        mod_all = lax.psum(mod_part, ("z", "x"))
        late = 0
    slottab, bothtab, rowtab = placement(late)
    tables, kaug = small_tables(meta + late)
    if fast:
        piece = own_weights[None, :2]
        z_a = [piece] + z_stage([piece] * 3)
        piece = after(own_weights[None, 2:4], z_a)
        z_b = [piece] + z_stage([piece] * 3)
        mod_one, slottab, bothtab, rowtab, tables, kaug = lax.optimization_barrier(
            (mod_one, slottab, bothtab, rowtab, tables, kaug)
        )
        mod_two = mod_one + lax.ppermute(mod_one, "z", xor_pairs(4, 1))
        mod_all = mod_two + lax.ppermute(mod_two, "z", xor_pairs(4, 2))
        z_a, z_b, rows_other, mod_all = lax.optimization_barrier((z_a, z_b, rows_other, mod_all))
        four_a, four_b = jnp.concatenate(z_a, axis=0), jnp.concatenate(z_b, axis=0)
    rows_mine = after(rows_mine, rows_other)
    xs, gs = assemble(meta, rows_mine, swap(rows_mine, "c"), rows_other, swap(rows_other, "c"))
    vec_own = jnp.stack([utterance_rows(y), swap(utterance_rows(1 - y), "y")])
    if fast:
        a_got, b_got = swap(four_a, "y"), swap(four_b, "x")
        a_got, b_got, xs, gs, vec_own = lax.optimization_barrier((a_got, b_got, xs, gs, vec_own))
        eight_a = jnp.concatenate([four_a, a_got], axis=0)
        eight_b = jnp.concatenate([four_b, b_got], axis=0)
        w_attn = (eight_a, swap(eight_a, "x"), eight_b, swap(eight_b, "y"))
        piece = after(own_weights[None, 4:], a_got)
        z_feed = [piece] + z_stage([piece] * 3)
        z_feed, w_attn = lax.optimization_barrier((z_feed, w_attn))
        four = jnp.concatenate(z_feed, axis=0)
        four_c, four_d = four[:, :2], four[:, 2:]
    else:
        gathered = [
            lax.all_gather(own_weights[None, 2 * i : 2 * i + 2], ("z", "x"), axis=0, tiled=True) for i in range(4)
        ]
        w_attn = (gathered[0], swap(gathered[0], "y"), gathered[1], swap(gathered[1], "y"))
    vec = side_by_side(true_blocks(vec_own, swap(vec_own, "c"), y, c))

    if fast:
        c_got, d_got = swap(four_c, "y"), swap(four_d, "x")
    h1, q, k, v = qkv(meta, rowtab, xs, vec, tables, w_attn)
    if fast:
        q, c_got, d_got = lax.optimization_barrier((q, c_got, d_got))
        eight_c = jnp.concatenate([four_c, c_got], axis=0)
        eight_d = jnp.concatenate([four_d, d_got], axis=0)
        w_feed = (eight_c, swap(eight_c, "x"), eight_d, swap(eight_d, "y"))
    else:
        w_feed = (gathered[2], swap(gathered[2], "y"), gathered[3], swap(gathered[3], "y"))
    o, qaug, pa = attend(meta, rowtab, q, k, v, kaug, *w_attn[2:])
    pa, w_feed = lax.optimization_barrier((pa, w_feed))
    pb = swap(pa, "c")
    pfk, pfs, g2a, n2, inv2, gb_feed, keep_c, send_c, keep_d, send_d = feed(
        meta, rowtab, slottab, xs, pa, pb, gs, vec, w_feed
    )
    g2b = swap(g2a, "c")

    def added(keep, got):
        total = keep.astype(F32) + got.astype(F32)
        return (total[:4], total[4:].astype(BF)) if fast else (total.astype(BF), None)

    def sent(total, low, axis):
        if not fast:
            return lax.psum_scatter(total, ("z", "x"), scatter_dimension=0, tiled=True)[0], None
        return total, swap(low, axis)

    def second_stage(keep, got, axis):
        return sent(*added(keep, got), axis)

    def third_stage(*states):
        if not fast:
            return [jnp.concatenate([state[0] for state in states], axis=0)]
        total = jnp.concatenate([keep + got.astype(F32) for keep, got in states], axis=1)
        low = total.astype(BF)
        return [total[0]] + z_stage([low[1], low[2], low[3]])

    first = lambda name: name if fast else "y"
    got_c, got_d = swap(send_c, first("x")), swap(send_d, "y")
    pfr = swap(after(pfs, g2b), "c")
    gx, go, sums_mid, sum_gate, keep_o, send_o = proj_back(
        meta, rowtab, slottab, n2, inv2, pa, pb, gs, g2a, g2b, o, vec, *w_attn[2:]
    )
    out_keep, out_send, sums_out = emit(meta, xs, pa, pb, gs, pfk, pfr, after(vec, go))
    go, got_c, got_d, out_send = lax.optimization_barrier((go, got_c, got_d, out_send))
    state_c = second_stage(keep_c, got_c, "y")
    state_d = second_stage(keep_d, got_d, "x")
    got_o, out_got = swap(send_o, "y"), swap(out_send, "y")
    gb_qkv, g1a, keep_x, send_x, keep_y, send_y = attend_back(
        rowtab, bothtab, q, k, v, go, o, qaug, kaug, tables, h1, w_attn
    )
    g1a, state_c, state_d, got_o, out_got = lax.optimization_barrier((g1a, state_c, state_d, got_o, out_got))
    g1b = swap(g1a, "c")
    got_x, got_y = swap(send_x, first("x")), swap(send_y, "y")
    grads_feed = third_stage(state_c, state_d)
    gin_keep, gin_send, sums_end = final(meta, xs, g1a, g1b, gx, vec)
    got_x, got_y, gin_keep, gin_send, sums_end = lax.optimization_barrier(
        (got_x, got_y, gin_keep, gin_send, sums_end)
    )
    halves = lambda v: v.reshape(n_dp, 2, rows // 2, CW)
    joined = lambda v, w: jnp.concatenate([v, halves(w)], axis=1)
    state_x = second_stage(keep_x, got_x, "y")
    state_y = second_stage(joined(keep_y, keep_o), joined(got_y, got_o), "x")

    hot = jnp.broadcast_to((jnp.arange(CW) == group_ids[y]).astype(F32)[None], (3, CW))
    vecs = collect(meta, gb_qkv, gb_feed, sums_mid, sum_gate, sums_out, sums_end, hot)[None]
    if fast:
        vecs = jnp.concatenate([vecs] + z_stage([vecs] * 3), axis=0)
        state_x, state_y, vecs = lax.optimization_barrier((state_x, state_y, vecs))
        out_keep = after(out_keep, vecs)
        same, cross = vecs[:, 0], vecs[:, 1]
        corner = lax.ppermute(cross, ("x", "y"), [(0, 3), (1, 2), (2, 1), (3, 0)])
        vecs = jnp.concatenate([same, swap(same, "x"), swap(cross, "y"), corner], axis=0)
    else:
        vecs = lax.all_gather(vecs, ("z", "x"), axis=0, tiled=True)
        vecs = jnp.concatenate([vecs[:, 0], swap(vecs[:, 1], "y")], axis=0)

    state = (weights, first_moments, second_moments, left_basis, right_basis)
    chain = soap(4, after(grads_feed, got_x), state, ())
    grads_attn = [v.reshape(4, rows, CW) for v in third_stage(state_x, state_y)]
    gin_got = swap(after(gin_send, vecs), "y").astype(F32)
    bias_grad = jnp.sum(vecs[:, :13], axis=0)
    grouped = jnp.einsum("ug,ukc->kgc", vecs[:, 13, :GROUPS], vecs[:, 7:13], precision=highest)
    grads_mod = jnp.einsum("kgr,kgc->krc", condk.astype(F32), grouped, precision=highest)
    chain = soap(8, [grads_mod], state, chain)
    chain = soap(0, grads_attn, state, after(chain, grads_attn))

    def both(mine, other):
        return jnp.where(
            y == 0, jnp.concatenate([mine, other], axis=0), jnp.concatenate([other, mine], axis=0)
        )

    block_out = both(out_keep, out_got)
    input_grad = both(gin_keep, gin_got)
    bias_first_new = vector_first * bias_first + (1.0 - vector_first) * bias_grad
    bias_second_new = vector_second * bias_second + (1.0 - vector_second) * bias_grad * bias_grad
    new_biases = biases - vector_rate * (bias_first_new / (1.0 - vector_first**STEP)) / (
        jnp.sqrt(bias_second_new / (1.0 - vector_second**STEP)) + vector_epsilon
    )
    return (block_out, input_grad) + tuple(map(by_matrix, chain)) + (bias_first_new, bias_second_new, new_biases)


def solution(mesh):
    n_dp = mesh.shape["dp"]
    fine = Mesh(mesh.devices.reshape(n_dp // 2, 2, 2, 2), ("z", "x", "y", "c"))
    dp, mp = ("z", "x"), ("y", "c")
    return jax.shard_map(
        functools.partial(body, n_dp == 8),
        mesh=fine,
        in_specs=(
            P(dp, mp),
            P(dp, mp),
            P(dp),
            P(dp),
            P(),
            P(dp, None, mp),
            P(dp, None, mp),
            P(dp, None, mp),
            P(),
            P(None, dp, None),
            P(None, mp, None),
            P(None, mp),
            P(None, mp),
            P(None, mp),
        ),
        out_specs=(
            P(dp, mp),
            P(dp, mp),
            P(dp, None, mp),
            P(dp, None, mp),
            P(dp, None, mp),
            P(dp, None, mp),
            P(dp, None, mp),
            P(None, mp),
            P(None, mp),
            P(None, mp),
        ),
        check_vma=False,
    )
```
